32 devices in a mesh: season: 2 (over core), cells: 16 (over z, y, x).
Axes of the slice: x: 2, y: 2, z: 4, core: 2. Of those that a mesh axis runs over, the one named last changes fastest.
Arguments:
- start_adjoint: float32 [2, 8, 32768], P('season', None, 'cells'), may hold values from -6 to 6
- adjoint_tiles: bfloat16 [2, 2, 256, 3, 128, 128], P('season', None, 'cells'), may hold values from -0.21875 to 0.21875
- column_tiles: int32 [2, 2, 256, 3], P('season', None, 'cells'), may hold values from 0 to 255, as said below
- source_jacobian: float32 [2, 2, 8, 8, 32768], P('season', None, None, None, 'cells'), may hold values from -0.9 to 0.9
- obs_owner: int32 [2, 4096, 1], P('season', 'cells'), may hold values from 0 to 15; in each aligned block of 256 rows (0 to 255, 256 to 511, ..., all dimensions but the last counted through in order) at most 32 rows name the same one
- obs_local: int32 [2, 4096], P('season', 'cells'), may hold values from 0 to 2047
- obs_day: int32 [2, 4096], P('season', 'cells'), may hold values from 0 to 1
- obs_tracer: int32 [2, 4096], P('season', 'cells'), may hold values from 0 to 7
- obs_misfit: float32 [2, 4096], P('season', 'cells'), may hold values from -6 to 6
Outputs:
- start_update: float32 [2, 8, 32768], P('season', None, 'cells')
The draws below stay inside these ranges and needn't reach their ends.
Inputs may be any that keep to these rules, and one draw needn't show every extreme that they name: `column_tiles`: entry [s, m, t, 0] equals t; every other entry lies within 8 tiles of t on the closed range of 256 tiles, indices taken modulo 256. `obs_owner`: in each aligned block of 256 observations (the list of one device) no owner is named more than 32 times, a bound that some block reaches.
All inputs are finite; a program needn't handle non-finite values.
Results may differ from the reference program's by a relative error of at most 0.0003.
Values sent between devices are 32-bit elements; how exact they have to be, the bound alone decides.
A program may use at most 64 MiB of HBM per device.

```python
import math
import jax
import jax.numpy as jnp
import numpy as np
from jax import lax

TRACERS = 8
TILE = 128
NB = 3
DAYS = 2
OBS_DEV = 256
REACH = 8
CAP = 32
SEASONS = 2
CELLS_DEV = 2048
TILES = 256
CELLS = 32768
OBS = 4096
N_CELLS = 16


def draw_column_tiles(key, part):
    offsets = jax.random.randint(key, (SEASONS, 2, TILES, NB), -REACH, REACH + 1)
    offsets = offsets.at[:, :, :, 0].set(0)
    offsets = offsets.at[:, :, 0, 1].set(REACH)
    offsets = offsets.at[:, :, 0, 2].set(-REACH)
    row_tiles = jnp.arange(TILES, dtype=jnp.int32)[None, None, :, None]
    return ((row_tiles + offsets) % TILES).astype(jnp.int32)


def place_ends(entries, key, low, largest):
    spot = [jax.random.randint(jax.random.fold_in(key, axis), (), 0, length) for axis, length in enumerate(entries.shape)]
    widest = entries.shape.index(max(entries.shape))
    next_to = spot[:widest] + [(spot[widest] + 1) % entries.shape[widest]] + spot[widest + 1:]
    return entries.at[tuple(spot)].set(low).at[tuple(next_to)].set(largest)


def steps_of(own_key, shape, split, low, largest):
    gain, own = 1.0, jax.random.fold_in(own_key, 6)
    for axis_at, parts in split:
        heights = jnp.exp(jax.random.uniform(jax.random.fold_in(own, axis_at), (parts,), jnp.float32, low / len(split), largest / len(split)))
        gain = gain * jnp.repeat(heights, shape[axis_at] // parts).reshape([-1 if axis == axis_at else 1 for axis in range(len(shape))])
    return gain


def assign_block(key, own, number, rows, amount, top, reach, lean):
    ranking = jax.random.permutation(key, amount)
    crowded, usual = shares(amount, rows * top, reach, lean, True), shares(amount, rows * top, reach, lean, False)
    places = jnp.arange(amount)

    def named(tallies, turn):
        used = int((tallies > 0).sum())
        fixed = max(1, used // 4)
        moved = fixed + (places - fixed + turn * (used - fixed)) % max(1, amount - fixed)
        return jnp.zeros((amount,), jnp.int32).at[ranking[jnp.where(places < fixed, places, moved)]].set(jnp.asarray(tallies, jnp.int32))

    tallies = jnp.where(number % 4 == 0, named(crowded, number // 4), named(usual, number - number // 4 - 1))
    mixed = jax.random.permutation(jax.random.fold_in(own, 3), amount)
    giver, receiver = mixed[0:amount // 2 * 2:2], mixed[1:amount // 2 * 2:2]
    room = jnp.minimum(tallies[giver] - 1, reach - tallies[receiver]) // 2
    room = jnp.where((giver == ranking[0]) | (receiver == ranking[0]) | (tallies[receiver] == 0), 0, jnp.maximum(room, 0))
    moved = jax.random.randint(jax.random.fold_in(own, 4), (amount // 2,), 0, 1 << 20) % (room + 1)
    tallies = tallies.at[giver].add(-moved).at[receiver].add(moved)
    members = jnp.searchsorted(jnp.cumsum(tallies), jnp.arange(rows * top), side="right").astype(jnp.int32)
    listing = members.reshape(top, rows).T
    listing = listing[jax.random.permutation(jax.random.fold_in(own, 1), rows)]
    turn = jax.random.randint(jax.random.fold_in(own, 2), (rows, 1), 0, top)
    return jnp.take_along_axis(listing, (jnp.arange(top)[None, :] + turn) % top, axis=1)


def shares(count, total, most, slope, full):
    weights = [(1 << 20) // math.isqrt(standing ** slope) + 1 for standing in range(1, count + 1)]
    largest = most if full else min(most, max(-(-total // count), total * weights[0] // sum(weights)))
    least = 1 if total - largest >= count - 1 else 0
    holding, rest = [largest] + [least] * (count - 1), total - largest - least * (count - 1)
    while rest > 0:
        candidates = [i for i in range(1, count) if holding[i] < largest] or [i for i in range(1, count) if holding[i] < most]
        pool, budget = sum([weights[i] for i in candidates]), rest
        for i in candidates:
            extra = min(most - holding[i], max(1, budget * weights[i] // pool), rest)
            holding[i] = holding[i] + extra
            rest = rest - extra
    return np.array(holding)


def normal_values(rng, dims, deviation, most, split=(), kind=jnp.bfloat16):
    gain = steps_of(rng, dims, split, -0.22, 0.18) if split else 1.0
    values = jax.random.normal(rng, dims, jnp.float32) * deviation * gain
    return jnp.minimum(jnp.maximum(values, -most), most).astype(kind)


def setup_inputs(seed: int = 0) -> dict:
    splits = jax.random.split(jax.random.key(seed), 10)
    start_adjoint = normal_values(splits[0], (SEASONS, TRACERS, CELLS), 1.0, 6.0, ((0, 2), (2, 16)), jnp.float32)
    adjoint_tiles = normal_values(splits[1], (SEASONS, 2, TILES, NB, TILE, TILE), (2 * TILE * NB) ** -0.5, 0.21875, ((0, 2), (2, 16)))
    column_tiles = draw_column_tiles(jax.random.fold_in(splits[9], 71), 0)
    source_jacobian = normal_values(splits[3], (SEASONS, DAYS, TRACERS, TRACERS, CELLS), 0.15, 0.9, ((0, 2), (4, 16)), jnp.float32)
    obs_owner_keys = jax.random.split(jax.random.fold_in(splits[4], 1), SEASONS * OBS // OBS_DEV)
    obs_owner_turns = jax.random.permutation(jax.random.fold_in(splits[4], 3), SEASONS * OBS // OBS_DEV)
    obs_owner = jax.vmap(lambda own, number: assign_block(jax.random.fold_in(splits[4], 2), own, number, OBS_DEV, N_CELLS, 1, CAP, 2))(obs_owner_keys, obs_owner_turns).reshape((SEASONS, OBS, 1))
    obs_local = place_ends(jax.random.randint(splits[5], (SEASONS, OBS), 0, CELLS_DEV), jax.random.fold_in(splits[5], 1), 0, CELLS_DEV - 1).astype(jnp.int32)
    obs_day = place_ends(jax.random.randint(splits[6], (SEASONS, OBS), 0, DAYS), jax.random.fold_in(splits[6], 1), 0, DAYS - 1).astype(jnp.int32)
    obs_tracer = place_ends(jax.random.randint(splits[7], (SEASONS, OBS), 0, TRACERS), jax.random.fold_in(splits[7], 1), 0, TRACERS - 1).astype(jnp.int32)
    obs_misfit = normal_values(splits[8], (SEASONS, OBS), 1.0, 6.0, ((0, 2), (1, 16)), jnp.float32)
    return dict(start_adjoint=start_adjoint, adjoint_tiles=adjoint_tiles, column_tiles=column_tiles, source_jacobian=source_jacobian, obs_owner=obs_owner, obs_local=obs_local, obs_day=obs_day, obs_tracer=obs_tracer, obs_misfit=obs_misfit)


def apply_matrix(matrix_tiles, column_ids, adjoint_field):
    blocks = adjoint_field.reshape(TRACERS, TILES, TILE)
    picked = jnp.take(blocks, column_ids.reshape(-1), axis=1).reshape(TRACERS, TILES, NB, TILE)
    product = jnp.einsum("tkac,rtkc->rta", matrix_tiles.astype(jnp.float32), picked, precision=lax.Precision.HIGHEST)
    return adjoint_field + product.reshape(TRACERS, CELLS)


def segment_forcing(values, slot_ids):
    return jax.ops.segment_sum(values, slot_ids, num_segments=DAYS * TRACERS * CELLS)


def reference(start_adjoint, adjoint_tiles, column_tiles, source_jacobian, obs_owner, obs_local, obs_day, obs_tracer, obs_misfit):
    end_adjoint = jnp.roll(start_adjoint, -1, axis=0)
    global_cell = (obs_owner[:, :, 0] * CELLS_DEV + obs_local).astype(jnp.int32)
    slot_ids = ((obs_day * TRACERS + obs_tracer) * CELLS + global_cell).astype(jnp.int32)
    forcing = jax.vmap(segment_forcing)(obs_misfit, slot_ids).reshape(SEASONS, DAYS, TRACERS, CELLS)

    def one_segment(inputs):
        adjoint, matrix_tiles, column_ids, jacobian, season_forcing = inputs
        for day_index in reversed(range(DAYS)):
            carried = apply_matrix(matrix_tiles[0], column_ids[0], adjoint)
            coupled = jnp.einsum("jrc,jc->rc", jacobian[day_index], carried, precision=lax.Precision.HIGHEST)
            adjoint = apply_matrix(matrix_tiles[1], column_ids[1], carried) + coupled + season_forcing[day_index]
        return adjoint

    return lax.map(one_segment, (end_adjoint, adjoint_tiles, column_tiles, source_jacobian, forcing))
```

```python
import functools

import jax
import jax.numpy as jnp
from jax import lax
from jax.experimental import pallas as pl
from jax.experimental.pallas import tpu as pltpu
from jax.sharding import PartitionSpec as P

REACH = 8
PIECES = 2
MESH = pl.DeviceIdType.MESH
F32 = jnp.float32
BF16 = jnp.bfloat16


def dot_nt(a, b):
    return lax.dot_general(a, b, (((1,), (1,)), ((), ())), preferred_element_type=F32)


def kernel(
    seasons,
    peers,
    cols_hbm,
    start_ref,
    tiles_hbm,
    jac_hbm,
    owner_hbm,
    local_hbm,
    day_hbm,
    tracer_hbm,
    misfit_hbm,
    out_hbm,
    cols_ref,
    owner_ref,
    local_ref,
    day_ref,
    tracer_ref,
    misfit_ref,
    tiles_vm,
    jac_vm,
    wide,
    packed,
    base,
    slots_out,
    slots_in,
    force,
    load_sem,
    send_sem,
    recv_sem,
    obs_send_sem,
    obs_recv_sem,
    relayed,
    relay_sem,
    go_sem,
    late_sem,
):
    s = lax.axis_index("season")
    c = lax.axis_index("cells")
    days, tracers = jac_vm.shape[0], jac_vm.shape[1]
    tiles_here, near = tiles_vm.shape[1], tiles_vm.shape[2]
    rows = tiles_vm.shape[-1]
    cells_here = tiles_here * rows
    halo = REACH * rows
    total_tiles = tiles_here * peers
    piece = halo // PIECES
    step = REACH // PIECES
    rounds = 2 * days
    own = slice(halo, halo + cells_here)

    left, right = lax.rem(c + peers - 1, peers), lax.rem(c + 1, peers)
    before, after = lax.rem(s + seasons - 1, seasons), lax.rem(s + 1, seasons)
    first, last, middle = c == 0, c == peers - 1, c == peers // 2
    barrier = pltpu.get_barrier_semaphore()

    def signal(semaphore, season, cell):
        pl.semaphore_signal(
            semaphore, inc=1, device_id=(season, cell), device_id_type=MESH
        )

    @pl.when(middle)
    def _():
        signal(barrier, s, 0)
        signal(barrier, before, peers - 1)

    @pl.when(jnp.logical_not(last))
    def _():
        signal(barrier, after, right)

    signal(barrier, after, c)
    signal(barrier, after, left)

    @pl.loop(c + 1, peers)
    def _(other):
        signal(barrier, s, other)

    pairs = (
        (owner_hbm, owner_ref),
        (local_hbm, local_ref),
        (day_hbm, day_ref),
        (tracer_hbm, tracer_ref),
        (misfit_hbm, misfit_ref),
        (cols_hbm, cols_ref),
        (tiles_hbm.at[0, 0], tiles_vm.at[0]),
        (tiles_hbm.at[0, 1], tiles_vm.at[1]),
        (jac_hbm.at[0], jac_vm),
    )
    loads = [pltpu.make_async_copy(a, b, load_sem.at[i]) for i, (a, b) in enumerate(pairs)]
    for load in loads:
        load.start()
    shift = rows.bit_length() - 1
    listed = local_ref.shape[1]
    cap = 2 * listed // peers
    per_tile = rows // cap
    slot_tiles = slots_out.shape[0]

    def compact():
        local = local_ref[...]
        row_key = (local >> shift) * (days * tracers) + day_ref[...] * tracers + tracer_ref[...]
        owner = owner_ref[...].astype(F32)
        misfit = misfit_ref[...]
        named = lax.broadcasted_iota(jnp.int32, (peers, listed), 0).astype(F32) == owner
        named = jnp.where(named, 1.0, 0.0)
        earlier = lax.broadcasted_iota(jnp.int32, (listed, listed), 0)
        earlier = earlier < lax.broadcasted_iota(jnp.int32, (listed, listed), 1)
        counts = jnp.dot(
            named.astype(BF16),
            jnp.where(earlier, 1.0, 0.0).astype(BF16),
            preferred_element_type=F32,
        )
        place = owner * cap + jnp.sum(named * counts, axis=0, keepdims=True)
        high = misfit.astype(BF16).astype(F32)
        middle = (misfit - high).astype(BF16).astype(F32)
        at = lax.broadcasted_iota(jnp.int32, (tracers, listed), 0)
        key, lane = row_key.astype(F32), (local & (rows - 1)).astype(F32)
        first = jnp.where(at == 0, key, jnp.where(at == 1, lane, jnp.where(at == 2, high, 0.0)))
        second = jnp.where(at == 2, middle, 0.0)
        third = jnp.where(at == 2, misfit - high - middle, 0.0)
        fields = jnp.concatenate([first, second, third, jnp.zeros_like(first)], axis=0)
        fields = fields.astype(BF16)
        for g in range(slot_tiles):
            ids = lax.broadcasted_iota(jnp.int32, (rows, listed), 0) + g * rows
            chosen = jnp.where(ids.astype(F32) == place, 1.0, 0.0).astype(BF16)
            got = dot_nt(fields, chosen)
            got = got[:8] + got[8:16] + got[16:24]
            slots_out[g] = got[:4]

    def copy(src, r, lanes, season, cell, which):
        return pltpu.make_async_remote_copy(
            src_ref=src,
            dst_ref=wide.at[r, :, lanes],
            send_sem=send_sem.at[which // (2 * PIECES)],
            recv_sem=recv_sem.at[r % 2, which],
            device_id=(season, cell),
            device_id_type=MESH,
        )

    def halo_copies(r):
        season = before if r == 0 else s
        copies = []
        for i in range(PIECES):
            at = i * piece
            if r == 0:
                head = start_ref.at[0, :, at : at + piece]
                tail = start_ref.at[0, :, cells_here - halo + at : cells_here - halo + at + piece]
            else:
                head = wide.at[r, :, halo + at : halo + at + piece]
                tail = wide.at[r, :, cells_here + at : cells_here + at + piece]
            behind = halo + cells_here + at
            copies += [
                copy(head, r, slice(behind, behind + piece), season, left, 2 * i),
                copy(tail, r, slice(at, at + piece), season, right, 2 * i + 1),
            ]
        return copies

    def obs_copy(o):
        return pltpu.make_async_remote_copy(
            src_ref=slots_out.at[lax.div(lax.rem(c + o, peers), per_tile)],
            dst_ref=slots_in.at[o],
            send_sem=obs_send_sem,
            recv_sem=obs_recv_sem,
            device_id=(s, lax.rem(c + o, peers)),
            device_id_type=MESH,
        )

    def all_of(ref, send, recv):
        return pltpu.make_async_remote_copy(
            src_ref=ref,
            dst_ref=ref,
            send_sem=send,
            recv_sem=recv,
            device_id=(s, left),
            device_id_type=MESH,
        )

    all_halos = all_of(wide.at[:, :, : 2 * halo], send_sem.at[0], recv_sem.at[0, 0])
    all_obs = all_of(slots_in.at[1:], obs_send_sem, obs_recv_sem)

    sends = [halo_copies(r) for r in range(rounds)]
    body = copy(start_ref.at[0], 0, own, before, c, 2 * PIECES)

    def relay_in(i):
        at = slice(i * piece, (i + 1) * piece)
        return pltpu.make_async_remote_copy(
            src_ref=start_ref.at[0, :, at],
            dst_ref=relayed.at[:, at],
            send_sem=send_sem.at[0],
            recv_sem=relay_sem.at[i],
            device_id=(s, peers // 2),
            device_id_type=MESH,
        )

    def relay_out(i):
        at = slice(i * piece, (i + 1) * piece)
        behind = halo + cells_here + i * piece
        return pltpu.make_async_remote_copy(
            src_ref=relayed.at[:, at],
            dst_ref=wide.at[0, :, behind : behind + piece],
            send_sem=relay_sem.at[PIECES],
            recv_sem=recv_sem.at[0, 2 * i],
            device_id=(before, peers - 1),
            device_id_type=MESH,
        )

    all_relayed = all_of(relayed, relay_sem.at[PIECES], relay_sem.at[0])

    pl.semaphore_wait(barrier, c + 3 + jnp.where(last, 1, 0))

    @pl.when(last)
    def _():
        signal(go_sem, after, peers // 2)

    @pl.loop(0, c)
    def _(other):
        signal(late_sem, s, other)

    @pl.when(first)
    def _():
        for i in reversed(range(PIECES)):
            relay_in(i).start()

    @pl.when(jnp.logical_not(first))
    def _():
        for i in reversed(range(PIECES)):
            sends[0][2 * i].start()

    for i in reversed(range(PIECES)):
        sends[0][2 * i + 1].start()
    body.start()
    for load in loads[:5]:
        load.wait()
    compact()

    @pl.when(middle)
    def _():
        pl.semaphore_wait(go_sem, 1)
        for i in reversed(range(PIECES)):
            relay_in(i).wait_recv()
            relay_out(i).start()

    @pl.when(jnp.logical_not(last))
    def _():
        pl.semaphore_wait(late_sem, peers - 1 - c)

    @pl.loop(1, peers)
    def _(o):
        obs_copy(o).start()

    def pack(r, first, count):
        for t in range(first, first + count):
            v = wide[r, :, at_tile(t)]
            high = v.astype(BF16).astype(F32)
            packed[t] = jnp.concatenate([high, v - high], axis=0).astype(BF16)

    def gather_forcing():
        lanes = lax.broadcasted_iota(jnp.int32, slots_out.shape[1:], 1)
        first = lax.rem(c, per_tile) * cap
        mine = (lanes >= first) & (lanes < first + cap)
        merged = []
        all_obs.wait_recv()
        for g in range(slot_tiles):
            total = jnp.zeros(slots_out.shape[1:], F32)
            for o in range(g * per_tile, (g + 1) * per_tile):
                block = slots_in[o] if o > 0 else slots_out[lax.div(c, per_tile)]
                block = jnp.where(mine, block, 0.0)
                shift = (-o * cap) % rows
                total += pltpu.roll(block, shift, 1) if shift else block
            merged.append(total)
        merged = jnp.concatenate(merged, axis=1)
        row, lane, misfit = merged[0:1], merged[1:2], merged[2:3]
        slots = slot_tiles * rows
        row_ids = lax.broadcasted_iota(jnp.int32, (force.shape[0], slots), 0).astype(F32)
        hit = lax.broadcasted_iota(jnp.int32, (rows, slots), 0).astype(F32) == lane
        high = misfit.astype(BF16).astype(F32)
        values = jnp.concatenate(
            [jnp.where(hit, high, 0.0), jnp.where(hit, misfit - high, 0.0)], axis=0
        ).astype(BF16)
        force[...] = dot_nt(jnp.where(row_ids == row, 1.0, 0.0).astype(BF16), values)

    def at_tile(t):
        return slice(t * rows, (t + 1) * rows)

    def shifted(t):
        return slice(halo + t * rows, halo + (t + 1) * rows)

    def own_terms(r, day):
        matrix = r % 2
        pack(r, REACH, tiles_here)
        for t in range(tiles_here):
            v = wide[r, :, shifted(t)]
            both = dot_nt(packed[REACH + t], tiles_vm[matrix, t, 0])
            total = v + both[:tracers] + both[tracers:]
            if matrix == 1:
                at = (t * days + day) * tracers
                total += force[at : at + tracers, :rows] + force[at : at + tracers, rows:]
                for j in range(tracers):
                    total += jac_vm[day, j, :, at_tile(t)] * v[j : j + 1]
            base[:, at_tile(t)] = total

    def far_terms(r, chosen):
        matrix = r % 2
        products = []
        for t in chosen:
            picks = []
            for k in range(1, near):
                ahead = cols_ref[0, k, matrix, t] + (total_tiles + REACH - c * tiles_here)
                if total_tiles & (total_tiles - 1) == 0:
                    ahead = ahead & (total_tiles - 1)
                else:
                    ahead = lax.rem(ahead, total_tiles)
                picks.append(packed[jnp.minimum(ahead, packed.shape[0] - 1)])
            stored = [tiles_vm[matrix, t, k] for k in range(1, near)]
            both = dot_nt(jnp.concatenate(picks, axis=1), jnp.concatenate(stored, axis=1))
            products.append(both[:tracers] + both[tracers:])
        return products

    def finish(r, chosen, products):
        for t, product in zip(chosen, products):
            total = base[:, at_tile(t)] + product
            if r == rounds - 1:
                out_hbm[0, :, at_tile(t)] = total
            else:
                wide[r + 1, :, shifted(t)] = total

    def left_side(r):
        for i in reversed(range(PIECES)):
            sends[r][2 * i + 1].wait_recv()
            pack(r, i * step, step)
            chosen = range(i * step, (i + 1) * step)
            finish(r, chosen, far_terms(r, chosen))
            if r < rounds - 1:
                sends[r + 1][2 * i].start()

    def right_side(r):
        for i in reversed(range(PIECES)):
            sends[r][2 * i].wait_recv()
            pack(r, REACH + tiles_here + i * step, step)
        from_tile = tiles_here - REACH
        chosen = [from_tile + (PIECES - 1 - t // step) * step + t % step for t in range(REACH)]
        products = far_terms(r, chosen)
        for i in range(PIECES):
            finish(r, chosen[i * step : (i + 1) * step], products[i * step : (i + 1) * step])
            if r < rounds - 1:
                sends[r + 1][2 * (PIECES - 1 - i) + 1].start()

    for r in range(rounds):
        day = days - 1 - r // 2
        if r == 0:
            body.wait_recv()
            loads[6].wait()
        if r == 1:
            loads[7].wait()
            loads[8].wait()
            gather_forcing()
        own_terms(r, day)
        if r == 0:
            loads[5].wait()
        if r < rounds - 1:
            left_side(r)
            right_side(r)
        else:
            all_halos.wait_send()

            @pl.when(middle)
            def _():
                all_relayed.wait_send()

            body.wait_send()
            all_obs.wait_send()
            right_side(r)
            left_side(r)


def on_device(
    seasons,
    peers,
    start_adjoint,
    adjoint_tiles,
    column_tiles,
    source_jacobian,
    obs_owner,
    obs_local,
    obs_day,
    obs_tracer,
    obs_misfit,
):
    days, tracers = source_jacobian.shape[1], source_jacobian.shape[2]
    tiles_here, near, rows = adjoint_tiles.shape[2], adjoint_tiles.shape[3], adjoint_tiles.shape[-1]
    cells_here = start_adjoint.shape[2]
    assert tiles_here == 2 * REACH
    wide_cells = cells_here + 2 * REACH * rows
    listed = obs_local.shape[1]
    rounds = 2 * days
    hbm = pl.BlockSpec(memory_space=pl.ANY)
    return pl.pallas_call(
        functools.partial(kernel, seasons, peers),
        out_shape=pltpu.VMEM(start_adjoint.shape, F32),
        in_specs=[hbm] * 9,
        out_specs=pl.BlockSpec(memory_space=pltpu.VMEM),
        scratch_shapes=[
            pltpu.SMEM((1, near, 2, tiles_here), jnp.int32),
        ]
        + [pltpu.VMEM((1, listed), jnp.int32)] * 4
        + [
            pltpu.VMEM((1, listed), F32),
            pltpu.VMEM((2, tiles_here, near, rows, rows), BF16),
            pltpu.VMEM((days, tracers, tracers, cells_here), F32),
            pltpu.VMEM((rounds, tracers, wide_cells), F32),
            pltpu.VMEM((tiles_here + 2 * REACH, 2 * tracers, rows), BF16),
            pltpu.VMEM((tracers, cells_here), F32),
            pltpu.VMEM((2 * listed // rows, 4, rows), F32),
            pltpu.VMEM((peers, 4, rows), F32),
            pltpu.VMEM((tiles_here * days * tracers, 2 * rows), F32),
            pltpu.SemaphoreType.DMA((9,)),
            pltpu.SemaphoreType.DMA((2,)),
            pltpu.SemaphoreType.DMA((2, 2 * PIECES + 1)),
            pltpu.SemaphoreType.DMA,
            pltpu.SemaphoreType.DMA,
            pltpu.VMEM((tracers, REACH * rows), F32),
            pltpu.SemaphoreType.DMA((PIECES + 1,)),
            pltpu.SemaphoreType.REGULAR,
            pltpu.SemaphoreType.REGULAR,
        ],
        compiler_params=pltpu.CompilerParams(collective_id=0, has_side_effects=True),
    )(
        column_tiles.transpose(0, 3, 1, 2),
        start_adjoint,
        adjoint_tiles,
        source_jacobian,
        obs_owner.reshape(1, listed),
        obs_local,
        obs_day,
        obs_tracer,
        obs_misfit,
    )


def solution(mesh):
    placed = (
        P("season", None, "cells"),
        P("season", None, "cells", None, None, None),
        P("season", None, "cells", None),
        P("season", None, None, None, "cells"),
        P("season", "cells", None),
        P("season", "cells"),
        P("season", "cells"),
        P("season", "cells"),
        P("season", "cells"),
    )
    return jax.shard_map(
        functools.partial(on_device, mesh.shape["season"], mesh.shape["cells"]),
        mesh=mesh,
        in_specs=placed,
        out_specs=P("season", None, "cells"),
        check_vma=False,
    )
```

```python
import functools

import jax
import jax.numpy as jnp
from jax import lax
from jax.experimental import pallas as pl
from jax.experimental.pallas import tpu as pltpu
from jax.sharding import PartitionSpec as P

REACH = 8
PIECES = 2
MESH = pl.DeviceIdType.MESH
F32 = jnp.float32
BF16 = jnp.bfloat16


def dot_nt(a, b):
    return lax.dot_general(a, b, (((1,), (1,)), ((), ())), preferred_element_type=F32)


def kernel(
    seasons,
    peers,
    cols_hbm,
    start_ref,
    tiles_hbm,
    jac_hbm,
    owner_hbm,
    local_hbm,
    day_hbm,
    tracer_hbm,
    misfit_hbm,
    out_hbm,
    cols_ref,
    owner_ref,
    local_ref,
    day_ref,
    tracer_ref,
    misfit_ref,
    tiles_vm,
    jac_vm,
    wide,
    packed,
    base,
    slots_out,
    slots_in,
    force,
    load_sem,
    send_sem,
    recv_sem,
    obs_send_sem,
    obs_recv_sem,
    relayed,
    relay_sem,
    late_sem,
):
    s = lax.axis_index("season")
    c = lax.axis_index("cells")
    days, tracers = jac_vm.shape[0], jac_vm.shape[1]
    tiles_here, near = tiles_vm.shape[1], tiles_vm.shape[2]
    rows = tiles_vm.shape[-1]
    cells_here = tiles_here * rows
    halo = REACH * rows
    total_tiles = tiles_here * peers
    piece = halo // PIECES
    step = REACH // PIECES
    rounds = 2 * days
    own = slice(halo, halo + cells_here)

    left, right = lax.rem(c + peers - 1, peers), lax.rem(c + 1, peers)
    before, after = lax.rem(s + seasons - 1, seasons), lax.rem(s + 1, seasons)
    middle = peers // 2
    first, last, relays = c == 0, c == peers - 1, (c == middle) & (lax.rem(s, 2) == 1)
    through = jnp.where(lax.rem(s, 2) == 1, s, before)
    barrier = pltpu.get_barrier_semaphore()

    def signal(semaphore, season, cell):
        pl.semaphore_signal(
            semaphore, inc=1, device_id=(season, cell), device_id_type=MESH
        )

    @pl.when(relays)
    def _():
        signal(barrier, s, 0)
        signal(barrier, after, 0)

    @pl.when(last)
    def _():
        signal(barrier, jnp.where(lax.rem(s, 2) == 1, s, after), middle)

    @pl.when(jnp.logical_not(last))
    def _():
        signal(barrier, after, right)

    signal(barrier, after, c)
    signal(barrier, after, left)

    @pl.loop(c + 1, peers)
    def _(other):
        signal(barrier, s, other)

    pairs = (
        (owner_hbm, owner_ref),
        (local_hbm, local_ref),
        (day_hbm, day_ref),
        (tracer_hbm, tracer_ref),
        (misfit_hbm, misfit_ref),
        (cols_hbm, cols_ref),
        (tiles_hbm.at[0, 0], tiles_vm.at[0]),
        (tiles_hbm.at[0, 1], tiles_vm.at[1]),
        (jac_hbm.at[0], jac_vm),
    )
    loads = [pltpu.make_async_copy(a, b, load_sem.at[i]) for i, (a, b) in enumerate(pairs)]
    for load in loads:
        load.start()
    shift = rows.bit_length() - 1
    listed = local_ref.shape[1]
    cap = 2 * listed // peers
    per_tile = rows // cap
    slot_tiles = slots_out.shape[0]

    def compact():
        local = local_ref[...]
        row_key = (local >> shift) * (days * tracers) + day_ref[...] * tracers + tracer_ref[...]
        owner = owner_ref[...].astype(F32)
        misfit = misfit_ref[...]
        named = lax.broadcasted_iota(jnp.int32, (peers, listed), 0).astype(F32) == owner
        named = jnp.where(named, 1.0, 0.0)
        earlier = lax.broadcasted_iota(jnp.int32, (listed, listed), 0)
        earlier = earlier < lax.broadcasted_iota(jnp.int32, (listed, listed), 1)
        counts = jnp.dot(
            named.astype(BF16),
            jnp.where(earlier, 1.0, 0.0).astype(BF16),
            preferred_element_type=F32,
        )
        place = owner * cap + jnp.sum(named * counts, axis=0, keepdims=True)
        high = misfit.astype(BF16).astype(F32)
        middle = (misfit - high).astype(BF16).astype(F32)
        at = lax.broadcasted_iota(jnp.int32, (tracers, listed), 0)
        key, lane = row_key.astype(F32), (local & (rows - 1)).astype(F32)
        first = jnp.where(at == 0, key, jnp.where(at == 1, lane, jnp.where(at == 2, high, 0.0)))
        second = jnp.where(at == 2, middle, 0.0)
        third = jnp.where(at == 2, misfit - high - middle, 0.0)
        fields = jnp.concatenate([first, second, third, jnp.zeros_like(first)], axis=0)
        fields = fields.astype(BF16)
        for g in range(slot_tiles):
            ids = lax.broadcasted_iota(jnp.int32, (rows, listed), 0) + g * rows
            chosen = jnp.where(ids.astype(F32) == place, 1.0, 0.0).astype(BF16)
            got = dot_nt(fields, chosen)
            got = got[:8] + got[8:16] + got[16:24]
            slots_out[g] = got[:4]

    def copy(src, r, lanes, season, cell, which):
        return pltpu.make_async_remote_copy(
            src_ref=src,
            dst_ref=wide.at[r, :, lanes],
            send_sem=send_sem.at[which // (2 * PIECES)],
            recv_sem=recv_sem.at[r % 2, which],
            device_id=(season, cell),
            device_id_type=MESH,
        )

    def halo_copies(r):
        season = before if r == 0 else s
        copies = []
        for i in range(PIECES):
            at = i * piece
            if r == 0:
                head = start_ref.at[0, :, at : at + piece]
                tail = start_ref.at[0, :, cells_here - halo + at : cells_here - halo + at + piece]
            else:
                head = wide.at[r, :, halo + at : halo + at + piece]
                tail = wide.at[r, :, cells_here + at : cells_here + at + piece]
            behind = halo + cells_here + at
            copies += [
                copy(head, r, slice(behind, behind + piece), season, left, 2 * i),
                copy(tail, r, slice(at, at + piece), season, right, 2 * i + 1),
            ]
        return copies

    def obs_copy(o):
        return pltpu.make_async_remote_copy(
            src_ref=slots_out.at[lax.div(lax.rem(c + o, peers), per_tile)],
            dst_ref=slots_in.at[o],
            send_sem=obs_send_sem,
            recv_sem=obs_recv_sem,
            device_id=(s, lax.rem(c + o, peers)),
            device_id_type=MESH,
        )

    def all_of(ref, send, recv):
        return pltpu.make_async_remote_copy(
            src_ref=ref,
            dst_ref=ref,
            send_sem=send,
            recv_sem=recv,
            device_id=(s, left),
            device_id_type=MESH,
        )

    all_halos = all_of(wide.at[:, :, : 2 * halo], send_sem.at[0], recv_sem.at[0, 0])
    all_obs = all_of(slots_in.at[1:], obs_send_sem, obs_recv_sem)

    sends = [halo_copies(r) for r in range(rounds)]
    body = copy(start_ref.at[0], 0, own, before, c, 2 * PIECES)

    def relay_in(i, flow):
        at = slice(i * piece, (i + 1) * piece)
        return pltpu.make_async_remote_copy(
            src_ref=start_ref.at[0, :, at],
            dst_ref=relayed.at[flow, :, at],
            send_sem=send_sem.at[0],
            recv_sem=relay_sem.at[flow, i],
            device_id=(through, middle),
            device_id_type=MESH,
        )

    def relay_out(i, flow):
        at = slice(i * piece, (i + 1) * piece)
        behind = halo + cells_here + i * piece
        return pltpu.make_async_remote_copy(
            src_ref=relayed.at[flow, :, at],
            dst_ref=wide.at[0, :, behind : behind + piece],
            send_sem=relay_sem.at[0, PIECES],
            recv_sem=recv_sem.at[0, 2 * i],
            device_id=(s if flow else before, peers - 1),
            device_id_type=MESH,
        )

    all_relayed = all_of(relayed, relay_sem.at[0, PIECES], relay_sem.at[0, 0])

    pl.semaphore_wait(barrier, c + 3 + jnp.where(relays, 2, 0))

    @pl.loop(0, c)
    def _(other):
        signal(late_sem, s, other)

    @pl.when(first)
    def _():
        for i in reversed(range(PIECES)):
            relay_in(i, lax.rem(s + 1, 2)).start()

    @pl.when(jnp.logical_not(first))
    def _():
        for i in reversed(range(PIECES)):
            sends[0][2 * i].start()

    for i in reversed(range(PIECES)):
        sends[0][2 * i + 1].start()
    body.start()

    @pl.when(relays)
    def _():
        for flow in range(2):
            for i in reversed(range(PIECES)):
                relay_in(i, flow).wait_recv()
                relay_out(i, flow).start()

    for load in loads[:5]:
        load.wait()
    compact()

    @pl.when(jnp.logical_not(last))
    def _():
        pl.semaphore_wait(late_sem, peers - 1 - c)

    @pl.loop(1, peers)
    def _(o):
        obs_copy(o).start()

    def pack(r, first, count):
        for t in range(first, first + count):
            v = wide[r, :, at_tile(t)]
            high = v.astype(BF16).astype(F32)
            packed[t] = jnp.concatenate([high, v - high], axis=0).astype(BF16)

    def gather_forcing():
        lanes = lax.broadcasted_iota(jnp.int32, slots_out.shape[1:], 1)
        first = lax.rem(c, per_tile) * cap
        mine = (lanes >= first) & (lanes < first + cap)
        merged = []
        all_obs.wait_recv()
        for g in range(slot_tiles):
            total = jnp.zeros(slots_out.shape[1:], F32)
            for o in range(g * per_tile, (g + 1) * per_tile):
                block = slots_in[o] if o > 0 else slots_out[lax.div(c, per_tile)]
                block = jnp.where(mine, block, 0.0)
                shift = (-o * cap) % rows
                total += pltpu.roll(block, shift, 1) if shift else block
            merged.append(total)
        merged = jnp.concatenate(merged, axis=1)
        row, lane, misfit = merged[0:1], merged[1:2], merged[2:3]
        slots = slot_tiles * rows
        row_ids = lax.broadcasted_iota(jnp.int32, (force.shape[0], slots), 0).astype(F32)
        hit = lax.broadcasted_iota(jnp.int32, (rows, slots), 0).astype(F32) == lane
        high = misfit.astype(BF16).astype(F32)
        values = jnp.concatenate(
            [jnp.where(hit, high, 0.0), jnp.where(hit, misfit - high, 0.0)], axis=0
        ).astype(BF16)
        force[...] = dot_nt(jnp.where(row_ids == row, 1.0, 0.0).astype(BF16), values)

    def at_tile(t):
        return slice(t * rows, (t + 1) * rows)

    def shifted(t):
        return slice(halo + t * rows, halo + (t + 1) * rows)

    def own_terms(r, day):
        matrix = r % 2
        pack(r, REACH, tiles_here)
        for t in range(tiles_here):
            v = wide[r, :, shifted(t)]
            both = dot_nt(packed[REACH + t], tiles_vm[matrix, t, 0])
            total = v + both[:tracers] + both[tracers:]
            if matrix == 1:
                at = (t * days + day) * tracers
                total += force[at : at + tracers, :rows] + force[at : at + tracers, rows:]
                for j in range(tracers):
                    total += jac_vm[day, j, :, at_tile(t)] * v[j : j + 1]
            base[:, at_tile(t)] = total

    def far_terms(r, chosen):
        matrix = r % 2
        products = []
        for t in chosen:
            picks = []
            for k in range(1, near):
                ahead = cols_ref[0, k, matrix, t] + (total_tiles + REACH - c * tiles_here)
                if total_tiles & (total_tiles - 1) == 0:
                    ahead = ahead & (total_tiles - 1)
                else:
                    ahead = lax.rem(ahead, total_tiles)
                picks.append(packed[jnp.minimum(ahead, packed.shape[0] - 1)])
            stored = [tiles_vm[matrix, t, k] for k in range(1, near)]
            both = dot_nt(jnp.concatenate(picks, axis=1), jnp.concatenate(stored, axis=1))
            products.append(both[:tracers] + both[tracers:])
        return products

    def finish(r, chosen, products):
        for t, product in zip(chosen, products):
            total = base[:, at_tile(t)] + product
            if r == rounds - 1:
                out_hbm[0, :, at_tile(t)] = total
            else:
                wide[r + 1, :, shifted(t)] = total

    def left_side(r):
        for i in reversed(range(PIECES)):
            sends[r][2 * i + 1].wait_recv()
            pack(r, i * step, step)
            chosen = range(i * step, (i + 1) * step)
            finish(r, chosen, far_terms(r, chosen))
            if r < rounds - 1:
                sends[r + 1][2 * i].start()

    def right_side(r):
        for i in reversed(range(PIECES)):
            sends[r][2 * i].wait_recv()
            pack(r, REACH + tiles_here + i * step, step)
        from_tile = tiles_here - REACH
        chosen = [from_tile + (PIECES - 1 - t // step) * step + t % step for t in range(REACH)]
        products = far_terms(r, chosen)
        for i in range(PIECES):
            finish(r, chosen[i * step : (i + 1) * step], products[i * step : (i + 1) * step])
            if r < rounds - 1:
                sends[r + 1][2 * (PIECES - 1 - i) + 1].start()

    for r in range(rounds):
        day = days - 1 - r // 2
        if r == 0:
            body.wait_recv()
            loads[6].wait()
        if r == 1:
            loads[7].wait()
            loads[8].wait()
            gather_forcing()
        own_terms(r, day)
        if r == 0:
            loads[5].wait()
        if r < rounds - 1:
            left_side(r)
            right_side(r)
        else:
            all_halos.wait_send()

            @pl.when(relays)
            def _():
                all_relayed.wait_send()

            body.wait_send()
            all_obs.wait_send()
            right_side(r)
            left_side(r)


def on_device(
    seasons,
    peers,
    start_adjoint,
    adjoint_tiles,
    column_tiles,
    source_jacobian,
    obs_owner,
    obs_local,
    obs_day,
    obs_tracer,
    obs_misfit,
):
    days, tracers = source_jacobian.shape[1], source_jacobian.shape[2]
    tiles_here, near, rows = adjoint_tiles.shape[2], adjoint_tiles.shape[3], adjoint_tiles.shape[-1]
    cells_here = start_adjoint.shape[2]
    assert tiles_here == 2 * REACH and seasons % 2 == 0
    wide_cells = cells_here + 2 * REACH * rows
    listed = obs_local.shape[1]
    rounds = 2 * days
    hbm = pl.BlockSpec(memory_space=pl.ANY)
    return pl.pallas_call(
        functools.partial(kernel, seasons, peers),
        out_shape=pltpu.VMEM(start_adjoint.shape, F32),
        in_specs=[hbm] * 9,
        out_specs=pl.BlockSpec(memory_space=pltpu.VMEM),
        scratch_shapes=[
            pltpu.SMEM((1, near, 2, tiles_here), jnp.int32),
        ]
        + [pltpu.VMEM((1, listed), jnp.int32)] * 4
        + [
            pltpu.VMEM((1, listed), F32),
            pltpu.VMEM((2, tiles_here, near, rows, rows), BF16),
            pltpu.VMEM((days, tracers, tracers, cells_here), F32),
            pltpu.VMEM((rounds, tracers, wide_cells), F32),
            pltpu.VMEM((tiles_here + 2 * REACH, 2 * tracers, rows), BF16),
            pltpu.VMEM((tracers, cells_here), F32),
            pltpu.VMEM((2 * listed // rows, 4, rows), F32),
            pltpu.VMEM((peers, 4, rows), F32),
            pltpu.VMEM((tiles_here * days * tracers, 2 * rows), F32),
            pltpu.SemaphoreType.DMA((9,)),
            pltpu.SemaphoreType.DMA((2,)),
            pltpu.SemaphoreType.DMA((2, 2 * PIECES + 1)),
            pltpu.SemaphoreType.DMA,
            pltpu.SemaphoreType.DMA,
            pltpu.VMEM((2, tracers, REACH * rows), F32),
            pltpu.SemaphoreType.DMA((2, PIECES + 1)),
            pltpu.SemaphoreType.REGULAR,
        ],
        compiler_params=pltpu.CompilerParams(collective_id=0, has_side_effects=True),
    )(
        column_tiles.transpose(0, 3, 1, 2),
        start_adjoint,
        adjoint_tiles,
        source_jacobian,
        obs_owner.reshape(1, listed),
        obs_local,
        obs_day,
        obs_tracer,
        obs_misfit,
    )


def solution(mesh):
    placed = (
        P("season", None, "cells"),
        P("season", None, "cells", None, None, None),
        P("season", None, "cells", None),
        P("season", None, None, None, "cells"),
        P("season", "cells", None),
        P("season", "cells"),
        P("season", "cells"),
        P("season", "cells"),
        P("season", "cells"),
    )
    return jax.shard_map(
        functools.partial(on_device, mesh.shape["season"], mesh.shape["cells"]),
        mesh=mesh,
        in_specs=placed,
        out_specs=P("season", None, "cells"),
        check_vma=False,
    )
```

```python
import functools

import jax
import jax.numpy as jnp
from jax import lax
from jax.experimental import pallas as pl
from jax.experimental.pallas import tpu as pltpu
from jax.sharding import PartitionSpec as P

REACH = 8
PIECES = 2
MESH = pl.DeviceIdType.MESH
F32 = jnp.float32
BF16 = jnp.bfloat16


def dot_nt(a, b):
    return lax.dot_general(a, b, (((1,), (1,)), ((), ())), preferred_element_type=F32)


def kernel(
    seasons,
    peers,
    cols_hbm,
    start_ref,
    tiles_hbm,
    jac_hbm,
    owner_hbm,
    local_hbm,
    day_hbm,
    tracer_hbm,
    misfit_hbm,
    out_hbm,
    cols_ref,
    owner_ref,
    local_ref,
    day_ref,
    tracer_ref,
    misfit_ref,
    tiles_vm,
    jac_vm,
    wide,
    packed,
    base,
    slots_out,
    slots_in,
    force,
    load_sem,
    send_sem,
    recv_sem,
    obs_send_sem,
    obs_recv_sem,
    relayed,
    relay_sem,
    late_sem,
    lent,
    lent_tiles,
    lent_listed,
    lent_cols,
    lent_field,
    lent_base,
    lent_out,
    lent_packed,
    lend_sem,
    lend_halo_sem,
):
    s = lax.axis_index("season")
    c = lax.axis_index("cells")
    days, tracers = jac_vm.shape[0], jac_vm.shape[1]
    tiles_here, near = tiles_vm.shape[1], tiles_vm.shape[2]
    rows = tiles_vm.shape[-1]
    cells_here = tiles_here * rows
    halo = REACH * rows
    total_tiles = tiles_here * peers
    piece = halo // PIECES
    step = REACH // PIECES
    rounds = 2 * days
    own = slice(halo, halo + cells_here)

    left, right = lax.rem(c + peers - 1, peers), lax.rem(c + 1, peers)
    before, after = lax.rem(s + seasons - 1, seasons), lax.rem(s + 1, seasons)
    middle = peers // 2
    first, last, relays = c == 0, c == peers - 1, (c == middle) & (lax.rem(s, 2) == 1)
    odd = lax.rem(s, 2) == 1
    through = jnp.where(odd, s, before)
    helps, lends, fed = last & odd, last & (lax.rem(s, 2) == 0), first & (lax.rem(s, 2) == 0)
    barrier = pltpu.get_barrier_semaphore()

    def signal(semaphore, season, cell):
        pl.semaphore_signal(
            semaphore, inc=1, device_id=(season, cell), device_id_type=MESH
        )

    @pl.when(relays)
    def _():
        signal(barrier, s, 0)
        signal(barrier, after, 0)

    @pl.when(helps)
    def _():
        signal(barrier, s, middle)
        signal(barrier, before, peers - 1)

    @pl.when(jnp.logical_not(last))
    def _():
        signal(barrier, after, right)

    signal(barrier, after, c)
    signal(barrier, after, left)

    @pl.loop(c + 1, peers)
    def _(other):
        signal(barrier, s, other)

    pairs = (
        (owner_hbm, owner_ref),
        (local_hbm, local_ref),
        (day_hbm, day_ref),
        (tracer_hbm, tracer_ref),
        (misfit_hbm, misfit_ref),
        (cols_hbm, cols_ref),
        (tiles_hbm.at[0, 0], tiles_vm.at[0]),
        (tiles_hbm.at[0, 1], tiles_vm.at[1]),
        (jac_hbm.at[0], jac_vm),
    )
    loads = [pltpu.make_async_copy(a, b, load_sem.at[i]) for i, (a, b) in enumerate(pairs)]
    stage = pltpu.make_async_copy(start_ref.at[0, :, :halo], relayed.at[0], lend_sem.at[0])

    @pl.when(first)
    def _():
        stage.start()

    for load in loads[:7]:
        load.start()
    shift = rows.bit_length() - 1
    listed = local_ref.shape[1]
    cap = 2 * listed // peers
    per_tile = rows // cap
    slot_tiles = slots_out.shape[0]

    def compact():
        local = local_ref[...]
        row_key = (local >> shift) * (days * tracers) + day_ref[...] * tracers + tracer_ref[...]
        owner = owner_ref[...].astype(F32)
        misfit = misfit_ref[...]
        named = lax.broadcasted_iota(jnp.int32, (peers, listed), 0).astype(F32) == owner
        named = jnp.where(named, 1.0, 0.0)
        earlier = lax.broadcasted_iota(jnp.int32, (listed, listed), 0)
        earlier = earlier < lax.broadcasted_iota(jnp.int32, (listed, listed), 1)
        counts = jnp.dot(
            named.astype(BF16),
            jnp.where(earlier, 1.0, 0.0).astype(BF16),
            preferred_element_type=F32,
        )
        place = owner * cap + jnp.sum(named * counts, axis=0, keepdims=True)
        high = misfit.astype(BF16).astype(F32)
        middle = (misfit - high).astype(BF16).astype(F32)
        at = lax.broadcasted_iota(jnp.int32, (tracers, listed), 0)
        key, lane = row_key.astype(F32), (local & (rows - 1)).astype(F32)
        first = jnp.where(at == 0, key, jnp.where(at == 1, lane, jnp.where(at == 2, high, 0.0)))
        second = jnp.where(at == 2, middle, 0.0)
        third = jnp.where(at == 2, misfit - high - middle, 0.0)
        fields = jnp.concatenate([first, second, third, jnp.zeros_like(first)], axis=0)
        fields = fields.astype(BF16)
        for g in range(slot_tiles):
            ids = lax.broadcasted_iota(jnp.int32, (rows, listed), 0) + g * rows
            chosen = jnp.where(ids.astype(F32) == place, 1.0, 0.0).astype(BF16)
            got = dot_nt(fields, chosen)
            got = got[:8] + got[8:16] + got[16:24]
            slots_out[g] = got[:4]

    def copy(src, r, lanes, season, cell, which):
        return pltpu.make_async_remote_copy(
            src_ref=src,
            dst_ref=wide.at[r, :, lanes],
            send_sem=send_sem.at[which // (2 * PIECES)],
            recv_sem=recv_sem.at[r % 2, which],
            device_id=(season, cell),
            device_id_type=MESH,
        )

    def halo_copies(r):
        season = before if r == 0 else s
        copies = []
        for i in range(PIECES):
            at = i * piece
            if r == 0:
                head = start_ref.at[0, :, at : at + piece]
                tail = start_ref.at[0, :, cells_here - halo + at : cells_here - halo + at + piece]
            else:
                head = wide.at[r, :, halo + at : halo + at + piece]
                tail = wide.at[r, :, cells_here + at : cells_here + at + piece]
            behind = halo + cells_here + at
            copies += [
                copy(head, r, slice(behind, behind + piece), season, left, 2 * i),
                copy(tail, r, slice(at, at + piece), season, right, 2 * i + 1),
            ]
        return copies

    def obs_copy(o):
        return pltpu.make_async_remote_copy(
            src_ref=slots_out.at[lax.div(lax.rem(c + o, peers), per_tile)],
            dst_ref=slots_in.at[o],
            send_sem=obs_send_sem,
            recv_sem=obs_recv_sem,
            device_id=(s, lax.rem(c + o, peers)),
            device_id_type=MESH,
        )

    def all_of(ref, send, recv):
        return pltpu.make_async_remote_copy(
            src_ref=ref,
            dst_ref=ref,
            send_sem=send,
            recv_sem=recv,
            device_id=(s, left),
            device_id_type=MESH,
        )

    all_halos = all_of(wide.at[:, :, : 2 * halo], send_sem.at[0], recv_sem.at[0, 0])
    all_obs = all_of(slots_in.at[1:], obs_send_sem, obs_recv_sem)

    sends = [halo_copies(r) for r in range(rounds)]
    body = copy(start_ref.at[0], 0, own, before, c, 2 * PIECES)

    def relay_in(i, flow):
        at = slice(i * piece, (i + 1) * piece)
        return pltpu.make_async_remote_copy(
            src_ref=relayed.at[0, :, at],
            dst_ref=relayed.at[flow, :, at],
            send_sem=send_sem.at[0],
            recv_sem=relay_sem.at[flow, i],
            device_id=(through, middle),
            device_id_type=MESH,
        )

    def relay_out(i, flow):
        at = slice(i * piece, (i + 1) * piece)
        if flow:
            behind = halo + cells_here + i * piece
            dst, recv = wide.at[0, :, behind : behind + piece], recv_sem.at[0, 2 * i]
        else:
            behind = cells_here + i * piece
            dst, recv = lent_field.at[0, :, behind : behind + piece], lend_halo_sem.at[0, i]
        return pltpu.make_async_remote_copy(
            src_ref=relayed.at[flow, :, at],
            dst_ref=dst,
            send_sem=lend_sem.at[0],
            recv_sem=recv,
            device_id=(s, peers - 1),
            device_id_type=MESH,
        )

    all_relayed = all_of(relayed, lend_sem.at[0], lend_sem.at[1])

    def lend(src, dst, send, recv):
        return pltpu.make_async_remote_copy(
            src_ref=src,
            dst_ref=dst,
            send_sem=send,
            recv_sem=recv,
            device_id=(after, peers - 1),
            device_id_type=MESH,
        )

    tail = slice(cells_here - halo, cells_here)
    lend_tiles = lend(lent, lent, lend_sem.at[0], lend_sem.at[1])
    lend_cols = lend(cols_hbm, lent_listed, lend_sem.at[2], lend_sem.at[3])
    lend_base = [
        lend(lent_out.at[i], lent_base.at[i], lend_sem.at[4], lend_sem.at[5 + i]) for i in range(2)
    ]
    lend_own = lend(
        wide.at[2, :, own], lent_field.at[1, :, :cells_here], send_sem.at[0], lend_sem.at[7]
    )
    feed = [
        lend(
            wide.at[2, :, halo + i * piece : halo + (i + 1) * piece],
            lent_field.at[1, :, cells_here + i * piece : cells_here + (i + 1) * piece],
            send_sem.at[0],
            lend_halo_sem.at[1, i],
        )
        for i in range(PIECES)
    ]
    help_own = pltpu.make_async_copy(
        start_ref.at[0], lent_field.at[0, :, :cells_here], lend_sem.at[0]
    )
    help_cols = pltpu.make_async_copy(lent_listed, lent_cols, lend_sem.at[2])
    all_lent = all_of(lent_out, lend_sem.at[4], lend_sem.at[5])
    all_helped = all_of(lent.at[:1], lend_sem.at[4], lend_sem.at[5])

    def pass_on(turn, i):
        behind = cells_here + i * piece
        return pltpu.make_async_remote_copy(
            src_ref=lent_field.at[turn, :, behind : behind + piece],
            dst_ref=wide.at[2 * turn, :, halo + behind : halo + behind + piece],
            send_sem=lend_sem.at[4],
            recv_sem=recv_sem.at[0, 2 * i],
            device_id=(before, peers - 1),
            device_id_type=MESH,
        )

    def help_copy(turn, i):
        return pltpu.make_async_remote_copy(
            src_ref=lent_out.at[turn, :, i * piece : (i + 1) * piece],
            dst_ref=wide.at[2 * turn + 1, :, i * piece : (i + 1) * piece],
            send_sem=lend_sem.at[4],
            recv_sem=recv_sem.at[1, 2 * i + 1],
            device_id=(before, 0),
            device_id_type=MESH,
        )

    pl.semaphore_wait(barrier, c + 3 + jnp.where(relays | lends, 1, 0))

    @pl.loop(0, c)
    def _(other):
        signal(late_sem, s, other)

    @pl.when(first)
    def _():
        stage.wait()
        for i in reversed(range(PIECES)):
            relay_in(i, lax.rem(s + 1, 2)).start()

    @pl.when(jnp.logical_not(first))
    def _():
        for i in reversed(range(PIECES)):
            sends[0][2 * i].start()

    for i in reversed(range(PIECES)):
        sends[0][2 * i + 1].start()
    body.start()

    loads[6].wait()
    for load in loads[7:]:
        load.start()

    @pl.when(lends)
    def _():
        lend_cols.start()
        for i in range(REACH):
            for k in range(1, near):
                lent[i, k - 1] = tiles_vm[0, tiles_here - REACH + i, k].astype(F32)
        lend_tiles.start()

    @pl.when(helps)
    def _():
        help_own.start()

    @pl.when(relays)
    def _():
        for flow in range(2):
            for i in reversed(range(PIECES)):
                relay_in(i, flow).wait_recv()
                relay_out(i, flow).start()

    for load in loads[:5]:
        load.wait()
    compact()
    @pl.when(jnp.logical_not(last))
    def _():
        pl.semaphore_wait(late_sem, peers - 1 - c)

    @pl.loop(1, peers)
    def _(o):
        obs_copy(o).start()

    def pack(r, first, count):
        for t in range(first, first + count):
            v = wide[r, :, at_tile(t)]
            high = v.astype(BF16).astype(F32)
            packed[t] = jnp.concatenate([high, v - high], axis=0).astype(BF16)

    def gather_forcing():
        lanes = lax.broadcasted_iota(jnp.int32, slots_out.shape[1:], 1)
        first = lax.rem(c, per_tile) * cap
        mine = (lanes >= first) & (lanes < first + cap)
        merged = []
        all_obs.wait_recv()
        for g in range(slot_tiles):
            total = jnp.zeros(slots_out.shape[1:], F32)
            for o in range(g * per_tile, (g + 1) * per_tile):
                block = slots_in[o] if o > 0 else slots_out[lax.div(c, per_tile)]
                block = jnp.where(mine, block, 0.0)
                shift = (-o * cap) % rows
                total += pltpu.roll(block, shift, 1) if shift else block
            merged.append(total)
        merged = jnp.concatenate(merged, axis=1)
        row, lane, misfit = merged[0:1], merged[1:2], merged[2:3]
        slots = slot_tiles * rows
        row_ids = lax.broadcasted_iota(jnp.int32, (force.shape[0], slots), 0).astype(F32)
        hit = lax.broadcasted_iota(jnp.int32, (rows, slots), 0).astype(F32) == lane
        high = misfit.astype(BF16).astype(F32)
        values = jnp.concatenate(
            [jnp.where(hit, high, 0.0), jnp.where(hit, misfit - high, 0.0)], axis=0
        ).astype(BF16)
        force[...] = dot_nt(jnp.where(row_ids == row, 1.0, 0.0).astype(BF16), values)

    def at_tile(t):
        return slice(t * rows, (t + 1) * rows)

    def shifted(t):
        return slice(halo + t * rows, halo + (t + 1) * rows)

    def own_terms(r, day):
        matrix = r % 2
        pack(r, REACH, tiles_here)
        for t in range(tiles_here):
            v = wide[r, :, shifted(t)]
            both = dot_nt(packed[REACH + t], tiles_vm[matrix, t, 0])
            total = v + both[:tracers] + both[tracers:]
            if matrix == 1:
                at = (t * days + day) * tracers
                total += force[at : at + tracers, :rows] + force[at : at + tracers, rows:]
                for j in range(tracers):
                    total += jac_vm[day, j, :, at_tile(t)] * v[j : j + 1]
            base[:, at_tile(t)] = total

    def far_terms(r, chosen):
        matrix = r % 2
        products = []
        for t in chosen:
            picks = []
            for k in range(1, near):
                ahead = cols_ref[0, k, matrix, t] + (total_tiles + REACH - c * tiles_here)
                if total_tiles & (total_tiles - 1) == 0:
                    ahead = ahead & (total_tiles - 1)
                else:
                    ahead = lax.rem(ahead, total_tiles)
                picks.append(packed[jnp.minimum(ahead, packed.shape[0] - 1)])
            stored = [tiles_vm[matrix, t, k] for k in range(1, near)]
            both = dot_nt(jnp.concatenate(picks, axis=1), jnp.concatenate(stored, axis=1))
            products.append(both[:tracers] + both[tracers:])
        return products

    def finish(r, chosen, products):
        for t, product in zip(chosen, products):
            total = base[:, at_tile(t)] + product
            if r == rounds - 1:
                out_hbm[0, :, at_tile(t)] = total
            else:
                wide[r + 1, :, shifted(t)] = total

    def split(v):
        high = v.astype(BF16).astype(F32)
        return jnp.concatenate([high, v - high], axis=0).astype(BF16)

    def help_with(turn):
        if turn == 0:
            lend_cols.wait_recv()
            help_cols.start()
            help_own.wait()
        else:
            lend_own.wait_recv()
        for t in range(tiles_here):
            lent_packed[t] = split(lent_field[turn, :, at_tile(t)])
        lend_base[turn].wait_recv()
        if turn == 0:
            help_cols.wait()
            lend_tiles.wait_recv()
            for i in range(REACH):
                for k in range(1, near):
                    lent_tiles[i, k - 1] = lent[i, k - 1].astype(BF16)
        for i in reversed(range(PIECES)):
            halo_piece(turn, i).wait_recv()
            for t in range(tiles_here + i * step, tiles_here + (i + 1) * step):
                lent_packed[t] = split(lent_field[turn, :, at_tile(t)])
        chosen = [(PIECES - 1 - t // step) * step + t % step for t in range(REACH)]
        products = []
        for t in chosen:
            picks = []
            for k in range(1, near):
                ahead = lent_cols[0, k, 0, tiles_here - REACH + t] + (total_tiles - c * tiles_here)
                if total_tiles & (total_tiles - 1) == 0:
                    ahead = ahead & (total_tiles - 1)
                else:
                    ahead = lax.rem(ahead, total_tiles)
                picks.append(lent_packed[jnp.minimum(ahead, lent_packed.shape[0] - 1)])
            stored = [lent_tiles[t, k - 1] for k in range(1, near)]
            both = dot_nt(jnp.concatenate(picks, axis=1), jnp.concatenate(stored, axis=1))
            products.append(both[:tracers] + both[tracers:])
        for i in range(PIECES):
            for j in range(i * step, (i + 1) * step):
                lanes = at_tile(chosen[j])
                lent_out[turn, :, lanes] = lent_base[turn, :, lanes] + products[j]
            help_copy(turn, PIECES - 1 - i).start()
        for i in reversed(range(PIECES)):
            pass_on(turn, i).start()

    def halo_piece(turn, i):
        return feed[i] if turn else relay_out(i, 0)

    def left_side(r):
        for i in reversed(range(PIECES)):
            sends[r][2 * i + 1].wait_recv()
            pack(r, i * step, step)
            chosen = range(i * step, (i + 1) * step)
            finish(r, chosen, far_terms(r, chosen))
            if r == 1:

                @pl.when(fed)
                def _():
                    feed[i].start()

                @pl.when(jnp.logical_not(fed))
                def _():
                    sends[r + 1][2 * i].start()

            elif r < rounds - 1:
                sends[r + 1][2 * i].start()

    def right_side(r):
        for i in reversed(range(PIECES)):
            sends[r][2 * i].wait_recv()
            pack(r, REACH + tiles_here + i * step, step)
        from_tile = tiles_here - REACH
        chosen = [from_tile + (PIECES - 1 - t // step) * step + t % step for t in range(REACH)]
        products = far_terms(r, chosen)
        for i in range(PIECES):
            finish(r, chosen[i * step : (i + 1) * step], products[i * step : (i + 1) * step])
            if r == 1:
                sends[r + 1][2 * (PIECES - 1 - i) + 1].start()
            elif r < rounds - 1:

                @pl.when(jnp.logical_not(lends))
                def _():
                    sends[r + 1][2 * (PIECES - 1 - i) + 1].start()

        if r == 1:

            @pl.when(lends)
            def _():
                lend_own.start()


    for r in range(rounds):
        day = days - 1 - r // 2
        if r == 0:
            body.wait_recv()
        if r == 1:
            loads[7].wait()
            loads[8].wait()
            gather_forcing()
        own_terms(r, day)
        if r % 2 == 0:

            @pl.when(lends)
            def _():
                lent_out[r // 2] = base[:, tail]
                lend_base[r // 2].start()

        if r == 0:
            loads[5].wait()

            @pl.when(helps)
            def _():
                help_with(0)

        if r < rounds - 1:
            left_side(r)
            if r == 2:

                @pl.when(helps)
                def _():
                    help_with(1)

            right_side(r)
        else:
            all_halos.wait_send()

            @pl.when(relays)
            def _():
                all_relayed.wait_send()

            @pl.when(helps)
            def _():
                all_helped.wait_send()

            @pl.when(lends)
            def _():
                all_lent.wait_send()
                lend_tiles.wait_send()
                lend_cols.wait_send()

            body.wait_send()
            all_obs.wait_send()
            right_side(r)
            left_side(r)


def on_device(
    seasons,
    peers,
    start_adjoint,
    adjoint_tiles,
    column_tiles,
    source_jacobian,
    obs_owner,
    obs_local,
    obs_day,
    obs_tracer,
    obs_misfit,
):
    days, tracers = source_jacobian.shape[1], source_jacobian.shape[2]
    tiles_here, near, rows = adjoint_tiles.shape[2], adjoint_tiles.shape[3], adjoint_tiles.shape[-1]
    cells_here = start_adjoint.shape[2]
    assert tiles_here == 2 * REACH and seasons % 2 == 0 and days == 2
    wide_cells = cells_here + 2 * REACH * rows
    listed = obs_local.shape[1]
    rounds = 2 * days
    hbm = pl.BlockSpec(memory_space=pl.ANY)
    return pl.pallas_call(
        functools.partial(kernel, seasons, peers),
        out_shape=pltpu.VMEM(start_adjoint.shape, F32),
        in_specs=[hbm] * 9,
        out_specs=pl.BlockSpec(memory_space=pltpu.VMEM),
        scratch_shapes=[
            pltpu.SMEM((1, near, 2, tiles_here), jnp.int32),
        ]
        + [pltpu.VMEM((1, listed), jnp.int32)] * 4
        + [
            pltpu.VMEM((1, listed), F32),
            pltpu.VMEM((2, tiles_here, near, rows, rows), BF16),
            pltpu.VMEM((days, tracers, tracers, cells_here), F32),
            pltpu.VMEM((rounds, tracers, wide_cells), F32),
            pltpu.VMEM((tiles_here + 2 * REACH, 2 * tracers, rows), BF16),
            pltpu.VMEM((tracers, cells_here), F32),
            pltpu.VMEM((2 * listed // rows, 4, rows), F32),
            pltpu.VMEM((peers, 4, rows), F32),
            pltpu.VMEM((tiles_here * days * tracers, 2 * rows), F32),
            pltpu.SemaphoreType.DMA((9,)),
            pltpu.SemaphoreType.DMA((2,)),
            pltpu.SemaphoreType.DMA((2, 2 * PIECES + 1)),
            pltpu.SemaphoreType.DMA,
            pltpu.SemaphoreType.DMA,
            pltpu.VMEM((2, tracers, REACH * rows), F32),
            pltpu.SemaphoreType.DMA((2, PIECES)),
            pltpu.SemaphoreType.REGULAR,
            pltpu.VMEM((REACH, near - 1, rows, rows), F32),
            pltpu.VMEM((REACH, near - 1, rows, rows), BF16),
            pltpu.VMEM((1, near, 2, tiles_here), jnp.int32),
            pltpu.SMEM((1, near, 2, tiles_here), jnp.int32),
            pltpu.VMEM((2, tracers, cells_here + REACH * rows), F32),
            pltpu.VMEM((2, tracers, REACH * rows), F32),
            pltpu.VMEM((2, tracers, REACH * rows), F32),
            pltpu.VMEM((tiles_here + REACH, 2 * tracers, rows), BF16),
            pltpu.SemaphoreType.DMA((8,)),
            pltpu.SemaphoreType.DMA((2, PIECES)),
        ],
        compiler_params=pltpu.CompilerParams(collective_id=0, has_side_effects=True),
    )(
        column_tiles.transpose(0, 3, 1, 2),
        start_adjoint,
        adjoint_tiles,
        source_jacobian,
        obs_owner.reshape(1, listed),
        obs_local,
        obs_day,
        obs_tracer,
        obs_misfit,
    )


def solution(mesh):
    placed = (
        P("season", None, "cells"),
        P("season", None, "cells", None, None, None),
        P("season", None, "cells", None),
        P("season", None, None, None, "cells"),
        P("season", "cells", None),
        P("season", "cells"),
        P("season", "cells"),
        P("season", "cells"),
        P("season", "cells"),
    )
    return jax.shard_map(
        functools.partial(on_device, mesh.shape["season"], mesh.shape["cells"]),
        mesh=mesh,
        in_specs=placed,
        out_specs=P("season", None, "cells"),
        check_vma=False,
    )
```

```python
import functools

import jax
import jax.numpy as jnp
from jax import lax
from jax.experimental import pallas as pl
from jax.experimental.pallas import tpu as pltpu
from jax.sharding import PartitionSpec as P

REACH = 8
PIECES = 2
MESH = pl.DeviceIdType.MESH
F32 = jnp.float32
BF16 = jnp.bfloat16


def dot_nt(a, b):
    return lax.dot_general(a, b, (((1,), (1,)), ((), ())), preferred_element_type=F32)


def kernel(
    seasons,
    peers,
    cols_hbm,
    start_ref,
    tiles_hbm,
    jac_hbm,
    owner_hbm,
    local_hbm,
    day_hbm,
    tracer_hbm,
    misfit_hbm,
    out_hbm,
    cols_ref,
    listed_ref,
    misfit_ref,
    tiles_vm,
    jac_vm,
    wide,
    packed,
    base,
    slots_out,
    slots_in,
    force,
    load_sem,
    send_sem,
    recv_sem,
    obs_send_sem,
    obs_recv_sem,
    relayed,
    late_sem,
    lent,
    lent_tiles,
    lent_listed,
    lent_cols,
    lent_field,
    lent_base,
    lent_out,
    lent_packed,
    lend_sem,
    lend_halo_sem,
):
    s = lax.axis_index("season")
    c = lax.axis_index("cells")
    days, tracers = jac_vm.shape[0], jac_vm.shape[1]
    tiles_here, near = tiles_vm.shape[1], tiles_vm.shape[2]
    rows = tiles_vm.shape[-1]
    cells_here = tiles_here * rows
    halo = REACH * rows
    total_tiles = tiles_here * peers
    piece = halo // PIECES
    step = REACH // PIECES
    rounds = 2 * days
    own = slice(halo, halo + cells_here)

    left, right = lax.rem(c + peers - 1, peers), lax.rem(c + 1, peers)
    before, after = lax.rem(s + seasons - 1, seasons), lax.rem(s + 1, seasons)
    middle = peers // 2
    first, last, relays = c == 0, c == peers - 1, (c == middle) & (lax.rem(s, 2) == 1)
    odd = lax.rem(s, 2) == 1
    through = jnp.where(odd, s, before)
    even = lax.rem(s, 2) == 0
    helps, lends, helps_first, lends_first = last & odd, last & even, first & odd, first & even
    barrier = pltpu.get_barrier_semaphore()

    def signal(semaphore, season, cell):
        pl.semaphore_signal(
            semaphore, inc=1, device_id=(season, cell), device_id_type=MESH
        )

    @pl.when(relays)
    def _():
        signal(barrier, s, 0)
        signal(barrier, after, 0)

    @pl.when(helps)
    def _():
        signal(barrier, s, middle)
        signal(barrier, before, peers - 1)

    @pl.when(helps_first)
    def _():
        signal(barrier, before, 0)

    @pl.when(jnp.logical_not(last))
    def _():
        signal(barrier, after, right)

    signal(barrier, after, c)
    signal(barrier, after, left)

    @pl.loop(c + 1, peers)
    def _(other):
        signal(barrier, s, other)

    pairs = (
        (owner_hbm, listed_ref.at[0]),
        (local_hbm, listed_ref.at[1]),
        (day_hbm, listed_ref.at[2]),
        (tracer_hbm, listed_ref.at[3]),
        (misfit_hbm, misfit_ref),
        (cols_hbm, cols_ref),
        (tiles_hbm.at[0, 0], tiles_vm.at[0]),
        (tiles_hbm.at[0, 1], tiles_vm.at[1]),
        (jac_hbm.at[0], jac_vm),
    )
    loads = [
        pltpu.make_async_copy(a, b, load_sem.at[max(i - 4, 0)]) for i, (a, b) in enumerate(pairs)
    ]
    all_lists = pltpu.make_async_copy(listed_ref, listed_ref, load_sem.at[0])
    stage = pltpu.make_async_copy(start_ref.at[0, :, :halo], relayed.at[0], lend_sem.at[0])

    @pl.when(first)
    def _():
        stage.start()

    for load in loads[:7]:
        load.start()
    shift = rows.bit_length() - 1
    listed = misfit_ref.shape[1]
    cap = 2 * listed // peers
    per_tile = rows // cap
    slot_tiles = slots_out.shape[0]

    def compact():
        local = listed_ref[1]
        row_key = (local >> shift) * (days * tracers) + listed_ref[2] * tracers + listed_ref[3]
        owner = listed_ref[0].astype(F32)
        misfit = misfit_ref[...]
        named = lax.broadcasted_iota(jnp.int32, (peers, listed), 0).astype(F32) == owner
        named = jnp.where(named, 1.0, 0.0)
        earlier = lax.broadcasted_iota(jnp.int32, (listed, listed), 0)
        earlier = earlier < lax.broadcasted_iota(jnp.int32, (listed, listed), 1)
        counts = jnp.dot(
            named.astype(BF16),
            jnp.where(earlier, 1.0, 0.0).astype(BF16),
            preferred_element_type=F32,
        )
        place = owner * cap + jnp.sum(named * counts, axis=0, keepdims=True)
        high = misfit.astype(BF16).astype(F32)
        middle = (misfit - high).astype(BF16).astype(F32)
        at = lax.broadcasted_iota(jnp.int32, (tracers, listed), 0)
        key, lane = row_key.astype(F32), (local & (rows - 1)).astype(F32)
        first = jnp.where(at == 0, key, jnp.where(at == 1, lane, jnp.where(at == 2, high, 0.0)))
        second = jnp.where(at == 2, middle, 0.0)
        third = jnp.where(at == 2, misfit - high - middle, 0.0)
        fields = jnp.concatenate([first, second, third, jnp.zeros_like(first)], axis=0)
        fields = fields.astype(BF16)
        for g in range(slot_tiles):
            ids = lax.broadcasted_iota(jnp.int32, (rows, listed), 0) + g * rows
            chosen = jnp.where(ids.astype(F32) == place, 1.0, 0.0).astype(BF16)
            got = dot_nt(fields, chosen)
            got = got[:8] + got[8:16] + got[16:24]
            slots_out[g] = got[:4]

    def receive_at(r, which):
        if which == 2 * PIECES:
            return 4 * PIECES
        if r == 3 and which % 2:
            return 4 * PIECES + 1 + which // 2
        return r % 2 * 2 * PIECES + which

    def copy(src, r, lanes, season, cell, which):
        return pltpu.make_async_remote_copy(
            src_ref=src,
            dst_ref=wide.at[r, :, lanes],
            send_sem=send_sem,
            recv_sem=recv_sem.at[receive_at(r, which)],
            device_id=(season, cell),
            device_id_type=MESH,
        )

    def halo_copies(r):
        season = before if r == 0 else s
        copies = []
        for i in range(PIECES):
            at = i * piece
            if r == 0:
                head = start_ref.at[0, :, at : at + piece]
                tail = start_ref.at[0, :, cells_here - halo + at : cells_here - halo + at + piece]
            else:
                head = wide.at[r, :, halo + at : halo + at + piece]
                tail = wide.at[r, :, cells_here + at : cells_here + at + piece]
            behind = halo + cells_here + at
            copies += [
                copy(head, r, slice(behind, behind + piece), season, left, 2 * i),
                copy(tail, r, slice(at, at + piece), season, right, 2 * i + 1),
            ]
        return copies

    def obs_copy(o):
        return pltpu.make_async_remote_copy(
            src_ref=slots_out.at[lax.div(lax.rem(c + o, peers), per_tile)],
            dst_ref=slots_in.at[o],
            send_sem=obs_send_sem,
            recv_sem=obs_recv_sem,
            device_id=(s, lax.rem(c + o, peers)),
            device_id_type=MESH,
        )

    def all_of(ref, send, recv):
        return pltpu.make_async_remote_copy(
            src_ref=ref,
            dst_ref=ref,
            send_sem=send,
            recv_sem=recv,
            device_id=(s, left),
            device_id_type=MESH,
        )

    all_halos = all_of(
        wide.at[:, :, : 2 * halo + cells_here // rounds], send_sem, recv_sem.at[0]
    )
    all_obs = all_of(slots_in.at[1:], obs_send_sem, obs_recv_sem)

    sends = [halo_copies(r) for r in range(rounds)]
    body = copy(start_ref.at[0], 0, own, before, c, 2 * PIECES)

    def relay_in(i, flow):
        at = slice(i * piece, (i + 1) * piece)
        return pltpu.make_async_remote_copy(
            src_ref=relayed.at[0, :, at],
            dst_ref=relayed.at[flow, :, at],
            send_sem=send_sem,
            recv_sem=lend_halo_sem.at[flow, i],
            device_id=(through, middle),
            device_id_type=MESH,
        )

    def relay_out(i, flow):
        at = slice(i * piece, (i + 1) * piece)
        if flow:
            behind = halo + cells_here + i * piece
            dst, recv = wide.at[0, :, behind : behind + piece], recv_sem.at[2 * i]
        else:
            behind = cells_here + i * piece
            dst, recv = lent_field.at[0, :, behind : behind + piece], lend_halo_sem.at[0, i]
        return pltpu.make_async_remote_copy(
            src_ref=relayed.at[flow, :, at],
            dst_ref=dst,
            send_sem=lend_sem.at[0],
            recv_sem=recv,
            device_id=(s, peers - 1),
            device_id_type=MESH,
        )

    all_relayed = all_of(relayed, lend_sem.at[0], lend_sem.at[1])

    def lend(src, dst, send, recv):
        return pltpu.make_async_remote_copy(
            src_ref=src,
            dst_ref=dst,
            send_sem=send,
            recv_sem=recv,
            device_id=(after, c),
            device_id_type=MESH,
        )

    tail = slice(cells_here - halo, cells_here)
    lend_tiles = lend(lent, lent, lend_sem.at[0], lend_sem.at[1])
    lend_cols = lend(cols_hbm, lent_listed, lend_sem.at[2], lend_sem.at[3])
    lend_base = [
        lend(lent_out.at[i], lent_base.at[i], lend_sem.at[4], lend_sem.at[5 + i]) for i in range(2)
    ]
    lend_own = [
        lend(wide.at[1, :, own], lent_field.at[0, :, :cells_here], lend_sem.at[4], lend_sem.at[6]),
        lend(wide.at[2, :, own], lent_field.at[1, :, :cells_here], send_sem, lend_sem.at[6]),
    ]
    lend_head = lend(lent_out.at[0], lent_base.at[0], send_sem, lend_sem.at[5])
    lend_both = lend(lent_field.at[1], lent_field.at[1], send_sem, lend_sem.at[6])
    help_own = pltpu.make_async_copy(
        start_ref.at[0], lent_field.at[0, :, :cells_here], lend_sem.at[0]
    )
    help_cols = pltpu.make_async_copy(lent_listed, lent_cols, lend_sem.at[2])
    all_lent = all_of(lent_out, lend_sem.at[4], lend_sem.at[5])
    all_helped = all_of(lent.at[:1], lend_sem.at[4], lend_sem.at[5])

    def pass_on(r, i):
        behind = cells_here + i * piece
        to = i * piece if r == 1 else halo + behind
        return pltpu.make_async_remote_copy(
            src_ref=lent_field.at[r // 2, :, behind : behind + piece],
            dst_ref=wide.at[r, :, to : to + piece],
            send_sem=lend_sem.at[4],
            recv_sem=recv_sem.at[receive_at(r, 2 * i + r % 2)],
            device_id=(before, c),
            device_id_type=MESH,
        )

    def help_copy(r, i):
        src = lent_out.at[r // 2, :, i * piece : (i + 1) * piece]
        behind = slice(cells_here + i * piece, cells_here + (i + 1) * piece)
        if r == 0:
            dst, recv, season, cell = lent_field.at[0, :, behind], lend_halo_sem.at[0, i], s, 0
        elif r == 1:
            dst, recv, season, cell = lent_field.at[1, :, behind], lend_halo_sem.at[1, i], s, peers - 1
        else:
            dst = wide.at[3, :, i * piece : (i + 1) * piece]
            recv, season, cell = recv_sem.at[receive_at(3, 2 * i + 1)], before, 0
        return pltpu.make_async_remote_copy(
            src_ref=src,
            dst_ref=dst,
            send_sem=lend_sem.at[4],
            recv_sem=recv,
            device_id=(season, cell),
            device_id_type=MESH,
        )

    def lend_matrix(matrix, row):
        for i in range(REACH):
            for k in range(1, near):
                lent[i, k - 1] = tiles_vm[matrix, row + i, k].astype(F32)
        lend_tiles.start()

    pl.semaphore_wait(barrier, c + 3 + jnp.where(relays | lends | lends_first, 1, 0))

    @pl.loop(0, c)
    def _(other):
        signal(late_sem, s, other)

    @pl.when(first)
    def _():
        stage.wait()
        for i in reversed(range(PIECES)):
            relay_in(i, lax.rem(s + 1, 2)).start()

    @pl.when(jnp.logical_not(first))
    def _():
        for i in reversed(range(PIECES)):
            sends[0][2 * i].start()

    for i in reversed(range(PIECES)):
        sends[0][2 * i + 1].start()
    body.start()

    @pl.when(lends | lends_first)
    def _():
        lend_cols.start()

    @pl.when(helps)
    def _():
        help_own.start()

    @pl.when(relays)
    def _():
        for flow in range(2):
            for i in reversed(range(PIECES)):
                relay_in(i, flow).wait_recv()
                relay_out(i, flow).start()

    all_lists.wait()
    compact()

    @pl.loop(0, c)
    def _(other):
        obs_copy(other - c + peers).start()

    loads[6].wait()
    for load in loads[7:]:
        load.start()

    @pl.when(lends)
    def _():
        lend_matrix(0, tiles_here - REACH)

    @pl.when(lends_first)
    def _():
        loads[7].wait()
        lend_matrix(1, 0)

    @pl.when(jnp.logical_not(last))
    def _():
        pl.semaphore_wait(late_sem, peers - 1 - c)

    @pl.loop(c + 1, peers)
    def _(other):
        obs_copy(other - c).start()

    def pack(r, first, count):
        for t in range(first, first + count):
            v = wide[r, :, at_tile(t)]
            high = v.astype(BF16).astype(F32)
            packed[t] = jnp.concatenate([high, v - high], axis=0).astype(BF16)

    def gather_forcing():
        lanes = lax.broadcasted_iota(jnp.int32, slots_out.shape[1:], 1)
        first = lax.rem(c, per_tile) * cap
        mine = (lanes >= first) & (lanes < first + cap)
        merged = []
        all_obs.wait_recv()
        for g in range(slot_tiles):
            total = jnp.zeros(slots_out.shape[1:], F32)
            for o in range(g * per_tile, (g + 1) * per_tile):
                block = slots_in[o] if o > 0 else slots_out[lax.div(c, per_tile)]
                block = jnp.where(mine, block, 0.0)
                shift = (-o * cap) % rows
                total += pltpu.roll(block, shift, 1) if shift else block
            merged.append(total)
        merged = jnp.concatenate(merged, axis=1)
        row, lane, misfit = merged[0:1], merged[1:2], merged[2:3]
        slots = slot_tiles * rows
        row_ids = lax.broadcasted_iota(jnp.int32, (force.shape[0], slots), 0).astype(F32)
        hit = lax.broadcasted_iota(jnp.int32, (rows, slots), 0).astype(F32) == lane
        high = misfit.astype(BF16).astype(F32)
        values = jnp.concatenate(
            [jnp.where(hit, high, 0.0), jnp.where(hit, misfit - high, 0.0)], axis=0
        ).astype(BF16)
        force[...] = dot_nt(jnp.where(row_ids == row, 1.0, 0.0).astype(BF16), values)

    def at_tile(t):
        return slice(t * rows, (t + 1) * rows)

    def shifted(t):
        return slice(halo + t * rows, halo + (t + 1) * rows)

    def own_terms(r, day):
        matrix = r % 2
        pack(r, REACH, tiles_here)
        for t in range(tiles_here):
            v = wide[r, :, shifted(t)]
            both = dot_nt(packed[REACH + t], tiles_vm[matrix, t, 0])
            total = v + both[:tracers] + both[tracers:]
            if matrix == 1:
                at = (t * days + day) * tracers
                total += force[at : at + tracers, :rows] + force[at : at + tracers, rows:]
                for j in range(tracers):
                    total += jac_vm[day, j, :, at_tile(t)] * v[j : j + 1]
            base[:, at_tile(t)] = total

    def far_terms(r, chosen):
        matrix = r % 2
        products = []
        for t in chosen:
            picks = []
            for k in range(1, near):
                ahead = cols_ref[0, k, matrix, t] + (total_tiles + REACH - c * tiles_here)
                if total_tiles & (total_tiles - 1) == 0:
                    ahead = ahead & (total_tiles - 1)
                else:
                    ahead = lax.rem(ahead, total_tiles)
                picks.append(packed[jnp.minimum(ahead, packed.shape[0] - 1)])
            stored = [tiles_vm[matrix, t, k] for k in range(1, near)]
            both = dot_nt(jnp.concatenate(picks, axis=1), jnp.concatenate(stored, axis=1))
            products.append(both[:tracers] + both[tracers:])
        return products

    def finish(r, chosen, products):
        for t, product in zip(chosen, products):
            total = base[:, at_tile(t)] + product
            if r == rounds - 1:
                out_hbm[0, :, at_tile(t)] = total
            else:
                wide[r + 1, :, shifted(t)] = total

    def split(v):
        high = v.astype(BF16).astype(F32)
        return jnp.concatenate([high, v - high], axis=0).astype(BF16)

    def help_far(r, chosen):
        row = 0 if r == 1 else tiles_here - REACH
        count = lent_packed.shape[0]
        products = []
        for t in chosen:
            picks = []
            for k in range(1, near):
                at = lent_cols[0, k, r % 2, row + t] + (total_tiles + REACH - c * tiles_here)
                if total_tiles & (total_tiles - 1) == 0:
                    at = at & (total_tiles - 1)
                else:
                    at = lax.rem(at, total_tiles)
                at = jnp.where(at < REACH, at + tiles_here, at - REACH)
                picks.append(lent_packed[jnp.minimum(at, count - 1)])
            stored = [lent_tiles[t, k - 1] for k in range(1, near)]
            both = dot_nt(jnp.concatenate(picks, axis=1), jnp.concatenate(stored, axis=1))
            products.append(both[:tracers] + both[tracers:])
        return products

    def help_pack(turn, first, count):
        for t in range(first, first + count):
            lent_packed[t] = split(lent_field[turn, :, at_tile(t)])

    def help_finish(turn, chosen, products):
        for t, product in zip(chosen, products):
            lent_out[turn, :, at_tile(t)] = lent_base[turn, :, at_tile(t)] + product

    def help_with(r):
        turn = r // 2
        if r < 2:
            lend_cols.wait_recv()
            help_cols.start()
            if r == 0:
                help_own.wait()
            else:
                lend_own[0].wait_recv()
        else:
            lend_both.wait_recv()
        help_pack(turn, 0, tiles_here)
        if r < 2:
            help_cols.wait()
            lend_tiles.wait_recv()
            for i in range(REACH):
                for k in range(1, near):
                    lent_tiles[i, k - 1] = lent[i, k - 1].astype(BF16)
            lend_base[0].wait_recv()
        rows_of = [range(i * step, (i + 1) * step) for i in reversed(range(PIECES))]
        if r == 1:
            for i, chosen in zip(reversed(range(PIECES)), rows_of):
                help_copy(0, i).wait_recv()
                help_pack(turn, tiles_here + i * step, step)
                help_finish(turn, chosen, help_far(r, chosen))
                help_copy(r, i).start()
        else:
            for i in reversed(range(PIECES)):
                (help_copy(1, i) if r else relay_out(i, 0)).wait_recv()
                help_pack(turn, tiles_here + i * step, step)
            products = help_far(r, [t for chosen in rows_of for t in chosen])
            for i, chosen in zip(reversed(range(PIECES)), rows_of):
                at = (PIECES - 1 - i) * step
                help_finish(turn, chosen, products[at : at + step])
                help_copy(r, i).start()
        for i in reversed(range(PIECES)):
            pass_on(r, i).start()

    def left_side(r):
        for i in reversed(range(PIECES)):
            sends[r][2 * i + 1].wait_recv()
            pack(r, i * step, step)
            chosen = range(i * step, (i + 1) * step)
            finish(r, chosen, far_terms(r, chosen))
            if r == 1:

                @pl.when(jnp.logical_not(lends_first))
                def _():
                    sends[r + 1][2 * i].start()

            elif r < rounds - 1:
                sends[r + 1][2 * i].start()

    def right_side(r):
        for i in reversed(range(PIECES)):
            sends[r][2 * i].wait_recv()
            pack(r, REACH + tiles_here + i * step, step)
        from_tile = tiles_here - REACH
        chosen = [from_tile + (PIECES - 1 - t // step) * step + t % step for t in range(REACH)]
        products = far_terms(r, chosen)
        for i in range(PIECES):
            finish(r, chosen[i * step : (i + 1) * step], products[i * step : (i + 1) * step])
            if r == 1:
                sends[r + 1][2 * (PIECES - 1 - i) + 1].start()
            elif r < rounds - 1:

                @pl.when(jnp.logical_not(lends))
                def _():
                    sends[r + 1][2 * (PIECES - 1 - i) + 1].start()

        if r == 1:

            @pl.when(lends)
            def _():
                lend_own[1].start()


    for r in range(rounds):
        day = days - 1 - r // 2
        if r == 0:
            body.wait_recv()
        if r == 1:

            @pl.when(jnp.logical_not(lends_first))
            def _():
                loads[7].wait()

            loads[8].wait()
            gather_forcing()
        own_terms(r, day)
        if r % 2 == 0:

            @pl.when(lends)
            def _():
                lent_out[r // 2] = base[:, tail]
                lend_base[r // 2].start()

        if r == 0:
            loads[5].wait()

            @pl.when(helps)
            def _():
                help_with(0)

        if r == 0:
            right_side(r)
            left_side(r)

            @pl.when(lends_first)
            def _():
                lend_own[0].start()

        elif r < rounds - 1:
            if r == 1:

                @pl.when(lends_first)
                def _():
                    lent_out[0] = base[:, :halo]
                    lend_head.start()

                @pl.when(helps_first)
                def _():
                    help_with(1)

            left_side(r)
            if r == 2:

                @pl.when(helps)
                def _():
                    help_with(2)

            right_side(r)

        else:
            right_side(r)
            all_halos.wait_send()

            @pl.when(relays)
            def _():
                all_relayed.wait_send()

            @pl.when(helps)
            def _():
                all_helped.wait_send()

            @pl.when(lends | lends_first | helps_first)
            def _():
                all_lent.wait_send()

            @pl.when(lends | lends_first)
            def _():
                lend_tiles.wait_send()
                lend_cols.wait_send()

            all_obs.wait_send()
            left_side(r)


def on_device(
    seasons,
    peers,
    start_adjoint,
    adjoint_tiles,
    column_tiles,
    source_jacobian,
    obs_owner,
    obs_local,
    obs_day,
    obs_tracer,
    obs_misfit,
):
    days, tracers = source_jacobian.shape[1], source_jacobian.shape[2]
    tiles_here, near, rows = adjoint_tiles.shape[2], adjoint_tiles.shape[3], adjoint_tiles.shape[-1]
    cells_here = start_adjoint.shape[2]
    assert tiles_here == 2 * REACH and seasons % 2 == 0 and days == 2 and peers > 2
    wide_cells = cells_here + 2 * REACH * rows
    listed = obs_local.shape[1]
    rounds = 2 * days
    hbm = pl.BlockSpec(memory_space=pl.ANY)
    return pl.pallas_call(
        functools.partial(kernel, seasons, peers),
        out_shape=pltpu.VMEM(start_adjoint.shape, F32),
        in_specs=[hbm] * 9,
        out_specs=pl.BlockSpec(memory_space=pltpu.VMEM),
        scratch_shapes=[
            pltpu.SMEM((1, near, 2, tiles_here), jnp.int32),
            pltpu.VMEM((5, 1, listed), jnp.int32),
            pltpu.VMEM((1, listed), F32),
            pltpu.VMEM((2, tiles_here, near, rows, rows), BF16),
            pltpu.VMEM((days, tracers, tracers, cells_here), F32),
            pltpu.VMEM((rounds, tracers, wide_cells), F32),
            pltpu.VMEM((tiles_here + 2 * REACH, 2 * tracers, rows), BF16),
            pltpu.VMEM((tracers, cells_here), F32),
            pltpu.VMEM((2 * listed // rows, 4, rows), F32),
            pltpu.VMEM((peers, 4, rows), F32),
            pltpu.VMEM((tiles_here * days * tracers, 2 * rows), F32),
            pltpu.SemaphoreType.DMA((5,)),
            pltpu.SemaphoreType.DMA,
            pltpu.SemaphoreType.DMA((5 * PIECES + 1,)),
            pltpu.SemaphoreType.DMA,
            pltpu.SemaphoreType.DMA,
            pltpu.VMEM((2, tracers, REACH * rows), F32),
            pltpu.SemaphoreType.REGULAR,
            pltpu.VMEM((REACH, near - 1, rows, rows), F32),
            pltpu.VMEM((REACH, near - 1, rows, rows), BF16),
            pltpu.VMEM((1, near, 2, tiles_here), jnp.int32),
            pltpu.SMEM((1, near, 2, tiles_here), jnp.int32),
            pltpu.VMEM((2, tracers, cells_here + REACH * rows), F32),
            pltpu.VMEM((2, tracers, REACH * rows), F32),
            pltpu.VMEM((2, tracers, REACH * rows), F32),
            pltpu.VMEM((tiles_here + REACH, 2 * tracers, rows), BF16),
            pltpu.SemaphoreType.DMA((7,)),
            pltpu.SemaphoreType.DMA((2, PIECES)),
        ],
        compiler_params=pltpu.CompilerParams(collective_id=0, has_side_effects=True),
    )(
        column_tiles.transpose(0, 3, 1, 2),
        start_adjoint,
        adjoint_tiles,
        source_jacobian,
        obs_owner.reshape(1, listed),
        obs_local,
        obs_day,
        obs_tracer,
        obs_misfit,
    )


def solution(mesh):
    placed = (
        P("season", None, "cells"),
        P("season", None, "cells", None, None, None),
        P("season", None, "cells", None),
        P("season", None, None, None, "cells"),
        P("season", "cells", None),
        P("season", "cells"),
        P("season", "cells"),
        P("season", "cells"),
        P("season", "cells"),
    )
    return jax.shard_map(
        functools.partial(on_device, mesh.shape["season"], mesh.shape["cells"]),
        mesh=mesh,
        in_specs=placed,
        out_specs=P("season", None, "cells"),
        check_vma=False,
    )
```

```python
import functools

import jax
import jax.numpy as jnp
from jax import lax
from jax.experimental import pallas as pl
from jax.experimental.pallas import tpu as pltpu
from jax.sharding import PartitionSpec as P

REACH = 8
PIECES = 2
MESH = pl.DeviceIdType.MESH
F32 = jnp.float32
BF16 = jnp.bfloat16


def dot_nt(a, b):
    return lax.dot_general(a, b, (((1,), (1,)), ((), ())), preferred_element_type=F32)


def kernel(
    seasons,
    peers,
    cols_hbm,
    start_ref,
    tiles_hbm,
    jac_hbm,
    owner_hbm,
    local_hbm,
    day_hbm,
    tracer_hbm,
    misfit_hbm,
    out_hbm,
    cols_ref,
    listed_ref,
    misfit_ref,
    tiles_vm,
    jac_vm,
    wide,
    packed,
    base,
    slots_out,
    slots_in,
    force,
    load_sem,
    send_sem,
    recv_sem,
    obs_send_sem,
    obs_recv_sem,
    relayed,
    late_sem,
    lent,
    lent_tiles,
    lent_listed,
    lent_cols,
    lent_field,
    lent_base,
    lent_out,
    lent_packed,
    lend_sem,
    lend_halo_sem,
):
    s = lax.axis_index("season")
    c = lax.axis_index("cells")
    days, tracers = jac_vm.shape[0], jac_vm.shape[1]
    tiles_here, near = tiles_vm.shape[1], tiles_vm.shape[2]
    rows = tiles_vm.shape[-1]
    cells_here = tiles_here * rows
    halo = REACH * rows
    total_tiles = tiles_here * peers
    piece = halo // PIECES
    step = REACH // PIECES
    rounds = 2 * days
    own = slice(halo, halo + cells_here)

    left, right = lax.rem(c + peers - 1, peers), lax.rem(c + 1, peers)
    before, after = lax.rem(s + seasons - 1, seasons), lax.rem(s + 1, seasons)
    middle = peers // 2
    first, last, relays = c == 0, c == peers - 1, (c == middle) & (lax.rem(s, 2) == 1)
    odd = lax.rem(s, 2) == 1
    through = jnp.where(odd, s, before)
    even = lax.rem(s, 2) == 0
    helps, lends, helps_first, lends_first = last & odd, last & even, first & odd, first & even
    barrier = pltpu.get_barrier_semaphore()

    def signal(semaphore, season, cell):
        pl.semaphore_signal(
            semaphore, inc=1, device_id=(season, cell), device_id_type=MESH
        )

    @pl.when(relays)
    def _():
        signal(barrier, s, 0)
        signal(barrier, after, 0)

    @pl.when(helps)
    def _():
        signal(barrier, s, middle)
        signal(barrier, before, peers - 1)

    @pl.when(helps_first)
    def _():
        signal(barrier, before, 0)

    @pl.when(jnp.logical_not(last))
    def _():
        signal(barrier, after, right)

    signal(barrier, after, c)
    signal(barrier, after, left)

    @pl.loop(c + 1, peers)
    def _(other):
        signal(barrier, s, other)

    pairs = (
        (owner_hbm, listed_ref.at[0]),
        (local_hbm, listed_ref.at[1]),
        (day_hbm, listed_ref.at[2]),
        (tracer_hbm, listed_ref.at[3]),
        (misfit_hbm, misfit_ref),
        (cols_hbm, cols_ref),
        (tiles_hbm.at[0, 0], tiles_vm.at[0]),
        (tiles_hbm.at[0, 1], tiles_vm.at[1]),
        (jac_hbm.at[0], jac_vm),
    )
    loads = [
        pltpu.make_async_copy(a, b, load_sem.at[max(i - 4, 0)]) for i, (a, b) in enumerate(pairs)
    ]
    all_lists = pltpu.make_async_copy(listed_ref, listed_ref, load_sem.at[0])
    stage = pltpu.make_async_copy(start_ref.at[0, :, :halo], relayed.at[0], lend_sem.at[0])

    @pl.when(first)
    def _():
        stage.start()

    for load in loads[:7]:
        load.start()
    shift = rows.bit_length() - 1
    listed = misfit_ref.shape[1]
    cap = 2 * listed // peers
    per_tile = rows // cap
    slot_tiles = slots_out.shape[0]

    def compact():
        local = listed_ref[1]
        row_key = (local >> shift) * (days * tracers) + listed_ref[2] * tracers + listed_ref[3]
        owner = listed_ref[0].astype(F32)
        misfit = misfit_ref[...]
        named = lax.broadcasted_iota(jnp.int32, (peers, listed), 0).astype(F32) == owner
        named = jnp.where(named, 1.0, 0.0)
        earlier = lax.broadcasted_iota(jnp.int32, (listed, listed), 0)
        earlier = earlier < lax.broadcasted_iota(jnp.int32, (listed, listed), 1)
        counts = jnp.dot(
            named.astype(BF16),
            jnp.where(earlier, 1.0, 0.0).astype(BF16),
            preferred_element_type=F32,
        )
        place = owner * cap + jnp.sum(named * counts, axis=0, keepdims=True)
        high = misfit.astype(BF16).astype(F32)
        middle = (misfit - high).astype(BF16).astype(F32)
        at = lax.broadcasted_iota(jnp.int32, (tracers, listed), 0)
        key, lane = row_key.astype(F32), (local & (rows - 1)).astype(F32)
        first = jnp.where(at == 0, key, jnp.where(at == 1, lane, jnp.where(at == 2, high, 0.0)))
        second = jnp.where(at == 2, middle, 0.0)
        third = jnp.where(at == 2, misfit - high - middle, 0.0)
        fields = jnp.concatenate([first, second, third, jnp.zeros_like(first)], axis=0)
        fields = fields.astype(BF16)
        for g in range(slot_tiles):
            ids = lax.broadcasted_iota(jnp.int32, (rows, listed), 0) + g * rows
            chosen = jnp.where(ids.astype(F32) == place, 1.0, 0.0).astype(BF16)
            got = dot_nt(fields, chosen)
            got = got[:8] + got[8:16] + got[16:24]
            slots_out[g] = got[:4]

    def receive_at(r, which):
        if which == 2 * PIECES:
            return 4 * PIECES
        if r == 3 and which % 2:
            return 4 * PIECES + 1 + which // 2
        return r % 2 * 2 * PIECES + which

    def copy(src, r, lanes, season, cell, which):
        return pltpu.make_async_remote_copy(
            src_ref=src,
            dst_ref=wide.at[r, :, lanes],
            send_sem=send_sem,
            recv_sem=recv_sem.at[receive_at(r, which)],
            device_id=(season, cell),
            device_id_type=MESH,
        )

    def halo_copies(r):
        season = before if r == 0 else s
        copies = []
        for i in range(PIECES):
            at = i * piece
            if r == 0:
                head = start_ref.at[0, :, at : at + piece]
                tail = start_ref.at[0, :, cells_here - halo + at : cells_here - halo + at + piece]
            else:
                head = wide.at[r, :, halo + at : halo + at + piece]
                tail = wide.at[r, :, cells_here + at : cells_here + at + piece]
            behind = halo + cells_here + at
            copies += [
                copy(head, r, slice(behind, behind + piece), season, left, 2 * i),
                copy(tail, r, slice(at, at + piece), season, right, 2 * i + 1),
            ]
        return copies

    def obs_copy(o):
        return pltpu.make_async_remote_copy(
            src_ref=slots_out.at[lax.div(lax.rem(c + o, peers), per_tile)],
            dst_ref=slots_in.at[o],
            send_sem=obs_send_sem,
            recv_sem=obs_recv_sem,
            device_id=(s, lax.rem(c + o, peers)),
            device_id_type=MESH,
        )

    def all_of(ref, send, recv):
        return pltpu.make_async_remote_copy(
            src_ref=ref,
            dst_ref=ref,
            send_sem=send,
            recv_sem=recv,
            device_id=(s, left),
            device_id_type=MESH,
        )

    all_halos = all_of(
        wide.at[:, :, : 2 * halo + cells_here // rounds], send_sem, recv_sem.at[0]
    )
    all_obs = all_of(slots_in.at[1:], obs_send_sem, obs_recv_sem)

    sends = [halo_copies(r) for r in range(rounds)]
    body = copy(start_ref.at[0], 0, own, before, c, 2 * PIECES)

    def relay_in(i, flow):
        at = slice(i * piece, (i + 1) * piece)
        return pltpu.make_async_remote_copy(
            src_ref=relayed.at[0, :, at],
            dst_ref=relayed.at[flow, :, at],
            send_sem=send_sem,
            recv_sem=lend_halo_sem.at[flow, i],
            device_id=(through, middle),
            device_id_type=MESH,
        )

    def relay_out(i, flow):
        at = slice(i * piece, (i + 1) * piece)
        if flow:
            behind = halo + cells_here + i * piece
            dst, recv = wide.at[0, :, behind : behind + piece], recv_sem.at[2 * i]
        else:
            behind = cells_here + i * piece
            dst, recv = lent_field.at[0, :, behind : behind + piece], lend_halo_sem.at[0, i]
        return pltpu.make_async_remote_copy(
            src_ref=relayed.at[flow, :, at],
            dst_ref=dst,
            send_sem=lend_sem.at[0],
            recv_sem=recv,
            device_id=(s, peers - 1),
            device_id_type=MESH,
        )

    all_relayed = all_of(relayed, lend_sem.at[0], lend_sem.at[1])

    def lend(src, dst, send, recv):
        return pltpu.make_async_remote_copy(
            src_ref=src,
            dst_ref=dst,
            send_sem=send,
            recv_sem=recv,
            device_id=(after, c),
            device_id_type=MESH,
        )

    tail = slice(cells_here - halo, cells_here)
    lend_tiles = lend(lent, lent, lend_sem.at[0], lend_sem.at[1])
    lend_cols = lend(cols_hbm, lent_listed, lend_sem.at[2], lend_sem.at[3])
    lend_base = [
        lend(lent_out.at[i], lent_base.at[i], lend_sem.at[4], lend_sem.at[5 + i]) for i in range(2)
    ]
    lend_own = [
        lend(wide.at[1, :, own], lent_field.at[0, :, :cells_here], lend_sem.at[4], lend_sem.at[6]),
        lend(wide.at[2, :, own], lent_field.at[1, :, :cells_here], send_sem, lend_sem.at[6]),
    ]
    lend_head = lend(lent_out.at[0], lent_base.at[0], send_sem, lend_sem.at[5])
    lend_both = lend(lent_field.at[1], lent_field.at[1], send_sem, lend_sem.at[6])
    help_own = pltpu.make_async_copy(
        start_ref.at[0], lent_field.at[0, :, :cells_here], lend_sem.at[0]
    )
    help_cols = pltpu.make_async_copy(lent_listed, lent_cols, lend_sem.at[2])
    all_lent = all_of(lent_out, lend_sem.at[4], lend_sem.at[5])
    all_helped = all_of(lent.at[:1], lend_sem.at[4], lend_sem.at[5])

    def pass_on(r, i):
        behind = cells_here + i * piece
        to = i * piece if r == 1 else halo + behind
        return pltpu.make_async_remote_copy(
            src_ref=lent_field.at[r // 2, :, behind : behind + piece],
            dst_ref=wide.at[r, :, to : to + piece],
            send_sem=lend_sem.at[4],
            recv_sem=recv_sem.at[receive_at(r, 2 * i + r % 2)],
            device_id=(before, c),
            device_id_type=MESH,
        )

    def help_copy(r, i):
        src = lent_out.at[r // 2, :, i * piece : (i + 1) * piece]
        behind = slice(cells_here + i * piece, cells_here + (i + 1) * piece)
        if r == 0:
            dst, recv, season, cell = lent_field.at[0, :, behind], lend_halo_sem.at[0, i], s, 0
        elif r == 1:
            dst, recv, season, cell = lent_field.at[1, :, behind], lend_halo_sem.at[1, i], s, peers - 1
        else:
            dst = wide.at[3, :, i * piece : (i + 1) * piece]
            recv, season, cell = recv_sem.at[receive_at(3, 2 * i + 1)], before, 0
        return pltpu.make_async_remote_copy(
            src_ref=src,
            dst_ref=dst,
            send_sem=lend_sem.at[4],
            recv_sem=recv,
            device_id=(season, cell),
            device_id_type=MESH,
        )

    def lend_matrix(matrix, row):
        for i in range(REACH):
            for k in range(1, near):
                lent[i, k - 1] = tiles_vm[matrix, row + i, k].astype(F32)
        lend_tiles.start()

    pl.semaphore_wait(barrier, c + 3 + jnp.where(relays | lends | lends_first, 1, 0))

    @pl.loop(0, c)
    def _(other):
        signal(late_sem, s, other)

    @pl.when(first)
    def _():
        stage.wait()
        for i in reversed(range(PIECES)):
            relay_in(i, lax.rem(s + 1, 2)).start()

    @pl.when(jnp.logical_not(first))
    def _():
        for i in reversed(range(PIECES)):
            sends[0][2 * i].start()

    for i in reversed(range(PIECES)):
        sends[0][2 * i + 1].start()
    body.start()

    @pl.when(lends | lends_first)
    def _():
        lend_cols.start()

    @pl.when(helps)
    def _():
        help_own.start()

    @pl.when(relays)
    def _():
        for flow in range(2):
            for i in reversed(range(PIECES)):
                relay_in(i, flow).wait_recv()
                relay_out(i, flow).start()

    all_lists.wait()
    compact()

    @pl.loop(0, c)
    def _(other):
        obs_copy(other - c + peers).start()

    loads[6].wait()
    for load in loads[7:]:
        load.start()

    @pl.when(lends)
    def _():
        lend_matrix(0, tiles_here - REACH)

    @pl.when(lends_first)
    def _():
        loads[7].wait()
        lend_matrix(1, 0)

    @pl.when(jnp.logical_not(last))
    def _():
        pl.semaphore_wait(late_sem, peers - 1 - c)

    @pl.loop(c + 1, peers)
    def _(other):
        obs_copy(other - c).start()

    def pack(r, first, count):
        for t in range(first, first + count):
            v = wide[r, :, at_tile(t)]
            high = v.astype(BF16).astype(F32)
            packed[t] = jnp.concatenate([high, v - high], axis=0).astype(BF16)

    def gather_forcing():
        lanes = lax.broadcasted_iota(jnp.int32, slots_out.shape[1:], 1)
        first = lax.rem(c, per_tile) * cap
        mine = (lanes >= first) & (lanes < first + cap)
        merged = []
        all_obs.wait_recv()
        for g in range(slot_tiles):
            total = jnp.zeros(slots_out.shape[1:], F32)
            for o in range(g * per_tile, (g + 1) * per_tile):
                block = slots_in[o] if o > 0 else slots_out[lax.div(c, per_tile)]
                block = jnp.where(mine, block, 0.0)
                shift = (-o * cap) % rows
                total += pltpu.roll(block, shift, 1) if shift else block
            merged.append(total)
        merged = jnp.concatenate(merged, axis=1)
        row, lane, misfit = merged[0:1], merged[1:2], merged[2:3]
        slots = slot_tiles * rows
        row_ids = lax.broadcasted_iota(jnp.int32, (force.shape[0], slots), 0).astype(F32)
        hit = lax.broadcasted_iota(jnp.int32, (rows, slots), 0).astype(F32) == lane
        high = misfit.astype(BF16).astype(F32)
        values = jnp.concatenate(
            [jnp.where(hit, high, 0.0), jnp.where(hit, misfit - high, 0.0)], axis=0
        ).astype(BF16)
        force[...] = dot_nt(jnp.where(row_ids == row, 1.0, 0.0).astype(BF16), values)

    def at_tile(t):
        return slice(t * rows, (t + 1) * rows)

    def shifted(t):
        return slice(halo + t * rows, halo + (t + 1) * rows)

    def own_terms(r, day):
        matrix = r % 2
        pack(r, REACH, tiles_here)
        for t in range(tiles_here):
            v = wide[r, :, shifted(t)]
            both = dot_nt(packed[REACH + t], tiles_vm[matrix, t, 0])
            total = v + both[:tracers] + both[tracers:]
            if matrix == 1:
                at = (t * days + day) * tracers
                total += force[at : at + tracers, :rows] + force[at : at + tracers, rows:]
                for j in range(tracers):
                    total += jac_vm[day, j, :, at_tile(t)] * v[j : j + 1]
            base[:, at_tile(t)] = total

    def far_terms(r, chosen):
        matrix = r % 2
        products = []
        for t in chosen:
            picks = []
            for k in range(1, near):
                ahead = cols_ref[0, k, matrix, t] + (total_tiles + REACH - c * tiles_here)
                if total_tiles & (total_tiles - 1) == 0:
                    ahead = ahead & (total_tiles - 1)
                else:
                    ahead = lax.rem(ahead, total_tiles)
                picks.append(packed[jnp.minimum(ahead, packed.shape[0] - 1)])
            stored = [tiles_vm[matrix, t, k] for k in range(1, near)]
            both = dot_nt(jnp.concatenate(picks, axis=1), jnp.concatenate(stored, axis=1))
            products.append(both[:tracers] + both[tracers:])
        return products

    def finish(r, chosen, products):
        for t, product in zip(chosen, products):
            total = base[:, at_tile(t)] + product
            if r == rounds - 1:
                out_hbm[0, :, at_tile(t)] = total
            else:
                wide[r + 1, :, shifted(t)] = total

    def split(v):
        high = v.astype(BF16).astype(F32)
        return jnp.concatenate([high, v - high], axis=0).astype(BF16)

    def help_far(r, chosen):
        row = 0 if r == 1 else tiles_here - REACH
        count = lent_packed.shape[0]
        products = []
        for t in chosen:
            picks = []
            for k in range(1, near):
                at = lent_cols[0, k, r % 2, row + t] + (total_tiles + REACH - c * tiles_here)
                if total_tiles & (total_tiles - 1) == 0:
                    at = at & (total_tiles - 1)
                else:
                    at = lax.rem(at, total_tiles)
                at = jnp.where(at < REACH, at + tiles_here, at - REACH)
                picks.append(lent_packed[jnp.minimum(at, count - 1)])
            stored = [lent_tiles[t, k - 1] for k in range(1, near)]
            both = dot_nt(jnp.concatenate(picks, axis=1), jnp.concatenate(stored, axis=1))
            products.append(both[:tracers] + both[tracers:])
        return products

    def help_pack(turn, first, count):
        for t in range(first, first + count):
            lent_packed[t] = split(lent_field[turn, :, at_tile(t)])

    def help_finish(turn, chosen, products):
        for t, product in zip(chosen, products):
            lent_out[turn, :, at_tile(t)] = lent_base[turn, :, at_tile(t)] + product

    def help_with(r):
        turn = r // 2
        if r < 2:
            lend_cols.wait_recv()
            help_cols.start()
            if r == 0:
                help_own.wait()
            else:
                lend_own[0].wait_recv()
        else:
            lend_both.wait_recv()
        help_pack(turn, 0, tiles_here)
        if r < 2:
            help_cols.wait()
            lend_tiles.wait_recv()
            for i in range(REACH):
                for k in range(1, near):
                    lent_tiles[i, k - 1] = lent[i, k - 1].astype(BF16)
            lend_base[0].wait_recv()
        rows_of = [range(i * step, (i + 1) * step) for i in reversed(range(PIECES))]
        if r == 1:
            for i, chosen in zip(reversed(range(PIECES)), rows_of):
                help_copy(0, i).wait_recv()
                help_pack(turn, tiles_here + i * step, step)
                help_finish(turn, chosen, help_far(r, chosen))
                help_copy(r, i).start()
        else:
            for i in reversed(range(PIECES)):
                (help_copy(1, i) if r else relay_out(i, 0)).wait_recv()
                help_pack(turn, tiles_here + i * step, step)
            products = help_far(r, [t for chosen in rows_of for t in chosen])
            for i, chosen in zip(reversed(range(PIECES)), rows_of):
                at = (PIECES - 1 - i) * step
                help_finish(turn, chosen, products[at : at + step])
                help_copy(r, i).start()
        for i in reversed(range(PIECES)):
            pass_on(r, i).start()

    def left_side(r):
        for i in reversed(range(PIECES)):
            sends[r][2 * i + 1].wait_recv()
            pack(r, i * step, step)
            chosen = range(i * step, (i + 1) * step)
            finish(r, chosen, far_terms(r, chosen))
            if r == 1:

                @pl.when(jnp.logical_not(lends_first))
                def _():
                    sends[r + 1][2 * i].start()

            elif r < rounds - 1:
                sends[r + 1][2 * i].start()

    def right_side(r):
        for i in reversed(range(PIECES)):
            sends[r][2 * i].wait_recv()
            pack(r, REACH + tiles_here + i * step, step)
        from_tile = tiles_here - REACH
        chosen = [from_tile + (PIECES - 1 - t // step) * step + t % step for t in range(REACH)]
        products = far_terms(r, chosen)
        for i in range(PIECES):
            finish(r, chosen[i * step : (i + 1) * step], products[i * step : (i + 1) * step])
            if r == 1:
                sends[r + 1][2 * (PIECES - 1 - i) + 1].start()
            elif r < rounds - 1:

                @pl.when(jnp.logical_not(lends))
                def _():
                    sends[r + 1][2 * (PIECES - 1 - i) + 1].start()


    for r in range(rounds):
        day = days - 1 - r // 2
        if r == 0:
            body.wait_recv()
        if r == 1:

            @pl.when(jnp.logical_not(lends_first))
            def _():
                loads[7].wait()

            loads[8].wait()
            gather_forcing()
        own_terms(r, day)
        if r % 2 == 0:

            @pl.when(lends)
            def _():
                lent_out[r // 2] = base[:, tail]
                lend_base[r // 2].start()

        if r == 0:
            loads[5].wait()

            @pl.when(helps)
            def _():
                help_with(0)

        if r == 0:
            right_side(r)
            left_side(r)

            @pl.when(lends_first)
            def _():
                lend_own[0].start()

        elif r < rounds - 1:
            if r == 1:

                @pl.when(lends_first)
                def _():
                    lent_out[0] = base[:, :halo]
                    lend_head.start()

                @pl.when(helps_first)
                def _():
                    help_with(1)

            if r == 2:

                @pl.when(helps)
                def _():
                    help_with(2)

            right_side(r)
            left_side(r)
            if r == 1:

                @pl.when(lends)
                def _():
                    lend_own[1].start()

        else:
            right_side(r)
            all_halos.wait_send()

            @pl.when(relays)
            def _():
                all_relayed.wait_send()

            @pl.when(helps)
            def _():
                all_helped.wait_send()

            @pl.when(lends | lends_first | helps_first)
            def _():
                all_lent.wait_send()

            @pl.when(lends | lends_first)
            def _():
                lend_tiles.wait_send()
                lend_cols.wait_send()

            all_obs.wait_send()
            left_side(r)


def on_device(
    seasons,
    peers,
    start_adjoint,
    adjoint_tiles,
    column_tiles,
    source_jacobian,
    obs_owner,
    obs_local,
    obs_day,
    obs_tracer,
    obs_misfit,
):
    days, tracers = source_jacobian.shape[1], source_jacobian.shape[2]
    tiles_here, near, rows = adjoint_tiles.shape[2], adjoint_tiles.shape[3], adjoint_tiles.shape[-1]
    cells_here = start_adjoint.shape[2]
    assert tiles_here == 2 * REACH and seasons % 2 == 0 and days == 2 and peers > 2
    wide_cells = cells_here + 2 * REACH * rows
    listed = obs_local.shape[1]
    rounds = 2 * days
    hbm = pl.BlockSpec(memory_space=pl.ANY)
    return pl.pallas_call(
        functools.partial(kernel, seasons, peers),
        out_shape=pltpu.VMEM(start_adjoint.shape, F32),
        in_specs=[hbm] * 9,
        out_specs=pl.BlockSpec(memory_space=pltpu.VMEM),
        scratch_shapes=[
            pltpu.SMEM((1, near, 2, tiles_here), jnp.int32),
            pltpu.VMEM((5, 1, listed), jnp.int32),
            pltpu.VMEM((1, listed), F32),
            pltpu.VMEM((2, tiles_here, near, rows, rows), BF16),
            pltpu.VMEM((days, tracers, tracers, cells_here), F32),
            pltpu.VMEM((rounds, tracers, wide_cells), F32),
            pltpu.VMEM((tiles_here + 2 * REACH, 2 * tracers, rows), BF16),
            pltpu.VMEM((tracers, cells_here), F32),
            pltpu.VMEM((2 * listed // rows, 4, rows), F32),
            pltpu.VMEM((peers, 4, rows), F32),
            pltpu.VMEM((tiles_here * days * tracers, 2 * rows), F32),
            pltpu.SemaphoreType.DMA((5,)),
            pltpu.SemaphoreType.DMA,
            pltpu.SemaphoreType.DMA((5 * PIECES + 1,)),
            pltpu.SemaphoreType.DMA,
            pltpu.SemaphoreType.DMA,
            pltpu.VMEM((2, tracers, REACH * rows), F32),
            pltpu.SemaphoreType.REGULAR,
            pltpu.VMEM((REACH, near - 1, rows, rows), F32),
            pltpu.VMEM((REACH, near - 1, rows, rows), BF16),
            pltpu.VMEM((1, near, 2, tiles_here), jnp.int32),
            pltpu.SMEM((1, near, 2, tiles_here), jnp.int32),
            pltpu.VMEM((2, tracers, cells_here + REACH * rows), F32),
            pltpu.VMEM((2, tracers, REACH * rows), F32),
            pltpu.VMEM((2, tracers, REACH * rows), F32),
            pltpu.VMEM((tiles_here + REACH, 2 * tracers, rows), BF16),
            pltpu.SemaphoreType.DMA((7,)),
            pltpu.SemaphoreType.DMA((2, PIECES)),
        ],
        compiler_params=pltpu.CompilerParams(collective_id=0, has_side_effects=True),
    )(
        column_tiles.transpose(0, 3, 1, 2),
        start_adjoint,
        adjoint_tiles,
        source_jacobian,
        obs_owner.reshape(1, listed),
        obs_local,
        obs_day,
        obs_tracer,
        obs_misfit,
    )


def solution(mesh):
    placed = (
        P("season", None, "cells"),
        P("season", None, "cells", None, None, None),
        P("season", None, "cells", None),
        P("season", None, None, None, "cells"),
        P("season", "cells", None),
        P("season", "cells"),
        P("season", "cells"),
        P("season", "cells"),
        P("season", "cells"),
    )
    return jax.shard_map(
        functools.partial(on_device, mesh.shape["season"], mesh.shape["cells"]),
        mesh=mesh,
        in_specs=placed,
        out_specs=P("season", None, "cells"),
        check_vma=False,
    )
```

```python
import functools

import jax
import jax.numpy as jnp
from jax import lax
from jax.experimental import pallas as pl
from jax.experimental.pallas import tpu as pltpu
from jax.sharding import PartitionSpec as P

REACH = 8
PIECES = 2
MESH = pl.DeviceIdType.MESH
F32 = jnp.float32
BF16 = jnp.bfloat16


def dot_nt(a, b):
    return lax.dot_general(a, b, (((1,), (1,)), ((), ())), preferred_element_type=F32)


def kernel(
    seasons,
    peers,
    cols_hbm,
    start_ref,
    tiles_hbm,
    jac_hbm,
    owner_hbm,
    local_hbm,
    day_hbm,
    tracer_hbm,
    misfit_hbm,
    out_hbm,
    cols_ref,
    listed_ref,
    misfit_ref,
    tiles_vm,
    jac_vm,
    wide,
    packed,
    base,
    slots_out,
    slots_in,
    force,
    load_sem,
    send_sem,
    recv_sem,
    obs_send_sem,
    obs_recv_sem,
    relayed,
    late_sem,
    lent,
    lent_tiles,
    lent_listed,
    lent_cols,
    lent_field,
    lent_base,
    lent_out,
    lent_packed,
    lend_sem,
    lend_halo_sem,
):
    s = lax.axis_index("season")
    c = lax.axis_index("cells")
    days, tracers = jac_vm.shape[0], jac_vm.shape[1]
    tiles_here, near = tiles_vm.shape[1], tiles_vm.shape[2]
    rows = tiles_vm.shape[-1]
    cells_here = tiles_here * rows
    halo = REACH * rows
    total_tiles = tiles_here * peers
    piece = halo // PIECES
    step = REACH // PIECES
    rounds = 2 * days
    own = slice(halo, halo + cells_here)

    left, right = lax.rem(c + peers - 1, peers), lax.rem(c + 1, peers)
    before, after = lax.rem(s + seasons - 1, seasons), lax.rem(s + 1, seasons)
    middle = peers // 2
    first, last, relays = c == 0, c == peers - 1, (c == middle) & (lax.rem(s, 2) == 1)
    odd = lax.rem(s, 2) == 1
    even = lax.rem(s, 2) == 0
    helps, lends, helps_first, lends_first = last & odd, last & even, first & odd, first & even
    barrier = pltpu.get_barrier_semaphore()

    def signal(semaphore, season, cell):
        pl.semaphore_signal(
            semaphore, inc=1, device_id=(season, cell), device_id_type=MESH
        )

    @pl.when(relays)
    def _():
        signal(barrier, s, 0)
        signal(barrier, lax.rem(s + 2, seasons), 0)

    @pl.when(helps)
    def _():
        signal(barrier, s, middle)
        signal(barrier, before, peers - 1)

    @pl.when(helps_first)
    def _():
        signal(barrier, before, 0)

    @pl.when(jnp.logical_not(last))
    def _():
        signal(barrier, after, right)

    signal(barrier, after, c)
    signal(barrier, after, left)

    @pl.loop(c + 1, peers)
    def _(other):
        signal(barrier, s, other)

    pairs = (
        (owner_hbm, listed_ref.at[0]),
        (local_hbm, listed_ref.at[1]),
        (day_hbm, listed_ref.at[2]),
        (tracer_hbm, listed_ref.at[3]),
        (misfit_hbm, misfit_ref),
        (cols_hbm, cols_ref),
        (tiles_hbm.at[0, 0], tiles_vm.at[0]),
        (tiles_hbm.at[0, 1], tiles_vm.at[1]),
        (jac_hbm.at[0], jac_vm),
    )
    places = (0, 0, 0, 0, 0, 1, 2, 0, 2)
    loads = [
        pltpu.make_async_copy(a, b, load_sem.at[at]) for at, (a, b) in zip(places, pairs)
    ]
    all_lists = pltpu.make_async_copy(listed_ref, listed_ref, load_sem.at[0])
    stage = pltpu.make_async_copy(start_ref.at[0, :, :halo], relayed.at[0], lend_sem.at[2])

    @pl.when(first)
    def _():
        stage.start()

    for load in loads[:7]:
        load.start()
    shift = rows.bit_length() - 1
    listed = misfit_ref.shape[1]
    cap = 2 * listed // peers
    per_tile = rows // cap
    slot_tiles = slots_out.shape[0]

    def compact():
        local = listed_ref[1]
        row_key = (local >> shift) * (days * tracers) + listed_ref[2] * tracers + listed_ref[3]
        owner = listed_ref[0].astype(F32)
        misfit = misfit_ref[...]
        named = lax.broadcasted_iota(jnp.int32, (peers, listed), 0).astype(F32) == owner
        named = jnp.where(named, 1.0, 0.0)
        earlier = lax.broadcasted_iota(jnp.int32, (listed, listed), 0)
        earlier = earlier < lax.broadcasted_iota(jnp.int32, (listed, listed), 1)
        counts = jnp.dot(
            named.astype(BF16),
            jnp.where(earlier, 1.0, 0.0).astype(BF16),
            preferred_element_type=F32,
        )
        place = owner * cap + jnp.sum(named * counts, axis=0, keepdims=True)
        high = misfit.astype(BF16).astype(F32)
        middle = (misfit - high).astype(BF16).astype(F32)
        at = lax.broadcasted_iota(jnp.int32, (tracers, listed), 0)
        key, lane = row_key.astype(F32), (local & (rows - 1)).astype(F32)
        first = jnp.where(at == 0, key, jnp.where(at == 1, lane, jnp.where(at == 2, high, 0.0)))
        second = jnp.where(at == 2, middle, 0.0)
        third = jnp.where(at == 2, misfit - high - middle, 0.0)
        fields = jnp.concatenate([first, second, third, jnp.zeros_like(first)], axis=0)
        fields = fields.astype(BF16)
        for g in range(slot_tiles):
            ids = lax.broadcasted_iota(jnp.int32, (rows, listed), 0) + g * rows
            chosen = jnp.where(ids.astype(F32) == place, 1.0, 0.0).astype(BF16)
            got = dot_nt(fields, chosen)
            got = got[:8] + got[8:16] + got[16:24]
            slots_out[g] = got[:4]

    def receive_at(r, which):
        if which == 2 * PIECES:
            return 4 * PIECES
        if r == rounds - 1 and which % 2:
            return 4 * PIECES + which // 2
        return r % 2 * 2 * PIECES + which

    def copy(src, r, lanes, season, cell, which):
        return pltpu.make_async_remote_copy(
            src_ref=src,
            dst_ref=wide.at[r, :, lanes],
            send_sem=send_sem,
            recv_sem=recv_sem.at[receive_at(r, which)],
            device_id=(season, cell),
            device_id_type=MESH,
        )

    def halo_copies(r):
        season = before if r == 0 else s
        copies = []
        for i in range(PIECES):
            at = i * piece
            if r == 0:
                head = start_ref.at[0, :, at : at + piece]
                tail = start_ref.at[0, :, cells_here - halo + at : cells_here - halo + at + piece]
            else:
                head = wide.at[r, :, halo + at : halo + at + piece]
                tail = wide.at[r, :, cells_here + at : cells_here + at + piece]
            behind = halo + cells_here + at
            copies += [
                copy(head, r, slice(behind, behind + piece), season, left, 2 * i),
                copy(tail, r, slice(at, at + piece), season, right, 2 * i + 1),
            ]
        return copies

    def obs_copy(o):
        return pltpu.make_async_remote_copy(
            src_ref=slots_out.at[lax.div(lax.rem(c + o, peers), per_tile)],
            dst_ref=slots_in.at[o],
            send_sem=obs_send_sem,
            recv_sem=obs_recv_sem,
            device_id=(s, lax.rem(c + o, peers)),
            device_id_type=MESH,
        )

    def all_of(ref, send, recv):
        return pltpu.make_async_remote_copy(
            src_ref=ref,
            dst_ref=ref,
            send_sem=send,
            recv_sem=recv,
            device_id=(s, left),
            device_id_type=MESH,
        )

    all_halos = all_of(
        wide.at[:, :, : 2 * halo + cells_here // rounds], send_sem, recv_sem.at[0]
    )
    all_obs = all_of(slots_in.at[1:], obs_send_sem, obs_recv_sem)

    sends = [halo_copies(r) for r in range(rounds)]
    body = copy(start_ref.at[0], 0, own, before, c, 2 * PIECES)

    def relay_in(i, flow):
        at = slice(i * piece, (i + 1) * piece)
        send = lend_sem.at[2] if flow else send_sem
        return pltpu.make_async_remote_copy(
            src_ref=relayed.at[flow, :, at],
            dst_ref=relayed.at[flow, :, at],
            send_sem=send,
            recv_sem=lend_halo_sem.at[flow, i],
            device_id=(lax.rem(s + seasons - 2, seasons) if flow else s, middle),
            device_id_type=MESH,
        )

    def relay_near(i):
        at = slice(i * piece, (i + 1) * piece)
        return pltpu.make_async_remote_copy(
            src_ref=relayed.at[0, :, at],
            dst_ref=relayed.at[1, :, at],
            send_sem=send_sem,
            recv_sem=lend_halo_sem.at[1, i],
            device_id=(after, 0),
            device_id_type=MESH,
        )

    def relay_out(i, flow):
        at = slice(i * piece, (i + 1) * piece)
        if flow:
            behind = halo + cells_here + i * piece
            dst, recv = wide.at[0, :, behind : behind + piece], recv_sem.at[2 * i]
        else:
            behind = cells_here + i * piece
            dst, recv = lent_field.at[0, :, behind : behind + piece], lend_halo_sem.at[0, i]
        return pltpu.make_async_remote_copy(
            src_ref=relayed.at[flow, :, at],
            dst_ref=dst,
            send_sem=lend_sem.at[0],
            recv_sem=recv,
            device_id=(s, peers - 1),
            device_id_type=MESH,
        )

    all_relayed = all_of(relayed, lend_sem.at[0], lend_sem.at[0])

    def lend(src, dst, send, recv):
        return pltpu.make_async_remote_copy(
            src_ref=src,
            dst_ref=dst,
            send_sem=send,
            recv_sem=recv,
            device_id=(after, c),
            device_id_type=MESH,
        )

    tail = slice(cells_here - halo, cells_here)
    lend_tiles = lend(lent, lent, lend_sem.at[0], lend_sem.at[0])
    lend_cols = lend(cols_hbm, lent_listed, lend_sem.at[1], lend_sem.at[1])
    lend_base = [
        lend(lent_out.at[i], lent_base.at[i], lend_sem.at[2], lend_sem.at[3 + i]) for i in range(2)
    ]
    lend_own = [
        lend(wide.at[1, :, own], lent_field.at[0, :, :cells_here], lend_sem.at[2], lend_sem.at[4]),
        lend(wide.at[2, :, own], lent_field.at[1, :, :cells_here], send_sem, lend_sem.at[4]),
    ]
    lend_head = lend(lent_out.at[0], lent_base.at[0], send_sem, lend_sem.at[3])
    lend_both = lend(lent_field.at[1], lent_field.at[1], send_sem, lend_sem.at[4])
    help_own = pltpu.make_async_copy(
        start_ref.at[0], lent_field.at[0, :, :cells_here], lend_sem.at[2]
    )
    help_cols = pltpu.make_async_copy(lent_listed, lent_cols, lend_sem.at[1])
    all_lent = all_of(lent_out, lend_sem.at[2], lend_sem.at[0])
    all_near = all_of(lent_field.at[1], lend_sem.at[2], lend_sem.at[0])
    all_helped = all_of(lent_field.at[:, :, : 2 * halo], lend_sem.at[2], lend_sem.at[0])

    def pass_on(r, i):
        behind = cells_here + i * piece
        to = i * piece if r == 1 else halo + behind
        return pltpu.make_async_remote_copy(
            src_ref=lent_field.at[r // 2, :, behind : behind + piece],
            dst_ref=wide.at[r, :, to : to + piece],
            send_sem=lend_sem.at[2],
            recv_sem=recv_sem.at[receive_at(r, 2 * i + r % 2)],
            device_id=(before, c),
            device_id_type=MESH,
        )

    def help_copy(r, i):
        src = lent_out.at[r // 2, :, i * piece : (i + 1) * piece]
        behind = slice(cells_here + i * piece, cells_here + (i + 1) * piece)
        if r == 0:
            dst, recv, season, cell = lent_field.at[0, :, behind], lend_halo_sem.at[0, i], s, 0
        elif r == 1:
            dst, recv, season, cell = lent_field.at[1, :, behind], lend_halo_sem.at[1, i], s, peers - 1
        else:
            dst = wide.at[3, :, i * piece : (i + 1) * piece]
            recv, season, cell = recv_sem.at[receive_at(3, 2 * i + 1)], before, 0
        return pltpu.make_async_remote_copy(
            src_ref=src,
            dst_ref=dst,
            send_sem=lend_sem.at[2],
            recv_sem=recv,
            device_id=(season, cell),
            device_id_type=MESH,
        )

    def lend_matrix(matrix, row):
        for i in range(REACH):
            for k in range(1, near):
                lent[i, k - 1] = tiles_vm[matrix, row + i, k].astype(F32)
        lend_tiles.start()

    pl.semaphore_wait(barrier, c + 3 + jnp.where(relays | lends | helps_first, 1, 0))

    @pl.loop(0, c)
    def _(other):
        signal(late_sem, s, other)

    @pl.when(lends_first)
    def _():
        stage.wait()
        for i in reversed(range(PIECES)):
            relay_near(i).start()

    @pl.when(helps_first)
    def _():
        stage.wait()
        for i in reversed(range(PIECES)):
            relay_in(i, 0).start()

    @pl.when(jnp.logical_not(first))
    def _():
        for i in reversed(range(PIECES)):
            sends[0][2 * i].start()

    for i in reversed(range(PIECES)):
        sends[0][2 * i + 1].start()
    body.start()

    @pl.when(helps_first)
    def _():
        for i in reversed(range(PIECES)):
            relay_near(i).wait_recv()
            relay_in(i, 1).start()

    @pl.when(lends | lends_first)
    def _():
        lend_cols.start()

    @pl.when(helps)
    def _():
        help_own.start()

    @pl.when(relays)
    def _():
        for flow in range(2):
            for i in reversed(range(PIECES)):
                relay_in(i, flow).wait_recv()
                relay_out(i, flow).start()

    all_lists.wait()
    compact()

    @pl.loop(0, c)
    def _(other):
        obs_copy(other - c + peers).start()

    loads[6].wait()
    for load in loads[7:]:
        load.start()

    @pl.when(lends)
    def _():
        lend_matrix(0, tiles_here - REACH)

    @pl.when(lends_first)
    def _():
        loads[7].wait()
        lend_matrix(1, 0)

    @pl.when(jnp.logical_not(last))
    def _():
        pl.semaphore_wait(late_sem, peers - 1 - c)

    @pl.loop(c + 1, peers)
    def _(other):
        obs_copy(other - c).start()

    def pack(r, first, count):
        for t in range(first, first + count):
            v = wide[r, :, at_tile(t)]
            high = v.astype(BF16).astype(F32)
            packed[t] = jnp.concatenate([high, v - high], axis=0).astype(BF16)

    def gather_forcing():
        lanes = lax.broadcasted_iota(jnp.int32, slots_out.shape[1:], 1)
        first = lax.rem(c, per_tile) * cap
        mine = (lanes >= first) & (lanes < first + cap)
        merged = []
        all_obs.wait_recv()
        for g in range(slot_tiles):
            total = jnp.zeros(slots_out.shape[1:], F32)
            for o in range(g * per_tile, (g + 1) * per_tile):
                block = slots_in[o] if o > 0 else slots_out[lax.div(c, per_tile)]
                block = jnp.where(mine, block, 0.0)
                shift = (-o * cap) % rows
                total += pltpu.roll(block, shift, 1) if shift else block
            merged.append(total)
        merged = jnp.concatenate(merged, axis=1)
        row, lane, misfit = merged[0:1], merged[1:2], merged[2:3]
        slots = slot_tiles * rows
        row_ids = lax.broadcasted_iota(jnp.int32, (force.shape[0], slots), 0).astype(F32)
        hit = lax.broadcasted_iota(jnp.int32, (rows, slots), 0).astype(F32) == lane
        high = misfit.astype(BF16).astype(F32)
        values = jnp.concatenate(
            [jnp.where(hit, high, 0.0), jnp.where(hit, misfit - high, 0.0)], axis=0
        ).astype(BF16)
        force[...] = dot_nt(jnp.where(row_ids == row, 1.0, 0.0).astype(BF16), values)

    def at_tile(t):
        return slice(t * rows, (t + 1) * rows)

    def shifted(t):
        return slice(halo + t * rows, halo + (t + 1) * rows)

    def own_terms(r, day):
        matrix = r % 2
        pack(r, REACH, tiles_here)
        for t in range(tiles_here):
            v = wide[r, :, shifted(t)]
            both = dot_nt(packed[REACH + t], tiles_vm[matrix, t, 0])
            total = v + both[:tracers] + both[tracers:]
            if matrix == 1:
                at = (t * days + day) * tracers
                total += force[at : at + tracers, :rows] + force[at : at + tracers, rows:]
                for j in range(tracers):
                    total += jac_vm[day, j, :, at_tile(t)] * v[j : j + 1]
            base[:, at_tile(t)] = total

    def far_terms(r, chosen):
        matrix = r % 2
        products = []
        for t in chosen:
            picks = []
            for k in range(1, near):
                ahead = cols_ref[0, k, matrix, t] + (total_tiles + REACH - c * tiles_here)
                if total_tiles & (total_tiles - 1) == 0:
                    ahead = ahead & (total_tiles - 1)
                else:
                    ahead = lax.rem(ahead, total_tiles)
                picks.append(packed[jnp.minimum(ahead, packed.shape[0] - 1)])
            stored = [tiles_vm[matrix, t, k] for k in range(1, near)]
            both = dot_nt(jnp.concatenate(picks, axis=1), jnp.concatenate(stored, axis=1))
            products.append(both[:tracers] + both[tracers:])
        return products

    def finish(r, chosen, products):
        for t, product in zip(chosen, products):
            total = base[:, at_tile(t)] + product
            if r == rounds - 1:
                out_hbm[0, :, at_tile(t)] = total
            else:
                wide[r + 1, :, shifted(t)] = total

    def split(v):
        high = v.astype(BF16).astype(F32)
        return jnp.concatenate([high, v - high], axis=0).astype(BF16)

    def help_far(r, chosen):
        row = 0 if r == 1 else tiles_here - REACH
        count = lent_packed.shape[0]
        products = []
        for t in chosen:
            picks = []
            for k in range(1, near):
                at = lent_cols[0, k, r % 2, row + t] + (total_tiles + REACH - c * tiles_here)
                if total_tiles & (total_tiles - 1) == 0:
                    at = at & (total_tiles - 1)
                else:
                    at = lax.rem(at, total_tiles)
                at = jnp.where(at < REACH, at + tiles_here, at - REACH)
                picks.append(lent_packed[jnp.minimum(at, count - 1)])
            stored = [lent_tiles[t, k - 1] for k in range(1, near)]
            both = dot_nt(jnp.concatenate(picks, axis=1), jnp.concatenate(stored, axis=1))
            products.append(both[:tracers] + both[tracers:])
        return products

    def help_pack(turn, first, count):
        for t in range(first, first + count):
            lent_packed[t] = split(lent_field[turn, :, at_tile(t)])

    def help_finish(turn, chosen, products):
        for t, product in zip(chosen, products):
            lent_out[turn, :, at_tile(t)] = lent_base[turn, :, at_tile(t)] + product

    def help_with(r):
        turn = r // 2
        if r < 2:
            lend_cols.wait_recv()
            help_cols.start()
            if r == 0:
                help_own.wait()
            else:
                lend_own[0].wait_recv()
        else:
            lend_both.wait_recv()
        help_pack(turn, 0, tiles_here)
        if r < 2:
            help_cols.wait()
            lend_tiles.wait_recv()
            for i in range(REACH):
                for k in range(1, near):
                    lent_tiles[i, k - 1] = lent[i, k - 1].astype(BF16)
            lend_base[0].wait_recv()
        rows_of = [range(i * step, (i + 1) * step) for i in reversed(range(PIECES))]
        if r == 1:
            for i, chosen in zip(reversed(range(PIECES)), rows_of):
                help_copy(0, i).wait_recv()
                help_pack(turn, tiles_here + i * step, step)
                help_finish(turn, chosen, help_far(r, chosen))
                help_copy(r, i).start()
        else:
            for i in reversed(range(PIECES)):
                (help_copy(1, i) if r else relay_out(i, 0)).wait_recv()
                help_pack(turn, tiles_here + i * step, step)
            products = help_far(r, [t for chosen in rows_of for t in chosen])
            for i, chosen in zip(reversed(range(PIECES)), rows_of):
                at = (PIECES - 1 - i) * step
                help_finish(turn, chosen, products[at : at + step])
                help_copy(r, i).start()
        for i in reversed(range(PIECES)):
            pass_on(r, i).start()

    def left_side(r):
        for i in reversed(range(PIECES)):
            sends[r][2 * i + 1].wait_recv()
            pack(r, i * step, step)
            chosen = range(i * step, (i + 1) * step)
            finish(r, chosen, far_terms(r, chosen))
            if r == 1:

                @pl.when(jnp.logical_not(lends_first))
                def _():
                    sends[r + 1][2 * i].start()

            elif r < rounds - 1:
                sends[r + 1][2 * i].start()

    def right_side(r):
        for i in reversed(range(PIECES)):
            sends[r][2 * i].wait_recv()
            pack(r, REACH + tiles_here + i * step, step)
        from_tile = tiles_here - REACH
        chosen = [from_tile + (PIECES - 1 - t // step) * step + t % step for t in range(REACH)]
        products = far_terms(r, chosen)
        for i in range(PIECES):
            finish(r, chosen[i * step : (i + 1) * step], products[i * step : (i + 1) * step])
            if r == 1:
                sends[r + 1][2 * (PIECES - 1 - i) + 1].start()
            elif r < rounds - 1:

                @pl.when(jnp.logical_not(lends))
                def _():
                    sends[r + 1][2 * (PIECES - 1 - i) + 1].start()


    for r in range(rounds):
        day = days - 1 - r // 2
        if r == 0:
            body.wait_recv()
        if r == 1:

            @pl.when(jnp.logical_not(lends_first))
            def _():
                loads[7].wait()

            loads[8].wait()
            gather_forcing()
        own_terms(r, day)
        if r % 2 == 0:

            @pl.when(lends)
            def _():
                lent_out[r // 2] = base[:, tail]
                lend_base[r // 2].start()

        if r == 0:
            loads[5].wait()

            @pl.when(helps)
            def _():
                help_with(0)

        if r == 0:
            right_side(r)
            left_side(r)

            @pl.when(lends_first)
            def _():
                lend_own[0].start()

        elif r < rounds - 1:
            if r == 1:

                @pl.when(lends_first)
                def _():
                    lent_out[0] = base[:, :halo]
                    lend_head.start()

            if r == 2:

                @pl.when(helps)
                def _():
                    help_with(2)

            right_side(r)
            if r == 1:

                @pl.when(helps_first)
                def _():
                    help_with(1)

            left_side(r)
            if r == 1:

                @pl.when(lends)
                def _():
                    lend_own[1].start()

        else:
            right_side(r)
            all_halos.wait_send()

            @pl.when(relays)
            def _():
                all_relayed.wait_send()

            @pl.when(helps)
            def _():
                all_helped.wait_send()

            @pl.when(helps_first)
            def _():
                all_near.wait_send()

            @pl.when(lends | lends_first)
            def _():
                all_lent.wait_send()

            @pl.when(lends | lends_first)
            def _():
                lend_tiles.wait_send()
                lend_cols.wait_send()

            all_obs.wait_send()
            left_side(r)


def on_device(
    seasons,
    peers,
    start_adjoint,
    adjoint_tiles,
    column_tiles,
    source_jacobian,
    obs_owner,
    obs_local,
    obs_day,
    obs_tracer,
    obs_misfit,
):
    days, tracers = source_jacobian.shape[1], source_jacobian.shape[2]
    tiles_here, near, rows = adjoint_tiles.shape[2], adjoint_tiles.shape[3], adjoint_tiles.shape[-1]
    cells_here = start_adjoint.shape[2]
    assert tiles_here == 2 * REACH and seasons % 2 == 0 and days == 2 and peers > 2
    wide_cells = cells_here + 2 * REACH * rows
    listed = obs_local.shape[1]
    rounds = 2 * days
    hbm = pl.BlockSpec(memory_space=pl.ANY)
    return pl.pallas_call(
        functools.partial(kernel, seasons, peers),
        out_shape=pltpu.VMEM(start_adjoint.shape, F32),
        in_specs=[hbm] * 9,
        out_specs=pl.BlockSpec(memory_space=pltpu.VMEM),
        scratch_shapes=[
            pltpu.SMEM((1, near, 2, tiles_here), jnp.int32),
            pltpu.VMEM((5, 1, listed), jnp.int32),
            pltpu.VMEM((1, listed), F32),
            pltpu.VMEM((2, tiles_here, near, rows, rows), BF16),
            pltpu.VMEM((days, tracers, tracers, cells_here), F32),
            pltpu.VMEM((rounds, tracers, wide_cells), F32),
            pltpu.VMEM((tiles_here + 2 * REACH, 2 * tracers, rows), BF16),
            pltpu.VMEM((tracers, cells_here), F32),
            pltpu.VMEM((2 * listed // rows, 4, rows), F32),
            pltpu.VMEM((peers, 4, rows), F32),
            pltpu.VMEM((tiles_here * days * tracers, 2 * rows), F32),
            pltpu.SemaphoreType.DMA((3,)),
            pltpu.SemaphoreType.DMA,
            pltpu.SemaphoreType.DMA((5 * PIECES,)),
            pltpu.SemaphoreType.DMA,
            pltpu.SemaphoreType.DMA,
            pltpu.VMEM((2, tracers, REACH * rows), F32),
            pltpu.SemaphoreType.REGULAR,
            pltpu.VMEM((REACH, near - 1, rows, rows), F32),
            pltpu.VMEM((REACH, near - 1, rows, rows), BF16),
            pltpu.VMEM((1, near, 2, tiles_here), jnp.int32),
            pltpu.SMEM((1, near, 2, tiles_here), jnp.int32),
            pltpu.VMEM((2, tracers, cells_here + REACH * rows), F32),
            pltpu.VMEM((2, tracers, REACH * rows), F32),
            pltpu.VMEM((2, tracers, REACH * rows), F32),
            pltpu.VMEM((tiles_here + REACH, 2 * tracers, rows), BF16),
            pltpu.SemaphoreType.DMA((5,)),
            pltpu.SemaphoreType.DMA((2, PIECES)),
        ],
        compiler_params=pltpu.CompilerParams(collective_id=0, has_side_effects=True),
    )(
        column_tiles.transpose(0, 3, 1, 2),
        start_adjoint,
        adjoint_tiles,
        source_jacobian,
        obs_owner.reshape(1, listed),
        obs_local,
        obs_day,
        obs_tracer,
        obs_misfit,
    )


def solution(mesh):
    placed = (
        P("season", None, "cells"),
        P("season", None, "cells", None, None, None),
        P("season", None, "cells", None),
        P("season", None, None, None, "cells"),
        P("season", "cells", None),
        P("season", "cells"),
        P("season", "cells"),
        P("season", "cells"),
        P("season", "cells"),
    )
    return jax.shard_map(
        functools.partial(on_device, mesh.shape["season"], mesh.shape["cells"]),
        mesh=mesh,
        in_specs=placed,
        out_specs=P("season", None, "cells"),
        check_vma=False,
    )
```

```python
import functools

import jax
import jax.numpy as jnp
from jax import lax
from jax.experimental import pallas as pl
from jax.experimental.pallas import tpu as pltpu
from jax.sharding import PartitionSpec as P

REACH = 8
PIECES = 2
MESH = pl.DeviceIdType.MESH
F32 = jnp.float32
BF16 = jnp.bfloat16


def dot_nt(a, b):
    return lax.dot_general(a, b, (((1,), (1,)), ((), ())), preferred_element_type=F32)


def kernel(
    seasons,
    peers,
    cols_hbm,
    start_ref,
    tiles_hbm,
    jac_hbm,
    owner_hbm,
    local_hbm,
    day_hbm,
    tracer_hbm,
    misfit_hbm,
    out_hbm,
    cols_ref,
    listed_ref,
    misfit_ref,
    tiles_vm,
    jac_vm,
    wide,
    packed,
    base,
    slots_out,
    slots_in,
    force,
    load_sem,
    send_sem,
    recv_sem,
    obs_send_sem,
    obs_recv_sem,
    relayed,
    late_sem,
    lent,
    lent_tiles,
    lent_listed,
    lent_cols,
    lent_field,
    lent_base,
    lent_out,
    lent_packed,
    lend_sem,
    lend_halo_sem,
):
    s = lax.axis_index("season")
    c = lax.axis_index("cells")
    days, tracers = jac_vm.shape[0], jac_vm.shape[1]
    tiles_here, near = tiles_vm.shape[1], tiles_vm.shape[2]
    rows = tiles_vm.shape[-1]
    cells_here = tiles_here * rows
    halo = REACH * rows
    total_tiles = tiles_here * peers
    piece = halo // PIECES
    step = REACH // PIECES
    rounds = 2 * days
    own = slice(halo, halo + cells_here)

    left, right = lax.rem(c + peers - 1, peers), lax.rem(c + 1, peers)
    before, after = lax.rem(s + seasons - 1, seasons), lax.rem(s + 1, seasons)
    middle = peers // 2
    first, last, relays = c == 0, c == peers - 1, (c == middle) & (lax.rem(s, 2) == 1)
    odd = lax.rem(s, 2) == 1
    even = lax.rem(s, 2) == 0
    helps, lends, helps_first, lends_first = last & odd, last & even, first & odd, first & even
    barrier = pltpu.get_barrier_semaphore()

    def signal(semaphore, season, cell):
        pl.semaphore_signal(
            semaphore, inc=1, device_id=(season, cell), device_id_type=MESH
        )

    @pl.when(relays)
    def _():
        signal(barrier, s, 0)
        signal(barrier, lax.rem(s + 2, seasons), 0)

    @pl.when(helps)
    def _():
        signal(barrier, s, middle)
        signal(barrier, before, peers - 1)

    @pl.when(helps_first)
    def _():
        signal(barrier, before, 0)

    @pl.when(jnp.logical_not(last))
    def _():
        signal(barrier, after, right)

    signal(barrier, after, c)
    signal(barrier, after, left)

    @pl.loop(c + 1, peers)
    def _(other):
        signal(barrier, s, other)

    pairs = (
        (owner_hbm, listed_ref.at[0]),
        (local_hbm, listed_ref.at[1]),
        (day_hbm, listed_ref.at[2]),
        (tracer_hbm, listed_ref.at[3]),
        (misfit_hbm, misfit_ref),
        (cols_hbm, cols_ref),
        (tiles_hbm.at[0, 0], tiles_vm.at[0]),
        (tiles_hbm.at[0, 1], tiles_vm.at[1]),
        (jac_hbm.at[0], jac_vm),
    )
    places = (0, 0, 0, 0, 0, 1, 2, 0, 2)
    loads = [
        pltpu.make_async_copy(a, b, load_sem.at[at]) for at, (a, b) in zip(places, pairs)
    ]
    all_lists = pltpu.make_async_copy(listed_ref, listed_ref, load_sem.at[0])
    stage = pltpu.make_async_copy(start_ref.at[0, :, :halo], relayed.at[0], lend_sem.at[2])

    @pl.when(first)
    def _():
        stage.start()

    for load in loads[:7]:
        load.start()
    shift = rows.bit_length() - 1
    listed = misfit_ref.shape[1]
    cap = 2 * listed // peers
    per_tile = rows // cap
    slot_tiles = slots_out.shape[0]

    def compact():
        local = listed_ref[1]
        row_key = (local >> shift) * (days * tracers) + listed_ref[2] * tracers + listed_ref[3]
        owner = listed_ref[0].astype(F32)
        misfit = misfit_ref[...]
        named = lax.broadcasted_iota(jnp.int32, (peers, listed), 0).astype(F32) == owner
        named = jnp.where(named, 1.0, 0.0)
        earlier = lax.broadcasted_iota(jnp.int32, (listed, listed), 0)
        earlier = earlier < lax.broadcasted_iota(jnp.int32, (listed, listed), 1)
        counts = jnp.dot(
            named.astype(BF16),
            jnp.where(earlier, 1.0, 0.0).astype(BF16),
            preferred_element_type=F32,
        )
        place = owner * cap + jnp.sum(named * counts, axis=0, keepdims=True)
        high = misfit.astype(BF16).astype(F32)
        middle = (misfit - high).astype(BF16).astype(F32)
        at = lax.broadcasted_iota(jnp.int32, (tracers, listed), 0)
        key, lane = row_key.astype(F32), (local & (rows - 1)).astype(F32)
        first = jnp.where(at == 0, key, jnp.where(at == 1, lane, jnp.where(at == 2, high, 0.0)))
        second = jnp.where(at == 2, middle, 0.0)
        third = jnp.where(at == 2, misfit - high - middle, 0.0)
        fields = jnp.concatenate([first, second, third, jnp.zeros_like(first)], axis=0)
        fields = fields.astype(BF16)
        for g in range(slot_tiles):
            ids = lax.broadcasted_iota(jnp.int32, (rows, listed), 0) + g * rows
            chosen = jnp.where(ids.astype(F32) == place, 1.0, 0.0).astype(BF16)
            got = dot_nt(fields, chosen)
            got = got[:8] + got[8:16] + got[16:24]
            slots_out[g] = got[:4]

    def receive_at(r, which):
        if which == 2 * PIECES:
            return 4 * PIECES
        if r == rounds - 1 and which % 2:
            return 4 * PIECES + which // 2
        return r % 2 * 2 * PIECES + which

    def copy(src, r, lanes, season, cell, which):
        return pltpu.make_async_remote_copy(
            src_ref=src,
            dst_ref=wide.at[r, :, lanes],
            send_sem=send_sem,
            recv_sem=recv_sem.at[receive_at(r, which)],
            device_id=(season, cell),
            device_id_type=MESH,
        )

    def halo_copies(r):
        season = before if r == 0 else s
        copies = []
        for i in range(PIECES):
            at = i * piece
            if r == 0:
                head = start_ref.at[0, :, at : at + piece]
                tail = start_ref.at[0, :, cells_here - halo + at : cells_here - halo + at + piece]
            else:
                head = wide.at[r, :, halo + at : halo + at + piece]
                tail = wide.at[r, :, cells_here + at : cells_here + at + piece]
            behind = halo + cells_here + at
            copies += [
                copy(head, r, slice(behind, behind + piece), season, left, 2 * i),
                copy(tail, r, slice(at, at + piece), season, right, 2 * i + 1),
            ]
        return copies

    def obs_copy(o):
        return pltpu.make_async_remote_copy(
            src_ref=slots_out.at[lax.div(lax.rem(c + o, peers), per_tile)],
            dst_ref=slots_in.at[o],
            send_sem=obs_send_sem,
            recv_sem=obs_recv_sem,
            device_id=(s, lax.rem(c + o, peers)),
            device_id_type=MESH,
        )

    def all_of(ref, send, recv):
        return pltpu.make_async_remote_copy(
            src_ref=ref,
            dst_ref=ref,
            send_sem=send,
            recv_sem=recv,
            device_id=(s, left),
            device_id_type=MESH,
        )

    all_halos = all_of(
        wide.at[:, :, : 2 * halo + cells_here // rounds], send_sem, recv_sem.at[0]
    )
    all_obs = all_of(slots_in.at[1:], obs_send_sem, obs_recv_sem)

    sends = [halo_copies(r) for r in range(rounds)]
    body = copy(start_ref.at[0], 0, own, before, c, 2 * PIECES)

    def relay_in(i, flow):
        at = slice(i * piece, (i + 1) * piece)
        send = lend_sem.at[2] if flow else send_sem
        return pltpu.make_async_remote_copy(
            src_ref=relayed.at[flow, :, at],
            dst_ref=relayed.at[flow, :, at],
            send_sem=send,
            recv_sem=lend_halo_sem.at[flow, i],
            device_id=(lax.rem(s + seasons - 2, seasons) if flow else s, middle),
            device_id_type=MESH,
        )

    half = piece // 2
    part_sems = [lend_halo_sem.at[0, i] for i in range(PIECES)]
    part_sems += [lend_sem.at[1], lend_sem.at[3]]

    def part_in(q):
        at = slice(q * half, (q + 1) * half)
        return pltpu.make_async_remote_copy(
            src_ref=relayed.at[0, :, at],
            dst_ref=relayed.at[0, :, at],
            send_sem=send_sem,
            recv_sem=part_sems[q],
            device_id=(s, middle),
            device_id_type=MESH,
        )

    def part_out(q):
        behind = cells_here + q * half
        return pltpu.make_async_remote_copy(
            src_ref=relayed.at[0, :, q * half : (q + 1) * half],
            dst_ref=lent_field.at[0, :, behind : behind + half],
            send_sem=lend_sem.at[0],
            recv_sem=lend_halo_sem.at[0, q // 2],
            device_id=(s, peers - 1),
            device_id_type=MESH,
        )

    def relay_near(i):
        at = slice(i * piece, (i + 1) * piece)
        return pltpu.make_async_remote_copy(
            src_ref=relayed.at[0, :, at],
            dst_ref=relayed.at[1, :, at],
            send_sem=send_sem,
            recv_sem=lend_halo_sem.at[1, i],
            device_id=(after, 0),
            device_id_type=MESH,
        )

    def relay_out(i, flow):
        at = slice(i * piece, (i + 1) * piece)
        if flow:
            behind = halo + cells_here + i * piece
            dst, recv = wide.at[0, :, behind : behind + piece], recv_sem.at[2 * i]
        else:
            behind = cells_here + i * piece
            dst, recv = lent_field.at[0, :, behind : behind + piece], lend_halo_sem.at[0, i]
        return pltpu.make_async_remote_copy(
            src_ref=relayed.at[flow, :, at],
            dst_ref=dst,
            send_sem=lend_sem.at[0],
            recv_sem=recv,
            device_id=(s, peers - 1),
            device_id_type=MESH,
        )

    all_relayed = all_of(relayed, lend_sem.at[0], lend_sem.at[0])

    def lend(src, dst, send, recv):
        return pltpu.make_async_remote_copy(
            src_ref=src,
            dst_ref=dst,
            send_sem=send,
            recv_sem=recv,
            device_id=(after, c),
            device_id_type=MESH,
        )

    tail = slice(cells_here - halo, cells_here)
    lend_tiles = lend(lent, lent, lend_sem.at[0], lend_sem.at[0])
    lend_cols = lend(cols_hbm, lent_listed, lend_sem.at[1], lend_sem.at[1])
    lend_base = [
        lend(lent_out.at[i], lent_base.at[i], lend_sem.at[2], lend_sem.at[3 + i]) for i in range(2)
    ]
    lend_own = [
        lend(wide.at[1, :, own], lent_field.at[0, :, :cells_here], lend_sem.at[2], lend_sem.at[4]),
        lend(wide.at[2, :, own], lent_field.at[1, :, :cells_here], send_sem, lend_sem.at[4]),
    ]
    lend_head = lend(lent_out.at[0], lent_base.at[0], send_sem, lend_sem.at[3])
    lend_both = lend(lent_field.at[1], lent_field.at[1], send_sem, lend_sem.at[4])
    help_own = pltpu.make_async_copy(
        start_ref.at[0], lent_field.at[0, :, :cells_here], lend_sem.at[2]
    )
    help_cols = pltpu.make_async_copy(lent_listed, lent_cols, lend_sem.at[1])
    all_lent = all_of(lent_out, lend_sem.at[2], lend_sem.at[0])
    all_near = all_of(lent_field.at[1], lend_sem.at[2], lend_sem.at[0])
    all_helped = all_of(lent_field.at[:, :, : 2 * halo], lend_sem.at[2], lend_sem.at[0])

    def pass_on(r, i):
        behind = cells_here + i * piece
        to = i * piece if r == 1 else halo + behind
        return pltpu.make_async_remote_copy(
            src_ref=lent_field.at[r // 2, :, behind : behind + piece],
            dst_ref=wide.at[r, :, to : to + piece],
            send_sem=lend_sem.at[2],
            recv_sem=recv_sem.at[receive_at(r, 2 * i + r % 2)],
            device_id=(before, c),
            device_id_type=MESH,
        )

    def help_copy(r, i):
        src = lent_out.at[r // 2, :, i * piece : (i + 1) * piece]
        behind = slice(cells_here + i * piece, cells_here + (i + 1) * piece)
        if r == 0:
            dst, recv, season, cell = lent_field.at[0, :, behind], lend_halo_sem.at[0, i], s, 0
        elif r == 1:
            dst, recv, season, cell = lent_field.at[1, :, behind], lend_halo_sem.at[1, i], s, peers - 1
        else:
            dst = wide.at[3, :, i * piece : (i + 1) * piece]
            recv, season, cell = recv_sem.at[receive_at(3, 2 * i + 1)], before, 0
        return pltpu.make_async_remote_copy(
            src_ref=src,
            dst_ref=dst,
            send_sem=lend_sem.at[2],
            recv_sem=recv,
            device_id=(season, cell),
            device_id_type=MESH,
        )

    def lend_matrix(matrix, row):
        for i in range(REACH):
            for k in range(1, near):
                lent[i, k - 1] = tiles_vm[matrix, row + i, k].astype(F32)
        lend_tiles.start()

    pl.semaphore_wait(barrier, c + 3 + jnp.where(relays | lends | helps_first, 1, 0))

    @pl.loop(0, c)
    def _(other):
        signal(late_sem, s, other)

    @pl.when(lends_first)
    def _():
        stage.wait()
        for i in reversed(range(PIECES)):
            relay_near(i).start()

    @pl.when(helps_first)
    def _():
        stage.wait()
        for q in reversed(range(2 * PIECES)):
            part_in(q).start()

    @pl.when(jnp.logical_not(first))
    def _():
        for i in reversed(range(PIECES)):
            sends[0][2 * i].start()

    for i in reversed(range(PIECES)):
        sends[0][2 * i + 1].start()
    body.start()

    @pl.when(helps_first)
    def _():
        for i in reversed(range(PIECES)):
            relay_near(i).wait_recv()
            relay_in(i, 1).start()

    @pl.when(lends | lends_first)
    def _():
        lend_cols.start()

    @pl.when(helps)
    def _():
        help_own.start()

    @pl.when(relays)
    def _():
        for q in reversed(range(2 * PIECES)):
            part_in(q).wait_recv()
            part_out(q).start()
        for i in reversed(range(PIECES)):
            relay_in(i, 1).wait_recv()
            relay_out(i, 1).start()

    all_lists.wait()
    compact()

    @pl.loop(0, c)
    def _(other):
        obs_copy(other - c + peers).start()

    loads[6].wait()
    for load in loads[7:]:
        load.start()

    @pl.when(lends)
    def _():
        lend_matrix(0, tiles_here - REACH)

    @pl.when(lends_first)
    def _():
        loads[7].wait()
        lend_matrix(1, 0)

    @pl.when(jnp.logical_not(last))
    def _():
        pl.semaphore_wait(late_sem, peers - 1 - c)

    @pl.loop(c + 1, peers)
    def _(other):
        obs_copy(other - c).start()

    def pack(r, first, count):
        for t in range(first, first + count):
            v = wide[r, :, at_tile(t)]
            high = v.astype(BF16).astype(F32)
            packed[t] = jnp.concatenate([high, v - high], axis=0).astype(BF16)

    def gather_forcing():
        lanes = lax.broadcasted_iota(jnp.int32, slots_out.shape[1:], 1)
        first = lax.rem(c, per_tile) * cap
        mine = (lanes >= first) & (lanes < first + cap)
        merged = []
        all_obs.wait_recv()
        for g in range(slot_tiles):
            total = jnp.zeros(slots_out.shape[1:], F32)
            for o in range(g * per_tile, (g + 1) * per_tile):
                block = slots_in[o] if o > 0 else slots_out[lax.div(c, per_tile)]
                block = jnp.where(mine, block, 0.0)
                shift = (-o * cap) % rows
                total += pltpu.roll(block, shift, 1) if shift else block
            merged.append(total)
        merged = jnp.concatenate(merged, axis=1)
        row, lane, misfit = merged[0:1], merged[1:2], merged[2:3]
        slots = slot_tiles * rows
        row_ids = lax.broadcasted_iota(jnp.int32, (force.shape[0], slots), 0).astype(F32)
        hit = lax.broadcasted_iota(jnp.int32, (rows, slots), 0).astype(F32) == lane
        high = misfit.astype(BF16).astype(F32)
        values = jnp.concatenate(
            [jnp.where(hit, high, 0.0), jnp.where(hit, misfit - high, 0.0)], axis=0
        ).astype(BF16)
        force[...] = dot_nt(jnp.where(row_ids == row, 1.0, 0.0).astype(BF16), values)

    def at_tile(t):
        return slice(t * rows, (t + 1) * rows)

    def shifted(t):
        return slice(halo + t * rows, halo + (t + 1) * rows)

    def own_terms(r, day):
        matrix = r % 2
        pack(r, REACH, tiles_here)
        for t in range(tiles_here):
            v = wide[r, :, shifted(t)]
            both = dot_nt(packed[REACH + t], tiles_vm[matrix, t, 0])
            total = v + both[:tracers] + both[tracers:]
            if matrix == 1:
                at = (t * days + day) * tracers
                total += force[at : at + tracers, :rows] + force[at : at + tracers, rows:]
                for j in range(tracers):
                    total += jac_vm[day, j, :, at_tile(t)] * v[j : j + 1]
            base[:, at_tile(t)] = total

    def far_terms(r, chosen):
        matrix = r % 2
        products = []
        for t in chosen:
            picks = []
            for k in range(1, near):
                ahead = cols_ref[0, k, matrix, t] + (total_tiles + REACH - c * tiles_here)
                if total_tiles & (total_tiles - 1) == 0:
                    ahead = ahead & (total_tiles - 1)
                else:
                    ahead = lax.rem(ahead, total_tiles)
                picks.append(packed[jnp.minimum(ahead, packed.shape[0] - 1)])
            stored = [tiles_vm[matrix, t, k] for k in range(1, near)]
            both = dot_nt(jnp.concatenate(picks, axis=1), jnp.concatenate(stored, axis=1))
            products.append(both[:tracers] + both[tracers:])
        return products

    def finish(r, chosen, products):
        for t, product in zip(chosen, products):
            total = base[:, at_tile(t)] + product
            if r == rounds - 1:
                out_hbm[0, :, at_tile(t)] = total
            else:
                wide[r + 1, :, shifted(t)] = total

    def split(v):
        high = v.astype(BF16).astype(F32)
        return jnp.concatenate([high, v - high], axis=0).astype(BF16)

    def help_far(r, chosen):
        row = 0 if r == 1 else tiles_here - REACH
        count = lent_packed.shape[0]
        products = []
        for t in chosen:
            picks = []
            for k in range(1, near):
                at = lent_cols[0, k, r % 2, row + t] + (total_tiles + REACH - c * tiles_here)
                if total_tiles & (total_tiles - 1) == 0:
                    at = at & (total_tiles - 1)
                else:
                    at = lax.rem(at, total_tiles)
                at = jnp.where(at < REACH, at + tiles_here, at - REACH)
                picks.append(lent_packed[jnp.minimum(at, count - 1)])
            stored = [lent_tiles[t, k - 1] for k in range(1, near)]
            both = dot_nt(jnp.concatenate(picks, axis=1), jnp.concatenate(stored, axis=1))
            products.append(both[:tracers] + both[tracers:])
        return products

    def help_pack(turn, first, count):
        for t in range(first, first + count):
            lent_packed[t] = split(lent_field[turn, :, at_tile(t)])

    def help_finish(turn, chosen, products):
        for t, product in zip(chosen, products):
            lent_out[turn, :, at_tile(t)] = lent_base[turn, :, at_tile(t)] + product

    def help_with(r):
        turn = r // 2
        if r < 2:
            lend_cols.wait_recv()
            help_cols.start()
            if r == 0:
                help_own.wait()
            else:
                lend_own[0].wait_recv()
        else:
            lend_both.wait_recv()
        help_pack(turn, 0, tiles_here)
        if r < 2:
            help_cols.wait()
            lend_tiles.wait_recv()
            for i in range(REACH):
                for k in range(1, near):
                    lent_tiles[i, k - 1] = lent[i, k - 1].astype(BF16)
            lend_base[0].wait_recv()
        rows_of = [range(i * step, (i + 1) * step) for i in reversed(range(PIECES))]
        if r == 1:
            for i, chosen in zip(reversed(range(PIECES)), rows_of):
                help_copy(0, i).wait_recv()
                help_pack(turn, tiles_here + i * step, step)
                help_finish(turn, chosen, help_far(r, chosen))
                help_copy(r, i).start()
        else:
            for i in reversed(range(PIECES)):
                (help_copy(1, i) if r else relay_out(i, 0)).wait_recv()
                help_pack(turn, tiles_here + i * step, step)
            products = help_far(r, [t for chosen in rows_of for t in chosen])
            for i, chosen in zip(reversed(range(PIECES)), rows_of):
                at = (PIECES - 1 - i) * step
                help_finish(turn, chosen, products[at : at + step])
                help_copy(r, i).start()
        for i in reversed(range(PIECES)):
            pass_on(r, i).start()

    def left_side(r):
        for i in reversed(range(PIECES)):
            sends[r][2 * i + 1].wait_recv()
            pack(r, i * step, step)
            chosen = range(i * step, (i + 1) * step)
            finish(r, chosen, far_terms(r, chosen))
            if r == 1:

                @pl.when(jnp.logical_not(lends_first))
                def _():
                    sends[r + 1][2 * i].start()

            elif r < rounds - 1:
                sends[r + 1][2 * i].start()

    def right_side(r):
        for i in reversed(range(PIECES)):
            sends[r][2 * i].wait_recv()
            pack(r, REACH + tiles_here + i * step, step)
        from_tile = tiles_here - REACH
        chosen = [from_tile + (PIECES - 1 - t // step) * step + t % step for t in range(REACH)]
        products = far_terms(r, chosen)
        for i in range(PIECES):
            finish(r, chosen[i * step : (i + 1) * step], products[i * step : (i + 1) * step])
            if r == 1:
                sends[r + 1][2 * (PIECES - 1 - i) + 1].start()
            elif r < rounds - 1:

                @pl.when(jnp.logical_not(lends))
                def _():
                    sends[r + 1][2 * (PIECES - 1 - i) + 1].start()


    for r in range(rounds):
        day = days - 1 - r // 2
        if r == 0:
            body.wait_recv()
        if r == 1:

            @pl.when(jnp.logical_not(lends_first))
            def _():
                loads[7].wait()

            loads[8].wait()
            gather_forcing()
        own_terms(r, day)
        if r % 2 == 0:

            @pl.when(lends)
            def _():
                lent_out[r // 2] = base[:, tail]
                lend_base[r // 2].start()

        if r == 0:
            loads[5].wait()

            @pl.when(helps)
            def _():
                help_with(0)

        if r == 0:
            right_side(r)
            left_side(r)

            @pl.when(lends_first)
            def _():
                lend_own[0].start()

        elif r < rounds - 1:
            if r == 1:

                @pl.when(lends_first)
                def _():
                    lent_out[0] = base[:, :halo]
                    lend_head.start()

            if r == 2:

                @pl.when(helps)
                def _():
                    help_with(2)

            right_side(r)
            if r == 1:

                @pl.when(helps_first)
                def _():
                    help_with(1)

            left_side(r)
            if r == 1:

                @pl.when(lends)
                def _():
                    lend_own[1].start()

        else:
            right_side(r)
            all_halos.wait_send()

            @pl.when(relays)
            def _():
                all_relayed.wait_send()

            @pl.when(helps)
            def _():
                all_helped.wait_send()

            @pl.when(helps_first)
            def _():
                all_near.wait_send()

            @pl.when(lends | lends_first)
            def _():
                all_lent.wait_send()

            @pl.when(lends | lends_first)
            def _():
                lend_tiles.wait_send()
                lend_cols.wait_send()

            all_obs.wait_send()
            left_side(r)


def on_device(
    seasons,
    peers,
    start_adjoint,
    adjoint_tiles,
    column_tiles,
    source_jacobian,
    obs_owner,
    obs_local,
    obs_day,
    obs_tracer,
    obs_misfit,
):
    days, tracers = source_jacobian.shape[1], source_jacobian.shape[2]
    tiles_here, near, rows = adjoint_tiles.shape[2], adjoint_tiles.shape[3], adjoint_tiles.shape[-1]
    cells_here = start_adjoint.shape[2]
    assert tiles_here == 2 * REACH and seasons % 2 == 0 and days == 2 and peers > 2
    wide_cells = cells_here + 2 * REACH * rows
    listed = obs_local.shape[1]
    rounds = 2 * days
    hbm = pl.BlockSpec(memory_space=pl.ANY)
    return pl.pallas_call(
        functools.partial(kernel, seasons, peers),
        out_shape=pltpu.VMEM(start_adjoint.shape, F32),
        in_specs=[hbm] * 9,
        out_specs=pl.BlockSpec(memory_space=pltpu.VMEM),
        scratch_shapes=[
            pltpu.SMEM((1, near, 2, tiles_here), jnp.int32),
            pltpu.VMEM((5, 1, listed), jnp.int32),
            pltpu.VMEM((1, listed), F32),
            pltpu.VMEM((2, tiles_here, near, rows, rows), BF16),
            pltpu.VMEM((days, tracers, tracers, cells_here), F32),
            pltpu.VMEM((rounds, tracers, wide_cells), F32),
            pltpu.VMEM((tiles_here + 2 * REACH, 2 * tracers, rows), BF16),
            pltpu.VMEM((tracers, cells_here), F32),
            pltpu.VMEM((2 * listed // rows, 4, rows), F32),
            pltpu.VMEM((peers, 4, rows), F32),
            pltpu.VMEM((tiles_here * days * tracers, 2 * rows), F32),
            pltpu.SemaphoreType.DMA((3,)),
            pltpu.SemaphoreType.DMA,
            pltpu.SemaphoreType.DMA((5 * PIECES,)),
            pltpu.SemaphoreType.DMA,
            pltpu.SemaphoreType.DMA,
            pltpu.VMEM((2, tracers, REACH * rows), F32),
            pltpu.SemaphoreType.REGULAR,
            pltpu.VMEM((REACH, near - 1, rows, rows), F32),
            pltpu.VMEM((REACH, near - 1, rows, rows), BF16),
            pltpu.VMEM((1, near, 2, tiles_here), jnp.int32),
            pltpu.SMEM((1, near, 2, tiles_here), jnp.int32),
            pltpu.VMEM((2, tracers, cells_here + REACH * rows), F32),
            pltpu.VMEM((2, tracers, REACH * rows), F32),
            pltpu.VMEM((2, tracers, REACH * rows), F32),
            pltpu.VMEM((tiles_here + REACH, 2 * tracers, rows), BF16),
            pltpu.SemaphoreType.DMA((5,)),
            pltpu.SemaphoreType.DMA((2, PIECES)),
        ],
        compiler_params=pltpu.CompilerParams(collective_id=0, has_side_effects=True),
    )(
        column_tiles.transpose(0, 3, 1, 2),
        start_adjoint,
        adjoint_tiles,
        source_jacobian,
        obs_owner.reshape(1, listed),
        obs_local,
        obs_day,
        obs_tracer,
        obs_misfit,
    )


def solution(mesh):
    placed = (
        P("season", None, "cells"),
        P("season", None, "cells", None, None, None),
        P("season", None, "cells", None),
        P("season", None, None, None, "cells"),
        P("season", "cells", None),
        P("season", "cells"),
        P("season", "cells"),
        P("season", "cells"),
        P("season", "cells"),
    )
    return jax.shard_map(
        functools.partial(on_device, mesh.shape["season"], mesh.shape["cells"]),
        mesh=mesh,
        in_specs=placed,
        out_specs=P("season", None, "cells"),
        check_vma=False,
    )
```

```python
import functools

import jax
import jax.numpy as jnp
from jax import lax
from jax.experimental import pallas as pl
from jax.experimental.pallas import tpu as pltpu
from jax.sharding import PartitionSpec as P

REACH = 8
PIECES = 2
MESH = pl.DeviceIdType.MESH
F32 = jnp.float32
BF16 = jnp.bfloat16


def dot_nt(a, b):
    return lax.dot_general(a, b, (((1,), (1,)), ((), ())), preferred_element_type=F32)


def kernel(
    seasons,
    peers,
    cols_hbm,
    start_ref,
    tiles_hbm,
    jac_hbm,
    owner_hbm,
    local_hbm,
    day_hbm,
    tracer_hbm,
    misfit_hbm,
    out_hbm,
    cols_ref,
    listed_ref,
    misfit_ref,
    tiles_vm,
    jac_vm,
    wide,
    packed,
    base,
    slots_out,
    slots_in,
    force,
    load_sem,
    send_sem,
    recv_sem,
    obs_send_sem,
    obs_recv_sem,
    relayed,
    late_sem,
    lent,
    lent_tiles,
    lent_listed,
    lent_cols,
    lent_field,
    lent_base,
    lent_out,
    lent_packed,
    lend_sem,
    lend_halo_sem,
):
    s = lax.axis_index("season")
    c = lax.axis_index("cells")
    days, tracers = jac_vm.shape[0], jac_vm.shape[1]
    tiles_here, near = tiles_vm.shape[1], tiles_vm.shape[2]
    rows = tiles_vm.shape[-1]
    cells_here = tiles_here * rows
    halo = REACH * rows
    total_tiles = tiles_here * peers
    piece = halo // PIECES
    step = REACH // PIECES
    rounds = 2 * days
    own = slice(halo, halo + cells_here)

    left, right = lax.rem(c + peers - 1, peers), lax.rem(c + 1, peers)
    before, after = lax.rem(s + seasons - 1, seasons), lax.rem(s + 1, seasons)
    middle = peers // 2
    first, last, relays = c == 0, c == peers - 1, (c == middle) & (lax.rem(s, 2) == 1)
    odd = lax.rem(s, 2) == 1
    even = lax.rem(s, 2) == 0
    helps, lends, helps_first, lends_first = last & odd, last & even, first & odd, first & even
    barrier = pltpu.get_barrier_semaphore()

    def signal(semaphore, season, cell):
        pl.semaphore_signal(
            semaphore, inc=1, device_id=(season, cell), device_id_type=MESH
        )

    @pl.when(relays)
    def _():
        signal(barrier, s, 0)
        signal(barrier, lax.rem(s + 2, seasons), 0)

    @pl.when(helps)
    def _():
        signal(barrier, s, middle)
        signal(barrier, before, peers - 1)

    @pl.when(helps_first)
    def _():
        signal(barrier, before, 0)

    @pl.when(jnp.logical_not(last))
    def _():
        signal(barrier, after, right)

    signal(barrier, after, c)
    signal(barrier, after, left)

    @pl.loop(c + 1, peers)
    def _(other):
        signal(barrier, s, other)

    pairs = (
        (owner_hbm, listed_ref.at[0]),
        (local_hbm, listed_ref.at[1]),
        (day_hbm, listed_ref.at[2]),
        (tracer_hbm, listed_ref.at[3]),
        (misfit_hbm, misfit_ref),
        (cols_hbm, cols_ref),
        (tiles_hbm.at[0, 0], tiles_vm.at[0]),
        (tiles_hbm.at[0, 1], tiles_vm.at[1]),
        (jac_hbm.at[0], jac_vm),
    )
    places = (0, 0, 0, 0, 0, 1, 2, 0, 2)
    loads = [
        pltpu.make_async_copy(a, b, load_sem.at[at]) for at, (a, b) in zip(places, pairs)
    ]
    all_lists = pltpu.make_async_copy(listed_ref, listed_ref, load_sem.at[0])
    stage = pltpu.make_async_copy(start_ref.at[0, :, :halo], relayed.at[0], lend_sem.at[2])

    @pl.when(first)
    def _():
        stage.start()

    for load in loads[:7]:
        load.start()
    shift = rows.bit_length() - 1
    listed = misfit_ref.shape[1]
    cap = 2 * listed // peers
    per_tile = rows // cap
    slot_tiles = slots_out.shape[0]

    def compact():
        local = listed_ref[1]
        row_key = (local >> shift) * (days * tracers) + listed_ref[2] * tracers + listed_ref[3]
        owner = listed_ref[0].astype(F32)
        misfit = misfit_ref[...]
        named = lax.broadcasted_iota(jnp.int32, (peers, listed), 0).astype(F32) == owner
        named = jnp.where(named, 1.0, 0.0)
        earlier = lax.broadcasted_iota(jnp.int32, (listed, listed), 0)
        earlier = earlier < lax.broadcasted_iota(jnp.int32, (listed, listed), 1)
        counts = jnp.dot(
            named.astype(BF16),
            jnp.where(earlier, 1.0, 0.0).astype(BF16),
            preferred_element_type=F32,
        )
        place = owner * cap + jnp.sum(named * counts, axis=0, keepdims=True)
        high = misfit.astype(BF16).astype(F32)
        middle = (misfit - high).astype(BF16).astype(F32)
        at = lax.broadcasted_iota(jnp.int32, (tracers, listed), 0)
        key, lane = row_key.astype(F32), (local & (rows - 1)).astype(F32)
        first = jnp.where(at == 0, key, jnp.where(at == 1, lane, jnp.where(at == 2, high, 0.0)))
        second = jnp.where(at == 2, middle, 0.0)
        third = jnp.where(at == 2, misfit - high - middle, 0.0)
        fields = jnp.concatenate([first, second, third, jnp.zeros_like(first)], axis=0)
        fields = fields.astype(BF16)
        for g in range(slot_tiles):
            ids = lax.broadcasted_iota(jnp.int32, (rows, listed), 0) + g * rows
            chosen = jnp.where(ids.astype(F32) == place, 1.0, 0.0).astype(BF16)
            got = dot_nt(fields, chosen)
            got = got[:8] + got[8:16] + got[16:24]
            slots_out[g] = got[:4]

    def receive_at(r, which):
        if which == 2 * PIECES:
            return 4 * PIECES
        if r == rounds - 1 and which % 2:
            return 4 * PIECES + which // 2
        return r % 2 * 2 * PIECES + which

    def receive_sem(r, which):
        at = receive_at(r, which)
        return recv_sem.at[at] if at <= 4 * PIECES else load_sem.at[at - 4 * PIECES - 1]

    def copy(src, r, lanes, season, cell, which):
        return pltpu.make_async_remote_copy(
            src_ref=src,
            dst_ref=wide.at[r, :, lanes],
            send_sem=send_sem,
            recv_sem=receive_sem(r, which),
            device_id=(season, cell),
            device_id_type=MESH,
        )

    def halo_copies(r):
        season = before if r == 0 else s
        copies = []
        for i in range(PIECES):
            at = i * piece
            if r == 0:
                head = start_ref.at[0, :, at : at + piece]
                tail = start_ref.at[0, :, cells_here - halo + at : cells_here - halo + at + piece]
            else:
                head = wide.at[r, :, halo + at : halo + at + piece]
                tail = wide.at[r, :, cells_here + at : cells_here + at + piece]
            behind = halo + cells_here + at
            copies += [
                copy(head, r, slice(behind, behind + piece), season, left, 2 * i),
                copy(tail, r, slice(at, at + piece), season, right, 2 * i + 1),
            ]
        return copies

    def obs_copy(o):
        return pltpu.make_async_remote_copy(
            src_ref=slots_out.at[lax.div(lax.rem(c + o, peers), per_tile)],
            dst_ref=slots_in.at[o],
            send_sem=obs_send_sem,
            recv_sem=obs_recv_sem,
            device_id=(s, lax.rem(c + o, peers)),
            device_id_type=MESH,
        )

    def all_of(ref, send, recv):
        return pltpu.make_async_remote_copy(
            src_ref=ref,
            dst_ref=ref,
            send_sem=send,
            recv_sem=recv,
            device_id=(s, left),
            device_id_type=MESH,
        )

    all_halos = all_of(
        wide.at[:, :, : 2 * halo + cells_here // rounds], send_sem, recv_sem.at[0]
    )
    all_obs = all_of(slots_in.at[1:], obs_send_sem, obs_recv_sem)

    sends = [halo_copies(r) for r in range(rounds)]
    body = copy(start_ref.at[0], 0, own, before, c, 2 * PIECES)

    def relay_in(i, flow):
        at = slice(i * piece, (i + 1) * piece)
        send = lend_sem.at[2] if flow else send_sem
        return pltpu.make_async_remote_copy(
            src_ref=relayed.at[flow, :, at],
            dst_ref=relayed.at[flow, :, at],
            send_sem=send,
            recv_sem=lend_halo_sem.at[flow, i],
            device_id=(lax.rem(s + seasons - 2, seasons) if flow else s, middle),
            device_id_type=MESH,
        )

    half = piece // 2
    part_sems = [lend_halo_sem.at[0, i] for i in range(PIECES)]
    part_sems += [lend_sem.at[1], lend_sem.at[3]]

    def part_in(q):
        at = slice(q * half, (q + 1) * half)
        return pltpu.make_async_remote_copy(
            src_ref=relayed.at[0, :, at],
            dst_ref=relayed.at[0, :, at],
            send_sem=send_sem,
            recv_sem=part_sems[q],
            device_id=(s, middle),
            device_id_type=MESH,
        )

    def part_out(q):
        behind = cells_here + q * half
        return pltpu.make_async_remote_copy(
            src_ref=relayed.at[0, :, q * half : (q + 1) * half],
            dst_ref=lent_field.at[0, :, behind : behind + half],
            send_sem=lend_sem.at[0],
            recv_sem=lend_halo_sem.at[0, q // 2],
            device_id=(s, peers - 1),
            device_id_type=MESH,
        )

    def relay_near(i):
        at = slice(i * piece, (i + 1) * piece)
        return pltpu.make_async_remote_copy(
            src_ref=relayed.at[0, :, at],
            dst_ref=relayed.at[1, :, at],
            send_sem=send_sem,
            recv_sem=lend_halo_sem.at[1, i],
            device_id=(after, 0),
            device_id_type=MESH,
        )

    def relay_out(i, flow):
        at = slice(i * piece, (i + 1) * piece)
        if flow:
            behind = halo + cells_here + i * piece
            dst, recv = wide.at[0, :, behind : behind + piece], recv_sem.at[2 * i]
        else:
            behind = cells_here + i * piece
            dst, recv = lent_field.at[0, :, behind : behind + piece], lend_halo_sem.at[0, i]
        return pltpu.make_async_remote_copy(
            src_ref=relayed.at[flow, :, at],
            dst_ref=dst,
            send_sem=lend_sem.at[0],
            recv_sem=recv,
            device_id=(s, peers - 1),
            device_id_type=MESH,
        )

    all_relayed = all_of(relayed, lend_sem.at[0], lend_sem.at[0])

    def lend(src, dst, send, recv):
        return pltpu.make_async_remote_copy(
            src_ref=src,
            dst_ref=dst,
            send_sem=send,
            recv_sem=recv,
            device_id=(after, c),
            device_id_type=MESH,
        )

    tail = slice(cells_here - halo, cells_here)
    lend_tiles = lend(lent, lent, lend_sem.at[0], lend_sem.at[0])
    lend_cols = lend(cols_hbm, lent_listed, lend_sem.at[1], lend_sem.at[1])
    lend_base = [
        lend(lent_out.at[i], lent_base.at[i], lend_sem.at[2], lend_sem.at[3 + i]) for i in range(2)
    ]
    lend_own = [
        lend(wide.at[1, :, own], lent_field.at[0, :, :cells_here], lend_sem.at[2], lend_sem.at[4]),
        lend(wide.at[2, :, own], lent_field.at[1, :, :cells_here], send_sem, lend_sem.at[4]),
    ]
    lend_head = lend(lent_out.at[0], lent_base.at[0], send_sem, lend_sem.at[3])
    lend_both = lend(lent_field.at[1], lent_field.at[1], send_sem, lend_sem.at[4])
    help_own = pltpu.make_async_copy(
        start_ref.at[0], lent_field.at[0, :, :cells_here], lend_sem.at[2]
    )
    help_cols = pltpu.make_async_copy(lent_listed, lent_cols, lend_sem.at[1])
    all_lent = all_of(lent_out, lend_sem.at[2], lend_sem.at[0])
    all_near = all_of(lent_field.at[1], lend_sem.at[2], lend_sem.at[0])
    all_helped = all_of(lent_field.at[:, :, : 2 * halo], lend_sem.at[2], lend_sem.at[0])

    def pass_on(r, i):
        behind = cells_here + i * piece
        to = i * piece if r == 1 else halo + behind
        return pltpu.make_async_remote_copy(
            src_ref=lent_field.at[r // 2, :, behind : behind + piece],
            dst_ref=wide.at[r, :, to : to + piece],
            send_sem=lend_sem.at[2],
            recv_sem=receive_sem(r, 2 * i + r % 2),
            device_id=(before, c),
            device_id_type=MESH,
        )

    def help_copy(r, i):
        src = lent_out.at[r // 2, :, i * piece : (i + 1) * piece]
        behind = slice(cells_here + i * piece, cells_here + (i + 1) * piece)
        if r == 0:
            dst, recv, season, cell = lent_field.at[0, :, behind], lend_halo_sem.at[0, i], s, 0
        elif r == 1:
            dst, recv, season, cell = lent_field.at[1, :, behind], lend_halo_sem.at[1, i], s, peers - 1
        else:
            dst = wide.at[3, :, i * piece : (i + 1) * piece]
            recv, season, cell = receive_sem(3, 2 * i + 1), before, 0
        return pltpu.make_async_remote_copy(
            src_ref=src,
            dst_ref=dst,
            send_sem=lend_sem.at[2],
            recv_sem=recv,
            device_id=(season, cell),
            device_id_type=MESH,
        )

    def lend_matrix(matrix, row):
        for i in range(REACH):
            for k in range(1, near):
                lent[i, k - 1] = tiles_vm[matrix, row + i, k].astype(F32)
        lend_tiles.start()

    pl.semaphore_wait(barrier, c + 3 + jnp.where(relays | lends | helps_first, 1, 0))

    @pl.loop(0, c)
    def _(other):
        signal(late_sem, s, other)

    @pl.when(lends_first)
    def _():
        stage.wait()
        for i in reversed(range(PIECES)):
            relay_near(i).start()

    @pl.when(helps_first)
    def _():
        stage.wait()
        for q in reversed(range(2 * PIECES)):
            part_in(q).start()

    @pl.when(jnp.logical_not(first))
    def _():
        for i in reversed(range(PIECES)):
            sends[0][2 * i].start()

    for i in reversed(range(PIECES)):
        sends[0][2 * i + 1].start()
    body.start()

    @pl.when(helps_first)
    def _():
        for i in reversed(range(PIECES)):
            relay_near(i).wait_recv()
            relay_in(i, 1).start()

    @pl.when(lends | lends_first)
    def _():
        lend_cols.start()

    @pl.when(helps)
    def _():
        help_own.start()

    @pl.when(relays)
    def _():
        for q in reversed(range(2 * PIECES)):
            part_in(q).wait_recv()
            part_out(q).start()
        for i in reversed(range(PIECES)):
            relay_in(i, 1).wait_recv()
            relay_out(i, 1).start()

    all_lists.wait()
    compact()

    @pl.loop(0, c)
    def _(other):
        obs_copy(other - c + peers).start()

    loads[6].wait()
    for load in loads[7:]:
        load.start()

    @pl.when(lends)
    def _():
        lend_matrix(0, tiles_here - REACH)

    @pl.when(lends_first)
    def _():
        loads[7].wait()
        lend_matrix(1, 0)

    @pl.when(jnp.logical_not(last))
    def _():
        pl.semaphore_wait(late_sem, peers - 1 - c)

    @pl.loop(c + 1, peers)
    def _(other):
        obs_copy(other - c).start()

    def pack(r, first, count):
        for t in range(first, first + count):
            v = wide[r, :, at_tile(t)]
            high = v.astype(BF16).astype(F32)
            packed[t] = jnp.concatenate([high, v - high], axis=0).astype(BF16)

    def gather_forcing():
        lanes = lax.broadcasted_iota(jnp.int32, slots_out.shape[1:], 1)
        first = lax.rem(c, per_tile) * cap
        mine = (lanes >= first) & (lanes < first + cap)
        merged = []
        all_obs.wait_recv()
        for g in range(slot_tiles):
            total = jnp.zeros(slots_out.shape[1:], F32)
            for o in range(g * per_tile, (g + 1) * per_tile):
                block = slots_in[o] if o > 0 else slots_out[lax.div(c, per_tile)]
                block = jnp.where(mine, block, 0.0)
                shift = (-o * cap) % rows
                total += pltpu.roll(block, shift, 1) if shift else block
            merged.append(total)
        merged = jnp.concatenate(merged, axis=1)
        row, lane, misfit = merged[0:1], merged[1:2], merged[2:3]
        slots = slot_tiles * rows
        row_ids = lax.broadcasted_iota(jnp.int32, (force.shape[0], slots), 0).astype(F32)
        hit = lax.broadcasted_iota(jnp.int32, (rows, slots), 0).astype(F32) == lane
        high = misfit.astype(BF16).astype(F32)
        values = jnp.concatenate(
            [jnp.where(hit, high, 0.0), jnp.where(hit, misfit - high, 0.0)], axis=0
        ).astype(BF16)
        force[...] = dot_nt(jnp.where(row_ids == row, 1.0, 0.0).astype(BF16), values)

    def at_tile(t):
        return slice(t * rows, (t + 1) * rows)

    def shifted(t):
        return slice(halo + t * rows, halo + (t + 1) * rows)

    def own_terms(r, day):
        matrix = r % 2
        pack(r, REACH, tiles_here)
        for t in range(tiles_here):
            v = wide[r, :, shifted(t)]
            both = dot_nt(packed[REACH + t], tiles_vm[matrix, t, 0])
            total = v + both[:tracers] + both[tracers:]
            if matrix == 1:
                at = (t * days + day) * tracers
                total += force[at : at + tracers, :rows] + force[at : at + tracers, rows:]
                for j in range(tracers):
                    total += jac_vm[day, j, :, at_tile(t)] * v[j : j + 1]
            base[:, at_tile(t)] = total

    def far_terms(r, chosen):
        matrix = r % 2
        products = []
        for t in chosen:
            picks = []
            for k in range(1, near):
                ahead = cols_ref[0, k, matrix, t] + (total_tiles + REACH - c * tiles_here)
                if total_tiles & (total_tiles - 1) == 0:
                    ahead = ahead & (total_tiles - 1)
                else:
                    ahead = lax.rem(ahead, total_tiles)
                picks.append(packed[jnp.minimum(ahead, packed.shape[0] - 1)])
            stored = [tiles_vm[matrix, t, k] for k in range(1, near)]
            both = dot_nt(jnp.concatenate(picks, axis=1), jnp.concatenate(stored, axis=1))
            products.append(both[:tracers] + both[tracers:])
        return products

    def finish(r, chosen, products):
        for t, product in zip(chosen, products):
            total = base[:, at_tile(t)] + product
            if r == rounds - 1:
                out_hbm[0, :, at_tile(t)] = total
            else:
                wide[r + 1, :, shifted(t)] = total

    def split(v):
        high = v.astype(BF16).astype(F32)
        return jnp.concatenate([high, v - high], axis=0).astype(BF16)

    def help_far(r, chosen):
        row = 0 if r == 1 else tiles_here - REACH
        count = lent_packed.shape[0]
        products = []
        for t in chosen:
            picks = []
            for k in range(1, near):
                at = lent_cols[0, k, r % 2, row + t] + (total_tiles + REACH - c * tiles_here)
                if total_tiles & (total_tiles - 1) == 0:
                    at = at & (total_tiles - 1)
                else:
                    at = lax.rem(at, total_tiles)
                at = jnp.where(at < REACH, at + tiles_here, at - REACH)
                picks.append(lent_packed[jnp.minimum(at, count - 1)])
            stored = [lent_tiles[t, k - 1] for k in range(1, near)]
            both = dot_nt(jnp.concatenate(picks, axis=1), jnp.concatenate(stored, axis=1))
            products.append(both[:tracers] + both[tracers:])
        return products

    def help_pack(turn, first, count):
        for t in range(first, first + count):
            lent_packed[t] = split(lent_field[turn, :, at_tile(t)])

    def help_finish(turn, chosen, products):
        for t, product in zip(chosen, products):
            lent_out[turn, :, at_tile(t)] = lent_base[turn, :, at_tile(t)] + product

    def help_with(r):
        turn = r // 2
        if r < 2:
            lend_cols.wait_recv()
            help_cols.start()
            if r == 0:
                help_own.wait()
            else:
                lend_own[0].wait_recv()
        else:
            lend_both.wait_recv()
        help_pack(turn, 0, tiles_here)
        if r < 2:
            help_cols.wait()
            lend_tiles.wait_recv()
            for i in range(REACH):
                for k in range(1, near):
                    lent_tiles[i, k - 1] = lent[i, k - 1].astype(BF16)
            lend_base[0].wait_recv()
        rows_of = [range(i * step, (i + 1) * step) for i in reversed(range(PIECES))]
        if r == 1:
            for i, chosen in zip(reversed(range(PIECES)), rows_of):
                help_copy(0, i).wait_recv()
                help_pack(turn, tiles_here + i * step, step)
                help_finish(turn, chosen, help_far(r, chosen))
                help_copy(r, i).start()
        else:
            for i in reversed(range(PIECES)):
                (help_copy(1, i) if r else relay_out(i, 0)).wait_recv()
                help_pack(turn, tiles_here + i * step, step)
            products = help_far(r, [t for chosen in rows_of for t in chosen])
            for i, chosen in zip(reversed(range(PIECES)), rows_of):
                at = (PIECES - 1 - i) * step
                help_finish(turn, chosen, products[at : at + step])
                help_copy(r, i).start()
        for i in reversed(range(PIECES)):
            pass_on(r, i).start()

    def left_side(r):
        for i in reversed(range(PIECES)):
            sends[r][2 * i + 1].wait_recv()
            pack(r, i * step, step)
            chosen = range(i * step, (i + 1) * step)
            finish(r, chosen, far_terms(r, chosen))
            if r == 1:

                @pl.when(jnp.logical_not(lends_first))
                def _():
                    sends[r + 1][2 * i].start()

            elif r < rounds - 1:
                sends[r + 1][2 * i].start()

    def right_side(r):
        for i in reversed(range(PIECES)):
            sends[r][2 * i].wait_recv()
            pack(r, REACH + tiles_here + i * step, step)
        from_tile = tiles_here - REACH
        chosen = [from_tile + (PIECES - 1 - t // step) * step + t % step for t in range(REACH)]
        products = far_terms(r, chosen)
        for i in range(PIECES):
            finish(r, chosen[i * step : (i + 1) * step], products[i * step : (i + 1) * step])
            if r == 1:
                sends[r + 1][2 * (PIECES - 1 - i) + 1].start()
            elif r < rounds - 1:

                @pl.when(jnp.logical_not(lends))
                def _():
                    sends[r + 1][2 * (PIECES - 1 - i) + 1].start()


    for r in range(rounds):
        day = days - 1 - r // 2
        if r == 0:
            body.wait_recv()
        if r == 1:

            @pl.when(jnp.logical_not(lends_first))
            def _():
                loads[7].wait()

            loads[8].wait()
            gather_forcing()
        own_terms(r, day)
        if r % 2 == 0:

            @pl.when(lends)
            def _():
                lent_out[r // 2] = base[:, tail]
                lend_base[r // 2].start()

        if r == 0:
            loads[5].wait()

            @pl.when(helps)
            def _():
                help_with(0)

        if r == 0:
            right_side(r)
            left_side(r)

            @pl.when(lends_first)
            def _():
                lend_own[0].start()

        elif r < rounds - 1:
            if r == 1:

                @pl.when(lends_first)
                def _():
                    lent_out[0] = base[:, :halo]
                    lend_head.start()

            if r == 2:

                @pl.when(helps)
                def _():
                    help_with(2)

            right_side(r)
            if r == 1:

                @pl.when(helps_first)
                def _():
                    help_with(1)

            left_side(r)
            if r == 1:

                @pl.when(lends)
                def _():
                    lend_own[1].start()

        else:
            right_side(r)
            all_halos.wait_send()

            @pl.when(relays)
            def _():
                all_relayed.wait_send()

            @pl.when(helps)
            def _():
                all_helped.wait_send()

            @pl.when(helps_first)
            def _():
                all_near.wait_send()

            @pl.when(lends | lends_first)
            def _():
                all_lent.wait_send()

            @pl.when(lends | lends_first)
            def _():
                lend_tiles.wait_send()
                lend_cols.wait_send()

            all_obs.wait_send()
            left_side(r)


def on_device(
    seasons,
    peers,
    start_adjoint,
    adjoint_tiles,
    column_tiles,
    source_jacobian,
    obs_owner,
    obs_local,
    obs_day,
    obs_tracer,
    obs_misfit,
):
    days, tracers = source_jacobian.shape[1], source_jacobian.shape[2]
    tiles_here, near, rows = adjoint_tiles.shape[2], adjoint_tiles.shape[3], adjoint_tiles.shape[-1]
    cells_here = start_adjoint.shape[2]
    assert tiles_here == 2 * REACH and seasons % 2 == 0 and days == 2 and peers > 2
    wide_cells = cells_here + 2 * REACH * rows
    listed = obs_local.shape[1]
    rounds = 2 * days
    hbm = pl.BlockSpec(memory_space=pl.ANY)
    return pl.pallas_call(
        functools.partial(kernel, seasons, peers),
        out_shape=pltpu.VMEM(start_adjoint.shape, F32),
        in_specs=[hbm] * 9,
        out_specs=pl.BlockSpec(memory_space=pltpu.VMEM),
        scratch_shapes=[
            pltpu.SMEM((1, near, 2, tiles_here), jnp.int32),
            pltpu.VMEM((5, 1, listed), jnp.int32),
            pltpu.VMEM((1, listed), F32),
            pltpu.VMEM((2, tiles_here, near, rows, rows), BF16),
            pltpu.VMEM((days, tracers, tracers, cells_here), F32),
            pltpu.VMEM((rounds, tracers, wide_cells), F32),
            pltpu.VMEM((tiles_here + 2 * REACH, 2 * tracers, rows), BF16),
            pltpu.VMEM((tracers, cells_here), F32),
            pltpu.VMEM((2 * listed // rows, 4, rows), F32),
            pltpu.VMEM((peers, 4, rows), F32),
            pltpu.VMEM((tiles_here * days * tracers, 2 * rows), F32),
            pltpu.SemaphoreType.DMA((3,)),
            pltpu.SemaphoreType.DMA,
            pltpu.SemaphoreType.DMA((4 * PIECES + 1,)),
            pltpu.SemaphoreType.DMA,
            pltpu.SemaphoreType.DMA,
            pltpu.VMEM((2, tracers, REACH * rows), F32),
            pltpu.SemaphoreType.REGULAR,
            pltpu.VMEM((REACH, near - 1, rows, rows), F32),
            pltpu.VMEM((REACH, near - 1, rows, rows), BF16),
            pltpu.VMEM((1, near, 2, tiles_here), jnp.int32),
            pltpu.SMEM((1, near, 2, tiles_here), jnp.int32),
            pltpu.VMEM((2, tracers, cells_here + REACH * rows), F32),
            pltpu.VMEM((2, tracers, REACH * rows), F32),
            pltpu.VMEM((2, tracers, REACH * rows), F32),
            pltpu.VMEM((tiles_here + REACH, 2 * tracers, rows), BF16),
            pltpu.SemaphoreType.DMA((5,)),
            pltpu.SemaphoreType.DMA((2, PIECES)),
        ],
        compiler_params=pltpu.CompilerParams(collective_id=0, has_side_effects=True),
    )(
        column_tiles.transpose(0, 3, 1, 2),
        start_adjoint,
        adjoint_tiles,
        source_jacobian,
        obs_owner.reshape(1, listed),
        obs_local,
        obs_day,
        obs_tracer,
        obs_misfit,
    )


def solution(mesh):
    placed = (
        P("season", None, "cells"),
        P("season", None, "cells", None, None, None),
        P("season", None, "cells", None),
        P("season", None, None, None, "cells"),
        P("season", "cells", None),
        P("season", "cells"),
        P("season", "cells"),
        P("season", "cells"),
        P("season", "cells"),
    )
    return jax.shard_map(
        functools.partial(on_device, mesh.shape["season"], mesh.shape["cells"]),
        mesh=mesh,
        in_specs=placed,
        out_specs=P("season", None, "cells"),
        check_vma=False,
    )
```
